32 devices in a mesh: dp: 4 (over z), row: 4 (over y, core), col: 2 (over x).
Axes of the slice: x: 2, y: 2, z: 4, core: 2. Of those that a mesh axis runs over, the one named last changes fastest.
Arguments:
- tokens: bfloat16 [8, 8, 128, 1536], P(None, ('row', 'col'), 'dp'), may hold values from -6 to 6
- seq_lengths: int32 [8], replicated, may hold values from 1 to 1024, 6144 in all
- seq_slots: int32 [8], replicated, may hold values from 0 to 7, each once
- w_attn: bfloat16 [1536, 6144], P('row', 'col'), may hold values from -0.15625 to 0.15625
- w_forget: bfloat16 [1536, 24], P('row', 'col'), may hold values from -0.15625 to 0.15625
- b_forget: bfloat16 [24], P('col'), may hold values from -1 to 7
- w_out: bfloat16 [1536, 1536], P('col', 'row'), may hold values from -0.625 to 0.625
- w_gate: bfloat16 [1536, 4096], P('row', 'col'), may hold values from -0.15625 to 0.15625
- w_up: bfloat16 [1536, 4096], P('row', 'col'), may hold values from -0.15625 to 0.15625
- w_down: bfloat16 [4096, 1536], P('col', 'row'), may hold values from -0.09375 to 0.09375
- gain_attn: bfloat16 [1536], P('row'), may hold values from 0.5 to 1.5
- gain_ffn: bfloat16 [1536], P('row'), may hold values from 0.5 to 1.5
- out_grad: bfloat16 [8, 8, 128, 1536], P('dp', ('row', 'col')), may hold values from -6 to 6
Outputs:
- block_out: bfloat16 [8, 8, 128, 1536], P('dp', ('row', 'col'))
- tokens_grad: bfloat16 [8, 8, 128, 1536], P(None, ('row', 'col'), 'dp')
- w_attn_grad: float32 [1536, 6144], P('row', 'col')
- w_forget_grad: float32 [1536, 24], P('row', 'col')
- b_forget_grad: float32 [24], P('col')
- w_out_grad: float32 [1536, 1536], P('col', 'row')
- w_gate_grad: float32 [1536, 4096], P('row', 'col')
- w_up_grad: float32 [1536, 4096], P('row', 'col')
- w_down_grad: float32 [4096, 1536], P('col', 'row')
- gain_attn_grad: float32 [1536], P('row')
- gain_ffn_grad: float32 [1536], P('row')
The draws below stay inside these ranges and needn't reach their ends.
Inputs may be any that keep to these rules, and one draw needn't show every extreme that they name: `seq_lengths`: the 8 lengths sum to 6144 and the longest is exactly 1024. `seq_slots`: every destination slot receives exactly one sequence; slots d with d // (2 * 1) equal belong to one data group, and d % (2 * 1) // 1 is the micro-batch.
All inputs are finite; a program needn't handle non-finite values.
Results may differ from the reference program's by a relative error of at most 0.022.
Values may be sent and summed in bfloat16 or wider, within the bound.
No kernel may reach another device: no remote copies, remote signals or barrier semaphores. Data moves between devices by JAX's collectives and lax.ppermute only.
A program may use at most 256 MiB of HBM per device.

```python
import math
import jax
import jax.numpy as jnp
import numpy as np
from jax import lax

D = 1536
H = 24
HEAD = 64
FF = 4096
MAXLEN = 1024
NPART = 8
PART_LEN = 128
NSEQ = 8
N_ROW = 4
N_COL = 2


def shard_levels(own_key, shape, shards, least, high):
    gain, own = 1.0, jax.random.fold_in(own_key, 6)
    for dim, blocks in shards:
        draws = jnp.exp(jax.random.uniform(jax.random.fold_in(own, dim), (blocks,), jnp.float32, least / len(shards), high / len(shards)))
        gain = gain * jnp.repeat(draws, shape[dim] // blocks).reshape([-1 if axis == dim else 1 for axis in range(len(shape))])
    return gain


def length_profile(number_of, total, reach, slope):
    portions = [(1 << 20) // math.isqrt(grade ** slope) + 1 for grade in range(2, number_of + 1)]
    rest, given = total - reach - (number_of - 1), [1] * (number_of - 1)
    while rest > 0:
        free = [i for i in range(number_of - 1) if given[i] < reach]
        whole, budget = sum([portions[i] for i in free]), rest
        for i in free:
            addition = min(reach - given[i], max(1, budget * portions[i] // whole), rest)
            given[i] = given[i] + addition
            rest = rest - addition
    return np.array([reach] + given)


def ragged(rng, count, total, reach, lean):
    if count == 2:
        one = jax.random.randint(rng, (), max(1, total - reach), min(reach, total - 1) + 1)
        return jnp.stack([one, total - one])
    lengths = jnp.asarray(length_profile(count, total, reach, lean), jnp.int32)
    couples = (count - 1) // 2
    source_of, taker = lengths[1:1 + 2 * couples:2], lengths[2:2 + 2 * couples:2]
    margin = jnp.minimum(source_of - 1, reach - taker)
    passed = jax.random.randint(jax.random.fold_in(rng, 1), (couples,), 0, 1 << 20) % (margin + 1)
    lengths = lengths.at[1:1 + 2 * couples:2].set(source_of - passed).at[2:2 + 2 * couples:2].set(taker + passed)
    return lengths[jax.random.permutation(jax.random.fold_in(rng, 2), count)]


def bell_draw(key, extent, scale, bound, shards=(), held_as=jnp.bfloat16):
    array = scale * jax.random.normal(key, extent, jnp.float32)
    if shards:
        array = array * shard_levels(key, extent, shards, -0.22, 0.18)
    return jnp.clip(array, -bound, bound).astype(held_as)


def setup_inputs(seed: int = 0) -> dict:
    key_of = jax.random.split(jax.random.key(seed), 14)
    tokens = bell_draw(key_of[0], (NSEQ, NPART, PART_LEN, D), 1.0, 6.0, ((1, 8), (2, 4)))
    seq_lengths = ragged(key_of[1], NSEQ, 3 * NSEQ * MAXLEN // 4, MAXLEN, 1).astype(jnp.int32)
    seq_slots = jax.random.permutation(key_of[2], NSEQ).astype(jnp.int32)
    w_attn = bell_draw(key_of[3], (D, 4 * H * HEAD), D ** -0.5, 0.15625, ((0, 4), (1, 2)))
    w_forget = bell_draw(key_of[4], (D, H), D ** -0.5, 0.15625, ((0, 4), (1, 2)))
    b_forget = jnp.clip(-1.0 + 8.0 * jax.random.uniform(key_of[5], (H,), jnp.float32) ** shard_levels(key_of[5], (H,), ((0, 2),), -0.2, 0.2), -1.0, 7.0).astype(jnp.bfloat16)
    w_out = bell_draw(key_of[6], (H * HEAD, D), (H * HEAD // 16) ** -0.5, 0.625, ((0, 2), (1, 4)))
    w_gate = bell_draw(key_of[7], (D, FF), D ** -0.5, 0.15625, ((0, 4), (1, 2)))
    w_up = bell_draw(key_of[8], (D, FF), D ** -0.5, 0.15625, ((0, 4), (1, 2)))
    w_down = bell_draw(key_of[9], (FF, D), FF ** -0.5, 0.09375, ((0, 2), (1, 4)))
    gain_attn = jnp.clip(1.0 + 0.1 * jax.random.normal(key_of[10], (D,), jnp.float32), 0.5, 1.5).astype(jnp.bfloat16)
    gain_ffn = jnp.clip(1.0 + 0.1 * jax.random.normal(key_of[11], (D,), jnp.float32), 0.5, 1.5).astype(jnp.bfloat16)
    out_grad = bell_draw(key_of[12], (NSEQ, NPART, PART_LEN, D), 1.0, 6.0, ((0, 4), (1, 8)))
    return {"tokens": tokens, "seq_lengths": seq_lengths, "seq_slots": seq_slots, "w_attn": w_attn, "w_forget": w_forget, "b_forget": b_forget, "w_out": w_out, "w_gate": w_gate, "w_up": w_up, "w_down": w_down, "gain_attn": gain_attn, "gain_ffn": gain_ffn, "out_grad": out_grad}


@jax.custom_vjp
def low(v):
    return lax.optimization_barrier(v.astype(jnp.bfloat16)).astype(jnp.float32)

@jax.custom_vjp
def low_back(v):
    return v

def low_keep(v):
    return (low(v), None)

def low_pass(kept, grad):
    return (grad,)

def back_keep(v):
    return (v, None)

def back_low(kept, grad):
    return (low(grad),)
low.defvjp(low_keep, low_pass)
low_back.defvjp(back_keep, back_low)
highest = lax.Precision.HIGHEST
norm_epsilon = 1e-06
masked_score = -1e+30

def rms_norm(values, gain_vec):
    inv_scale = lax.rsqrt(lax.optimization_barrier(jnp.mean(values * values, axis=-1, keepdims=True)) + norm_epsilon)
    return values * inv_scale * gain_vec

def one_sequence(weights, seq_rows, seq_len):
    w_attn, w_forget, b_forget, w_out, w_gate, w_up, w_down, gain_attn, gain_ffn = weights
    normed = low(rms_norm(seq_rows, gain_attn))
    projected = low_back(jnp.dot(normed, w_attn, precision=highest)).reshape(MAXLEN, H, 4, HEAD)
    queries = low(projected[:, :, 0, :])
    key_rows = low(projected[:, :, 1, :])
    value_rows = low(projected[:, :, 2, :])
    gate_pre = projected[:, :, 3, :]
    logits = low_back(jnp.dot(normed, w_forget, precision=highest) + b_forget)
    prefix = jnp.cumsum(jax.nn.log_sigmoid(logits), axis=0)
    prefix_heads = prefix.T
    raw_scores = jnp.einsum('ihe,jhe->hij', queries, key_rows, precision=highest) * HEAD ** (-0.5)
    raw_scores = low_back(raw_scores + prefix_heads[:, :, None] - prefix_heads[:, None, :])
    places = jnp.arange(MAXLEN, dtype=jnp.int32)
    scores = jnp.where(places[None, :] <= places[:, None], raw_scores, masked_score)
    log_total = jax.nn.logsumexp(scores, axis=-1, keepdims=True)
    attn_probs = low(jnp.exp(scores - log_total))
    mixed_heads = low_back(jnp.einsum('hij,jhe->ihe', attn_probs, value_rows, precision=highest))
    gated_heads = low((mixed_heads * jax.nn.sigmoid(gate_pre)).reshape(MAXLEN, H * HEAD))
    attn_branch = low_back(jnp.dot(gated_heads, w_out, precision=highest))
    middle = seq_rows + attn_branch
    normed_ffn = low(rms_norm(middle, gain_ffn))
    gate_proj = low_back(jnp.dot(normed_ffn, w_gate, precision=highest))
    up_proj = low_back(jnp.dot(normed_ffn, w_up, precision=highest))
    hidden = low(jax.nn.silu(gate_proj) * up_proj)
    ffn_branch = low_back(jnp.dot(hidden, w_down, precision=highest))
    final_rows = middle + ffn_branch
    return jnp.where((places < seq_len)[:, None], final_rows, 0.0)

def reference(tokens, seq_lengths, seq_slots, w_attn, w_forget, b_forget, w_out, w_gate, w_up, w_down, gain_attn, gain_ffn, out_grad):
    inverse = jnp.zeros((NSEQ,), jnp.int32).at[seq_slots].set(jnp.arange(NSEQ, dtype=jnp.int32))
    dest_len = seq_lengths[inverse]
    weights = tuple((wmat.astype(jnp.float32) for wmat in (w_attn, w_forget, b_forget, w_out, w_gate, w_up, w_down, gain_attn, gain_ffn)))

    def forward(token_rows, *params):
        dest_rows = token_rows.reshape(NSEQ, MAXLEN, D)[inverse]

        def per_sequence(entry_pair):
            return one_sequence(params, entry_pair[0], entry_pair[1])
        outputs = lax.map(jax.checkpoint(per_sequence), (dest_rows, dest_len))
        return outputs.reshape(NSEQ, N_ROW * N_COL, MAXLEN // (N_ROW * N_COL), D)
    result, pullback = jax.vjp(forward, tokens.astype(jnp.float32), *weights)
    gradients = pullback(out_grad.astype(jnp.float32))
    return (result.astype(jnp.bfloat16), gradients[0].astype(jnp.bfloat16), gradients[1], gradients[2], gradients[3], gradients[4], gradients[5], gradients[6], gradients[7], gradients[8], gradients[9])
```

```python
import jax
import jax.numpy as jnp
from jax import lax
from jax.sharding import PartitionSpec as P

bf16 = jnp.bfloat16
f32 = jnp.float32
norm_epsilon = 1e-06
masked_score = -1e30


def product(spec, left, right):
    return jnp.einsum(spec, left, right, preferred_element_type=f32)


def inverse_scale(values):
    return lax.rsqrt(jnp.mean(values * values, axis=-1, keepdims=True) + norm_epsilon)


def norm_backward(values, inv_scale, gain_vec, grad_normed):
    weighted = grad_normed * gain_vec
    inner = jnp.mean(weighted * values, axis=-1, keepdims=True)
    grad_values = inv_scale * weighted - values * (inv_scale * inv_scale * inv_scale) * inner
    grad_gain = jnp.sum(grad_normed * values * inv_scale, axis=(0, 1))
    return (grad_values, grad_gain)


def swap_pair(values):
    count = lax.axis_size("row")
    return lax.ppermute(values, "row", [(r, r ^ 2) for r in range(count)])


def swap_core(values):
    count = lax.axis_size("row")
    return lax.ppermute(values, "row", [(r, r ^ 1) for r in range(count)])


def swap_col(values):
    count = lax.axis_size("col")
    return lax.ppermute(values, "col", [(r, r ^ 1) for r in range(count)])


def pick(values, index, axis):
    return lax.dynamic_index_in_dim(values, index, axis, keepdims=False)


def ordered(own, other, index, axis):
    return jnp.where(index == 0, jnp.stack([own, other], axis), jnp.stack([other, own], axis))


def turned(values, pair):
    half = values.shape[-1] // 2
    swapped = jnp.concatenate([values[..., half:], values[..., :half]], axis=-1)
    return jnp.where(pair == 0, values, swapped)


def gather_quad(values, core, col):
    wide = ordered(values, swap_col(values), col, 1)
    full = ordered(wide, swap_core(wide), core, 1)
    return full.reshape(-1, values.shape[-1])


def scatter_quad(partial_sum, core, col):
    rows, width = partial_sum.shape
    parts = partial_sum.astype(bf16).reshape(2, 2, 2, rows // 8, width)
    sums = (
        pick(parts, core, 1).astype(f32) + swap_core(pick(parts, 1 - core, 1)).astype(f32)
    ).astype(bf16)
    return pick(sums, col, 1).astype(f32) + swap_col(pick(sums, 1 - col, 1)).astype(f32)


def sum_groups(values):
    count = lax.axis_size("dp")
    if count != 4:
        return lax.psum(values, "dp")
    place = lax.axis_index("dp")
    inner = (place == 1) | (place == 2)

    def plus(left, right):
        return (left.astype(f32) + right.astype(f32)).astype(values.dtype)

    first = plus(values, lax.ppermute(values, "dp", [(0, 1), (3, 2)]))
    second = plus(first, lax.ppermute(first, "dp", [(1, 2), (2, 1)]))
    outer = lax.ppermute(second, "dp", [(1, 0), (2, 3)])
    return jnp.where(inner, second, outer)


def fetch_rows(shard, core):
    block, wide = shard.shape
    halves = shard.reshape(block, 2, wide // 2)
    mine = ordered(pick(halves, core, 1), swap_core(pick(halves, 1 - core, 1)), core, 0)
    mine = mine.reshape(2 * block, wide // 2)
    return jnp.concatenate([mine, swap_pair(mine)], axis=0)


def fetch_cols(shard, core):
    tall, block = shard.shape
    halves = shard.reshape(2, tall // 2, block)
    mine = ordered(pick(halves, core, 0), swap_core(pick(halves, 1 - core, 0)), core, 1)
    mine = mine.reshape(tall // 2, 2 * block)
    return jnp.concatenate([mine, swap_pair(mine)], axis=1)


def return_rows(left, right, core):
    half = left.shape[1] // 2
    away = product("rk,rn->kn", left[:, half:], right).astype(bf16)
    own = product("rk,rn->kn", left[:, :half], right).astype(bf16)
    own = (own.astype(f32) + swap_pair(away).astype(f32)).astype(bf16)
    total = sum_groups(own).reshape(2, half // 2, right.shape[1])
    got = swap_core(pick(total, 1 - core, 0))
    return (
        ordered(pick(total, core, 0), got, core, 1)
        .reshape(half // 2, 2 * right.shape[1])
        .astype(f32)
    )


def return_cols(left, right, core):
    half = right.shape[1] // 2
    away = product("rk,rn->kn", left, right[:, half:]).astype(bf16)
    own = product("rk,rn->kn", left, right[:, :half]).astype(bf16)
    own = (own.astype(f32) + swap_pair(away).astype(f32)).astype(bf16)
    total = sum_groups(own).reshape(left.shape[1], 2, half // 2)
    got = swap_core(pick(total, 1 - core, 1))
    return (
        ordered(pick(total, core, 1), got, core, 0)
        .reshape(2 * left.shape[1], half // 2)
        .astype(f32)
    )


def masked_scores(queries, keys, prefix):
    raw_scores = product("ihe,jhe->hij", queries, keys) * queries.shape[2] ** (-0.5)
    raw_scores = raw_scores + prefix.T[:, :, None] - prefix.T[:, None, :]
    places = jnp.arange(keys.shape[0], dtype=jnp.int32)
    return jnp.where(places[None, :] <= places[:, None], raw_scores, masked_score)


def shards(
    tokens,
    seq_lengths,
    seq_slots,
    w_attn,
    w_forget,
    b_forget,
    w_out,
    w_gate,
    w_up,
    w_down,
    gain_attn,
    gain_ffn,
    out_grad,
):
    count_seq = seq_slots.shape[0]
    piece_rows = tokens.shape[2]
    width = tokens.shape[3]
    groups = lax.axis_size("dp")
    row_index = lax.axis_index("row")
    pair, core = row_index // 2, row_index % 2
    col = lax.axis_index("col")
    group = lax.axis_index("dp")
    part_rows = out_grad.shape[2]
    own_heads = b_forget.shape[0] // 2
    all_heads = b_forget.shape[0] * lax.axis_size("col")

    small = jnp.concatenate([w_forget, gain_attn[:, None], gain_ffn[:, None]], axis=1)
    small = ordered(small, swap_core(small), core, 0).reshape(-1, small.shape[1])
    small = jnp.concatenate([small, swap_pair(small)], axis=0)
    forget_full = pick(small[:, : 2 * own_heads].reshape(width, 2, own_heads), core, 1)
    gain_one = small[:, 2 * own_heads].astype(f32)
    gain_two = small[:, 2 * own_heads + 1].astype(f32)
    bias = pick(b_forget.reshape(2, own_heads), core, 0).astype(f32)

    inverse = (
        jnp.zeros((count_seq,), jnp.int32).at[seq_slots].set(jnp.arange(count_seq, dtype=jnp.int32))
    )
    by_pair = inverse.reshape(groups, 2)
    flat_tokens = tokens.reshape(count_seq, piece_rows, width)
    kept = jnp.take(flat_tokens, pick(by_pair, pair, 1), axis=0)
    sent = jnp.take(flat_tokens, pick(by_pair, 1 - pair, 1), axis=0)
    outgoing = turned(ordered(kept, swap_pair(sent), pair, 1), pair)
    outgoing = outgoing.reshape(2 * groups, piece_rows, width)
    rows = lax.all_to_all(outgoing, "dp", split_axis=0, concat_axis=1, tiled=True)

    attn_full = fetch_rows(w_attn, core)
    out_full = fetch_cols(w_out, core)
    gate_full = fetch_rows(w_gate, core)
    up_full = fetch_rows(w_up, core)
    down_full = fetch_cols(w_down, core)

    my_length = seq_lengths[pick(by_pair[group], pair, 0)]
    places = (
        (jnp.arange(2)[:, None] * 4 + 2 * core + col) * part_rows + jnp.arange(part_rows)[None, :]
    ).astype(jnp.int32)
    valid = (places < my_length)[:, :, None]

    rows_val = rows.astype(f32)
    scale_one = inverse_scale(rows_val)
    normed_one = (rows_val * scale_one * gain_one).astype(bf16)
    wide_one = gather_quad(normed_one, core, col)
    length = wide_one.shape[0]
    head_size = attn_full.shape[1] // (4 * own_heads)
    projected = product("rd,de->re", wide_one, attn_full).reshape(length, own_heads, 4, head_size)
    logits = product("rd,dh->rh", wide_one, forget_full) + bias
    queries = projected[:, :, 0, :].astype(bf16)
    keys = projected[:, :, 1, :].astype(bf16)
    vals = projected[:, :, 2, :].astype(bf16)
    gate_sig = jax.nn.sigmoid(projected[:, :, 3, :])
    prefix = jnp.cumsum(jax.nn.log_sigmoid(logits), axis=0)
    scores = masked_scores(queries, keys, prefix)
    log_total = jax.nn.logsumexp(scores, axis=-1, keepdims=True)
    soft_low = jnp.exp(scores - log_total).astype(bf16)
    mixed = product("hij,jhe->ihe", soft_low, vals)
    gated = (mixed * gate_sig).astype(bf16).reshape(length, own_heads * head_size)
    middle = rows_val + scatter_quad(product("rf,fd->rd", gated, out_full), core, col)
    scale_two = inverse_scale(middle)
    normed_two = (middle * scale_two * gain_two).astype(bf16)
    wide_two = gather_quad(normed_two, core, col)
    gate_proj = product("rd,df->rf", wide_two, gate_full)
    up_proj = product("rd,df->rf", wide_two, up_full)
    hidden = (jax.nn.silu(gate_proj) * up_proj).astype(bf16)
    final = middle + scatter_quad(product("rf,fd->rd", hidden, down_full), core, col)
    final = turned(jnp.where(valid, final, 0.0).astype(bf16), pair)
    block_out = ordered(pick(final, pair, 0), swap_pair(pick(final, 1 - pair, 0)), pair, 0)

    cots = out_grad.reshape(2, part_rows, width)
    cots = ordered(pick(cots, pair, 0), swap_pair(pick(cots, 1 - pair, 0)), pair, 0)
    grad_final = jnp.where(valid, turned(cots, pair), jnp.zeros((), bf16))
    wide_grad = gather_quad(grad_final, core, col)
    grad_final = grad_final.astype(f32)
    grad_hidden = product("rd,fd->rf", wide_grad, down_full)
    gate_sigm = jax.nn.sigmoid(gate_proj)
    grad_gate = (grad_hidden * up_proj * gate_sigm * (1.0 + gate_proj * (1.0 - gate_sigm))).astype(
        bf16
    )
    grad_up = (grad_hidden * gate_proj * gate_sigm).astype(bf16)
    grad_normed_two = scatter_quad(
        product("rf,df->rd", grad_gate, gate_full) + product("rf,df->rd", grad_up, up_full),
        core,
        col,
    )
    down_grad = return_cols(hidden, wide_grad, core)
    gate_grad = return_rows(wide_two, grad_gate, core)
    up_grad = return_rows(wide_two, grad_up, core)
    back_two, gain_two_term = norm_backward(middle, scale_two, gain_two, grad_normed_two)
    grad_middle = grad_final + back_two
    wide_mid = gather_quad(grad_middle.astype(bf16), core, col)
    grad_gated = product("rd,fd->rf", wide_mid, out_full).reshape(length, own_heads, head_size)
    out_weight_grad = return_cols(gated, wide_mid, core)
    grad_mixed = (grad_gated * gate_sig).astype(bf16)
    grad_gate_pre = (grad_gated * mixed * gate_sig * (1.0 - gate_sig)).astype(bf16)
    soft_full = jnp.exp(scores - log_total)
    grad_soft = product("ihe,jhe->hij", grad_mixed, vals)
    inner = jnp.sum(soft_full * grad_soft, axis=-1, keepdims=True)
    grad_scores = (soft_full * (grad_soft - inner)).astype(bf16)
    score_scale = head_size ** (-0.5)
    grad_query = (product("hij,jhe->ihe", grad_scores, keys) * score_scale).astype(bf16)
    grad_key = (product("hij,ihe->jhe", grad_scores, queries) * score_scale).astype(bf16)
    grad_value = product("hij,ihe->jhe", soft_low, grad_mixed).astype(bf16)
    score_grad_wide = grad_scores.astype(f32)
    grad_prefix = (jnp.sum(score_grad_wide, axis=2) - jnp.sum(score_grad_wide, axis=1)).T
    grad_decay = jnp.flip(jnp.cumsum(jnp.flip(grad_prefix, 0), axis=0), 0)
    grad_logits = (grad_decay * jax.nn.sigmoid(-logits)).astype(bf16)
    grad_projected = jnp.stack([grad_query, grad_key, grad_value, grad_gate_pre], axis=2).reshape(
        length, own_heads * 4 * head_size
    )
    attn_grad = return_rows(wide_one, grad_projected, core)
    grad_normed_one = scatter_quad(
        product("re,de->rd", grad_projected, attn_full)
        + product("rh,dh->rd", grad_logits, forget_full),
        core,
        col,
    )
    back_one, gain_one_term = norm_backward(rows_val, scale_one, gain_one, grad_normed_one)
    grad_rows = (grad_middle + back_one).astype(bf16)
    returned = turned(
        lax.all_to_all(grad_rows, "dp", split_axis=1, concat_axis=0, tiled=True), pair
    ).reshape(groups, 2, piece_rows, width)
    by_slot = ordered(pick(returned, pair, 1), swap_pair(pick(returned, 1 - pair, 1)), pair, 1)
    tokens_grad = jnp.take(by_slot.reshape(count_seq, piece_rows, width), seq_slots, axis=0)

    forget_term = product("rh,rd->hd", grad_logits, wide_one)
    bias_term = jnp.sum(grad_logits.astype(f32), axis=0)
    tall = -(-(all_heads + 3) // 8) * 8
    pack = jnp.zeros((tall, width), f32)
    first_head = (2 * col + core) * own_heads
    pack = lax.dynamic_update_slice(pack, forget_term, (first_head, 0))
    pack = pack.at[all_heads].set(gain_one_term).at[all_heads + 1].set(gain_two_term)
    pack = turned(pack, pair)
    pack = lax.dynamic_update_slice(pack, bias_term[None], (all_heads + 2, first_head))
    pack = pack + swap_core(pack)
    pack = pack + swap_col(pack)
    pack = pack + swap_pair(pack)
    pack = sum_groups(pack)
    block = gain_attn.shape[0]
    mine = lax.dynamic_slice_in_dim(pack, row_index * block, block, 1)
    forget_grad = lax.dynamic_slice_in_dim(mine, col * 2 * own_heads, 2 * own_heads, 0).T
    bias_grad = lax.dynamic_slice_in_dim(pack[all_heads + 2], col * 2 * own_heads, 2 * own_heads)
    return (
        block_out[:, None],
        tokens_grad[:, None],
        attn_grad,
        forget_grad,
        bias_grad,
        out_weight_grad,
        gate_grad,
        up_grad,
        down_grad,
        mine[all_heads],
        mine[all_heads + 1],
    )


def solution(mesh):
    return jax.shard_map(
        shards,
        mesh=mesh,
        in_specs=(
            P(None, ("row", "col"), "dp", None),
            P(),
            P(),
            P("row", "col"),
            P("row", "col"),
            P("col"),
            P("col", "row"),
            P("row", "col"),
            P("row", "col"),
            P("col", "row"),
            P("row"),
            P("row"),
            P("dp", ("row", "col"), None, None),
        ),
        out_specs=(
            P("dp", ("row", "col"), None, None),
            P(None, ("row", "col"), "dp", None),
            P("row", "col"),
            P("row", "col"),
            P("col"),
            P("col", "row"),
            P("row", "col"),
            P("row", "col"),
            P("col", "row"),
            P("row"),
            P("row"),
        ),
        check_vma=False,
    )
```

```python
import jax
import jax.numpy as jnp
from jax import lax
from jax.experimental import pallas as pl
from jax.experimental.pallas import tpu as pltpu
from jax.sharding import PartitionSpec as P

bf16 = jnp.bfloat16
f32 = jnp.float32
norm_epsilon = 1e-06
masked_score = -1e30
STEP = 256


def after(values, *others):
    return lax.optimization_barrier((values, *others))[0]


def swap_pair(values):
    count = lax.axis_size("row")
    return lax.ppermute(values, "row", [(r, r ^ 2) for r in range(count)])


def swap_core(values):
    count = lax.axis_size("row")
    return lax.ppermute(values, "row", [(r, r ^ 1) for r in range(count)])


def swap_col(values):
    count = lax.axis_size("col")
    return lax.ppermute(values, "col", [(r, r ^ 1) for r in range(count)])


def pick(values, index, axis):
    return lax.dynamic_index_in_dim(values, index, axis, keepdims=False)


def joined(own, other, index, axis):
    return jnp.where(
        index == 0, jnp.concatenate([own, other], axis), jnp.concatenate([other, own], axis)
    )


def turned(values, pair):
    half = values.shape[-1] // 2
    swapped = jnp.concatenate([values[..., half:], values[..., :half]], axis=-1)
    return jnp.where(pair == 0, values, swapped)


def gather_quad(values):
    across = swap_col(values)
    return [values, swap_core(values), across, swap_core(across)]


def dot_nt(left, right):
    return lax.dot_general(left, right, (((1,), (1,)), ((), ())), preferred_element_type=f32)


def dot_nn(left, right):
    return lax.dot_general(left, right, (((1,), (0,)), ((), ())), preferred_element_type=f32)


def dot_tn(left, right):
    return lax.dot_general(left, right, (((0,), (0,)), ((), ())), preferred_element_type=f32)


def shape_of(shape, dtype):
    return jax.ShapeDtypeStruct(shape, dtype)


def run(name, body, grid, ins, in_specs, out_shape, out_specs, scratch=(), scalars=None, alias=None):
    return pl.pallas_call(
        body,
        grid_spec=pltpu.PrefetchScalarGridSpec(
            num_scalar_prefetch=0 if scalars is None else 1,
            grid=grid,
            in_specs=in_specs,
            out_specs=out_specs,
            scratch_shapes=list(scratch),
        ),
        out_shape=out_shape,
        input_output_aliases=alias or {},
        name=name,
    )(*(() if scalars is None else (scalars,)), *ins)


def whole(shape):
    return pl.BlockSpec(shape, lambda *_: (0,) * len(shape))


def add(left, right):
    rows, cols = left.shape
    size = rows // 2

    def body(left_ref, right_ref, out_ref):
        out_ref[...] = (left_ref[...].astype(f32) + right_ref[...].astype(f32)).astype(out_ref.dtype)

    spec = pl.BlockSpec((size, cols), lambda i: (i, 0))
    return run("add", body, (2,), [left, right], [spec] * 2, shape_of(left.shape, left.dtype), spec)


def cut(shard, index, axis):
    shape = list(shard.shape)
    shape[axis] //= 2

    def body(_, in_ref, out_ref):
        out_ref[...] = in_ref[...]

    return run(
        "cut",
        body,
        (1,),
        [shard],
        [pl.BlockSpec(tuple(shape), lambda i, s: (s[0], 0) if axis == 0 else (0, s[0]))],
        shape_of(tuple(shape), shard.dtype),
        whole(tuple(shape)),
        scalars=index.reshape(1),
    )


def lay(got, shard, core, axis):
    rows, cols = got.shape
    out = (2 * rows, cols) if axis == 1 else (rows, 2 * cols)

    def body(s, shard_ref, got_ref, out_ref):
        @pl.when(pl.program_id(0) == s[0])
        def _():
            out_ref[...] = shard_ref[...]

        @pl.when(pl.program_id(0) != s[0])
        def _():
            out_ref[...] = got_ref[...]

    return run(
        "lay",
        body,
        (2,),
        [shard, got],
        [
            pl.BlockSpec((rows, cols), lambda i, s: (0, s[0]) if axis == 1 else (s[0], 0)),
            whole((rows, cols)),
        ],
        shape_of(out, shard.dtype),
        pl.BlockSpec((rows, cols), lambda i, s: (i, 0) if axis == 1 else (0, i)),
        scalars=core.reshape(1),
    )


def lay_two(got_left, got_right, shards, core):
    gots = [got_left, got_right]
    rows, cols = gots[0].shape

    def body(s, left_ref, right_ref, got_left_ref, got_right_ref, out_ref):
        mine = pl.program_id(0) == s[0]
        for at, (own_ref, got_ref) in enumerate(((left_ref, got_left_ref), (right_ref, got_right_ref))):

            @pl.when((pl.program_id(1) == at) & mine)
            def _():
                out_ref[...] = own_ref[...]

            @pl.when((pl.program_id(1) == at) & jnp.logical_not(mine))
            def _():
                out_ref[...] = got_ref[...]

    return run(
        "lay_two",
        body,
        (2, 2),
        [*shards, *gots],
        [pl.BlockSpec((rows, cols), lambda i, j, s: (0, s[0]))] * 2 + [whole((rows, cols))] * 2,
        shape_of((2 * rows, 2 * cols), gots[0].dtype),
        pl.BlockSpec((rows, cols), lambda i, j, s: (i, j)),
        scalars=core.reshape(1),
    )


def inverse_scale(values):
    return lax.rsqrt(jnp.mean(values * values, axis=-1, keepdims=True) + norm_epsilon)


def turn_block(values, pair):
    half = values.shape[-1] // 2
    return jnp.where(
        pair == 0, values, jnp.concatenate([values[..., half:], values[..., :half]], axis=-1)
    )


def norm(rows, gain):
    count, width = rows.shape

    def body(rows_ref, gain_ref, out_ref):
        values = rows_ref[...].astype(f32)
        out_ref[...] = (values * inverse_scale(values) * gain_ref[...]).astype(bf16)

    spec = pl.BlockSpec((count // 2, width), lambda i: (i, 0))
    return run(
        "norm", body, (2,), [rows, gain], [spec, whole((1, width))], shape_of(rows.shape, bf16), spec
    )


def sum_norm(rows, own, beside, across, gain):
    count, width = rows.shape

    def body(rows_ref, own_ref, beside_ref, across_ref, gain_ref, middle_ref, out_ref):
        total = own_ref[...].astype(f32) + beside_ref[...].astype(f32) + across_ref[...].astype(f32)
        values = rows_ref[...].astype(f32) + total
        middle_ref[...] = values
        out_ref[...] = (values * inverse_scale(values) * gain_ref[...]).astype(bf16)

    spec = pl.BlockSpec((count // 2, width), lambda i: (i, 0))
    return run(
        "sum_norm",
        body,
        (2,),
        [rows, own, beside, across, gain],
        [spec] * 4 + [whole((1, width))],
        [shape_of(rows.shape, f32), shape_of(rows.shape, bf16)],
        [spec] * 2,
    )


def norm_backward(values, own, beside, across, base, gain, kind):
    count, width = values.shape
    grid = 2

    def body(values_ref, own_ref, beside_ref, across_ref, base_ref, gain_ref, *out_refs):
        grad = own_ref[...].astype(f32) + beside_ref[...].astype(f32) + across_ref[...].astype(f32)
        vals = values_ref[...].astype(f32)
        scale = inverse_scale(vals)
        weighted = grad * gain_ref[...]
        inner = jnp.mean(weighted * vals, axis=-1, keepdims=True)
        total = base_ref[...].astype(f32) + (scale * weighted - vals * (scale * scale * scale) * inner)
        if kind == "both":
            out_refs[0][...] = total
        out_refs[-2][...] = total.astype(bf16)
        term = jnp.sum(grad * vals * scale, axis=0, keepdims=True)

        @pl.when(pl.program_id(0) == 0)
        def _():
            out_refs[-1][...] = term

        @pl.when(pl.program_id(0) != 0)
        def _():
            out_refs[-1][...] += term

    spec = pl.BlockSpec((count // grid, width), lambda i: (i, 0))
    shapes = [shape_of((count, width), f32)] if kind == "both" else []
    shapes += [shape_of((count, width), bf16), shape_of((1, width), f32)]
    return run(
        "norm_backward",
        body,
        (grid,),
        [values, own, beside, across, base, gain],
        [spec] * 5 + [whole((1, width))],
        shapes,
        [spec] * (len(shapes) - 1) + [whole((1, width))],
    )


def arrange_tokens(arrived, kept, pair):
    groups, size, width = kept.shape

    def body(s, kept_ref, arrived_ref, out_ref):
        @pl.when(pl.program_id(0) == s[0])
        def _():
            out_ref[:, 0] = turn_block(kept_ref[...], s[0])

        @pl.when(pl.program_id(0) != s[0])
        def _():
            out_ref[:, 0] = turn_block(arrived_ref[...], s[0])

    return run(
        "arrange_tokens",
        body,
        (2,),
        [kept, arrived],
        [whole(kept.shape)] * 2,
        shape_of((groups, 2, size, width), bf16),
        pl.BlockSpec((groups, 1, size, width), lambda h, s: (0, h, 0, 0)),
        scalars=pair.reshape(1),
    )


def is_valid(s, half, size):
    first = (half * 4 + 2 * s[1] + s[2]) * size
    return first + lax.broadcasted_iota(jnp.int32, (size, 1), 0) < s[3]


def arrange_cotangent(cots, other, scalars):
    _, size, width = cots.shape

    def body(s, own_ref, other_ref, out_ref):
        half = pl.program_id(0)
        good = is_valid(s, half, size)

        @pl.when(half == s[0])
        def _():
            out_ref[...] = jnp.where(good, turn_block(own_ref[0].astype(f32), s[0]), 0.0).astype(bf16)

        @pl.when(half != s[0])
        def _():
            out_ref[...] = jnp.where(good, turn_block(other_ref[...].astype(f32), s[0]), 0.0).astype(bf16)

    return run(
        "arrange_cotangent",
        body,
        (2,),
        [cots, other],
        [pl.BlockSpec((1, size, width), lambda h, s: (s[0], 0, 0)), whole((size, width))],
        shape_of((2 * size, width), bf16),
        pl.BlockSpec((size, width), lambda h, s: (h, 0)),
        scalars=scalars,
    )


def final_rows(middle, own, beside, across, scalars):
    count, width = middle.shape
    size = count // 2

    def body(s, middle_ref, own_ref, beside_ref, across_ref, out_ref):
        total = own_ref[...].astype(f32) + beside_ref[...].astype(f32) + across_ref[...].astype(f32)
        good = is_valid(s, pl.program_id(0), size)
        out_ref[...] = turn_block(jnp.where(good, middle_ref[...] + total, 0.0), s[0]).astype(bf16)

    spec = pl.BlockSpec((size, width), lambda h, s: (h, 0))
    return run(
        "final_rows",
        body,
        (2,),
        [middle, own, beside, across],
        [spec] * 4,
        shape_of((count, width), bf16),
        spec,
        scalars=scalars,
    )


def part_of(where_ref, chunk, half):
    core = jnp.bitwise_xor(where_ref[0], chunk % 2)
    col = jnp.bitwise_xor(where_ref[1], chunk // 2)
    return half * 4 + core * 2 + col


def scan_lanes(values, backwards):
    count = values.shape[1]
    lane = lax.broadcasted_iota(jnp.int32, values.shape, 1)
    step = 1
    while step < count:
        if backwards:
            moved = pltpu.roll(values, count - step, 1)
            values = values + jnp.where(lane < count - step, moved, 0.0)
        else:
            moved = pltpu.roll(values, step, 1)
            values = values + jnp.where(lane >= step, moved, 0.0)
        step *= 2
    return values


def log_sigmoid(values):
    return jnp.minimum(values, 0.0) - jnp.log1p(jnp.exp(-jnp.abs(values)))


def attention_forward(chunks, own_w, other_w, forget, bias, where, heads, head_size):
    each, width = chunks[0].shape
    count, half = 4 * each, width // 2
    size = count // 8
    pairs = heads // 2
    per = 4 * head_size
    step = min(STEP, count)

    def body(where_ref, x0, x1, x2, x3, own_ref, other_ref, forget_ref, bias_ref,
             gated_ref, rows, mixed_ref, logit_ref, prefix_ref, base_ref, cols):
        pid = pl.program_id(0)
        xs = (x0, x1, x2, x3)

        @pl.when(pid == 0)
        def _():
            for chunk in range(4):
                logits = dot_nt(forget_ref[...], xs[chunk][...]) + bias_ref[:, 0:1]
                for side in range(2):
                    start = pl.multiple_of(part_of(where_ref, chunk, side) * size, size)
                    logit_ref[:, pl.ds(start, size)] = logits[:, side * size : (side + 1) * size]
            sums = scan_lanes(log_sigmoid(logit_ref[...]), False)
            prefix_ref[...] = sums
            for part in range(8):
                block = sums[:, part * size : (part + 1) * size]
                tall = jnp.concatenate([block, jnp.zeros((128 - 8, size), f32)], axis=0)
                cols[part * size : (part + 1) * size, :] = tall.T

        for chunk in range(4):
            made = dot_nn(xs[chunk][:, :half], own_ref[...]) + dot_nn(xs[chunk][:, half:], other_ref[...])
            made = made.astype(bf16)
            for side in range(2):
                start = pl.multiple_of(part_of(where_ref, chunk, side) * size, size)
                rows[pl.ds(start, size), :] = made[side * size : (side + 1) * size]
        lane = lax.broadcasted_iota(jnp.int32, (step, 128), 1)
        apart = lax.broadcasted_iota(jnp.int32, (step, step), 1) <= lax.broadcasted_iota(
            jnp.int32, (step, step), 0
        )
        for first in range(0, count, step):
            last = first + step
            mixed_two, gated_two, base_two = [], [], []
            for side in range(2):
                at = side * per
                head = pid * 2 + side
                query = rows[first:last, at : at + head_size]
                key = rows[0:last, at + head_size : at + 2 * head_size]
                value = rows[0:last, at + 2 * head_size : at + 3 * head_size]
                gate = rows[first:last, at + 3 * head_size : at + 4 * head_size].astype(f32)
                own = jnp.sum(jnp.where(lane == head, cols[first:last, :], 0.0), axis=1, keepdims=True)
                allp = prefix_ref[pl.ds(head, 1), 0:last]
                score = dot_nt(query, key) * head_size ** (-0.5) + own - allp
                tail = jnp.where(apart, score[:, first:last], masked_score)
                score = tail if first == 0 else jnp.concatenate([score[:, :first], tail], axis=1)
                top = jnp.max(score, axis=1, keepdims=True)
                weight = jnp.exp(score - top)
                total = jnp.sum(weight, axis=1, keepdims=True)
                mixed = dot_nn(weight.astype(bf16), value) / total
                mixed_two.append(mixed)
                gated_two.append(mixed * jax.nn.sigmoid(gate))
                base_two.append(own - top - jnp.log(total))
            mixed_ref[first:last, :] = jnp.concatenate(mixed_two, axis=1)
            gated = jnp.concatenate(gated_two, axis=1).astype(bf16)
            base_ref[0, first:last, :] = jnp.where(lane == 0, base_two[0], base_two[1])
            for part in range(first // size, last // size):
                core = jnp.bitwise_xor(where_ref[0], (part // 2) % 2)
                col = jnp.bitwise_xor(where_ref[1], part % 2)
                start = pl.multiple_of(((col * 2 + core) * 2 + part // 4) * size, size)
                off = part * size - first
                gated_ref[pl.ds(start, size), :] = gated[off : off + size]

    return run(
        "attention_forward",
        body,
        (pairs,),
        [*chunks, own_w, other_w, forget, bias],
        [whole((each, width))] * 4
        + [pl.BlockSpec((half, 2 * per), lambda p, w: (0, p))] * 2
        + [whole((8, width)), whole((8, 128))],
        [
            shape_of((count, heads * head_size), bf16),
            shape_of((count, heads * per), bf16),
            shape_of((count, heads * head_size), f32),
            shape_of((8, count), f32),
            shape_of((8, count), f32),
            shape_of((pairs, count, 128), f32),
        ],
        [
            pl.BlockSpec((count, 2 * head_size), lambda p, w: (0, p)),
            pl.BlockSpec((count, 2 * per), lambda p, w: (0, p)),
            pl.BlockSpec((count, 2 * head_size), lambda p, w: (0, p)),
            whole((8, count)),
            whole((8, count)),
            pl.BlockSpec((1, count, 128), lambda p, w: (p, 0, 0)),
        ],
        [pltpu.VMEM((count, 128), f32)],
        where,
    )


def attention_backward(chunks, outs_w, attn_w, forget, saved, where, heads, head_size):
    projected, mixed, logits, prefix, base = saved
    each, width = chunks[0].shape
    count, own_half = 4 * each, width // 2
    size = count // 8
    pairs = heads // 2
    per = 4 * head_size
    step = min(STEP, count)
    scale = head_size ** (-0.5)

    def body(where_ref, m0, m1, m2, m3, out0_ref, out1_ref, attn0_ref, attn1_ref, forget_ref,
             rows, mixes, logit_ref, prefix_ref, base_ref,
             proj_ref, dlog_ref, p0, p1, p2, p3,
             grads, key_sum, value_sum, query_out, places, acc):
        pid = pl.program_id(0)
        for chunk, ref in enumerate((m0, m1, m2, m3)):
            made = dot_nt(ref[:, :own_half], out0_ref[...]) + dot_nt(ref[:, own_half:], out1_ref[...])
            for side in range(2):
                start = pl.multiple_of(part_of(where_ref, chunk, side) * size, size)
                grads[pl.ds(start, size), :] = made[side * size : (side + 1) * size]
        lane_all = lax.broadcasted_iota(jnp.int32, (count, 128), 1)
        apart = lax.broadcasted_iota(jnp.int32, (step, step), 1) <= lax.broadcasted_iota(
            jnp.int32, (step, step), 0
        )
        sums = []
        outs = []
        one = jnp.ones((count, 1), bf16)
        pad = jnp.zeros((count, 128 - head_size - 1), bf16)
        for side in range(2):
            at = side * per
            head = pid * 2 + side
            query = rows[:, at : at + head_size]
            key = rows[:, at + head_size : at + 2 * head_size]
            value = rows[:, at + 2 * head_size : at + 3 * head_size]
            gate = jax.nn.sigmoid(rows[:, at + 3 * head_size : at + 4 * head_size].astype(f32))
            grad = grads[:, side * head_size : (side + 1) * head_size]
            mix = mixes[:, side * head_size : (side + 1) * head_size]
            grad_mix = (grad * gate).astype(bf16)
            inner = jnp.sum(grad_mix.astype(f32) * mix, axis=1, keepdims=True)
            grad_gate = grad * mix * gate * (1.0 - gate)
            query_one = jnp.concatenate([query, one, pad], axis=1)
            key_one = jnp.concatenate([key, one, pad], axis=1)
            key_sum[...] = jnp.zeros((count, 128), f32)
            value_sum[...] = jnp.zeros((count, head_size), f32)
            for first in range(0, count, step):
                last = first + step
                own = base_ref[0, first:last, side : side + 1]
                allp = prefix_ref[pl.ds(head, 1), 0:last]
                score = dot_nt(query[first:last], key[0:last]) * scale + own - allp
                tail = jnp.where(apart, score[:, first:last], masked_score)
                score = tail if first == 0 else jnp.concatenate([score[:, :first], tail], axis=1)
                probs = jnp.exp(score)
                grad_probs = dot_nt(grad_mix[first:last], value[0:last])
                grad_score = (probs * (grad_probs - inner[first:last])).astype(bf16)
                query_out[first:last, :] = dot_nn(grad_score, key_one[0:last])
                key_sum[0:last, :] += dot_tn(grad_score, query_one[first:last])
                value_sum[0:last, :] += dot_tn(probs.astype(bf16), grad_mix[first:last])
            dq = query_out[...]
            dk = key_sum[...]
            sums.append(dq[:, head_size : head_size + 1] - dk[:, head_size : head_size + 1])
            outs += [dq[:, :head_size] * scale, dk[:, :head_size] * scale, value_sum[...], grad_gate]
        full = jnp.concatenate(outs, axis=1).astype(bf16)
        for part in range(8):
            core = jnp.bitwise_xor(where_ref[0], (part // 2) % 2)
            col = jnp.bitwise_xor(where_ref[1], part % 2)
            start = pl.multiple_of(((col * 2 + core) * 2 + part // 4) * size, size)
            proj_ref[pl.ds(start, size), :] = full[part * size : (part + 1) * size]
        both = jnp.where(lane_all == 0, sums[0], jnp.where(lane_all == 1, sums[1], 0.0))

        @pl.when(pid == 0)
        def _():
            places[...] = jnp.zeros((8, count), f32)

        for part in range(8):
            here = slice(part * size, (part + 1) * size)
            flat = both[here].T
            for k in range(pairs):

                @pl.when(pid == k)
                def _():
                    places[2 * k : 2 * k + 2, here] = flat[0:2, :]

        for chunk in range(4):
            here = slice(chunk * each, (chunk + 1) * each)
            block = proj_ref[here, :]
            left = dot_nt(block, attn0_ref[...])
            right = dot_nt(block, attn1_ref[...])

            @pl.when(pid == 0)
            def _():
                acc[here, :own_half] = left
                acc[here, own_half:] = right

            @pl.when(pid != 0)
            def _():
                acc[here, :own_half] += left
                acc[here, own_half:] += right

        @pl.when(pid == pairs - 1)
        def _():
            run_sums = scan_lanes(places[...], True)
            grad_logits = run_sums * jax.nn.sigmoid(-logit_ref[...])
            places[...] = grad_logits
            for chunk, ref in enumerate((p0, p1, p2, p3)):
                for side in range(2):
                    start = pl.multiple_of(part_of(where_ref, chunk, side) * size, size)
                    at = chunk * each + side * size
                    dlog_ref[:, at : at + size] = places[:, pl.ds(start, size)]
                here = slice(chunk * each, (chunk + 1) * each)
                extra = dot_tn(dlog_ref[:, here].astype(bf16), forget_ref[...])
                ref[...] = (acc[here, :] + extra).astype(bf16)

    return run(
        "attention_backward",
        body,
        (pairs,),
        [*chunks, *outs_w, *attn_w, forget, projected, mixed, logits, prefix, base],
        [whole((each, width))] * 4
        + [pl.BlockSpec((2 * head_size, own_half), lambda p, w: (p, 0))] * 2
        + [pl.BlockSpec((own_half, 2 * per), lambda p, w: (0, p))] * 2
        + [
            whole((8, width)),
            pl.BlockSpec((count, 2 * per), lambda p, w: (0, p)),
            pl.BlockSpec((count, 2 * head_size), lambda p, w: (0, p)),
            whole((8, count)),
            whole((8, count)),
            pl.BlockSpec((1, count, 128), lambda p, w: (p, 0, 0)),
        ],
        [shape_of((count, heads * per), bf16), shape_of((8, count), f32)]
        + [shape_of((each, width), bf16)] * 4,
        [pl.BlockSpec((count, 2 * per), lambda p, w: (0, p)), whole((8, count))]
        + [whole((each, width))] * 4,
        [
            pltpu.VMEM((count, 2 * head_size), f32),
            pltpu.VMEM((count, 128), f32),
            pltpu.VMEM((count, head_size), f32),
            pltpu.VMEM((count, 128), f32),
            pltpu.VMEM((8, count), f32),
            pltpu.VMEM((count, width), f32),
        ],
        where,
    )


def to_width(values, own_w, other_w, name):
    count, inner = values.shape
    half = own_w.shape[1]
    each = count // 4

    def body(values_ref, own_ref, other_ref, *out_refs):
        for chunk in (2, 3, 0, 1):
            rows = values_ref[chunk * each : (chunk + 1) * each, :]
            out_refs[chunk][:, :half] = dot_nn(rows, own_ref[...]).astype(bf16)
            out_refs[chunk][:, half:] = dot_nn(rows, other_ref[...]).astype(bf16)

    return run(
        name,
        body,
        (1,),
        [values, own_w, other_w],
        [whole(values.shape), whole(own_w.shape), whole(other_w.shape)],
        [shape_of((each, 2 * half), bf16)] * 4,
        [whole((each, 2 * half))] * 4,
    )


TILE = 256


def ffn_forward(chunks, both_w):
    each, width = chunks[0].shape
    count, half = 4 * each, width // 2
    units = both_w[0].shape[1] // 2
    tiles = units // TILE

    def body(x0, x1, x2, x3, gate0, gate1, up0, up1, gate_ref, up_ref, hidden_ref):
        for chunk, ref in enumerate((x0, x1, x2, x3)):
            here = slice(chunk * each, (chunk + 1) * each)
            gate = dot_nn(ref[:, :half], gate0[...]) + dot_nn(ref[:, half:], gate1[...])
            up = dot_nn(ref[:, :half], up0[...]) + dot_nn(ref[:, half:], up1[...])
            gate_ref[here, :] = gate.astype(bf16)
            up_ref[here, :] = up.astype(bf16)
            hidden_ref[here, :] = (gate * jax.nn.sigmoid(gate) * up).astype(bf16)

    gate_spec = pl.BlockSpec((half, TILE), lambda j: (0, j))
    up_spec = pl.BlockSpec((half, TILE), lambda j: (0, tiles + j))
    out = pl.BlockSpec((count, TILE), lambda j: (0, j))
    return run(
        "ffn_forward",
        body,
        (tiles,),
        [*chunks, *both_w, *both_w],
        [whole((each, width))] * 4 + [gate_spec] * 2 + [up_spec] * 2,
        [shape_of((count, units), bf16)] * 3,
        [out] * 3,
    )


def ffn_backward(chunks, down_w, both_w, gate_proj, up_proj):
    each, width = chunks[0].shape
    count, half = 4 * each, width // 2
    units = both_w[0].shape[1] // 2
    tiles = units // TILE
    last = tiles - 1

    def body(g0, g1, g2, g3, down0, down1, gate0, gate1, up0, up1, gate_ref, up_ref,
             grad_gate_ref, grad_up_ref, p0, p1, p2, p3, acc):
        pid = pl.program_id(0)
        outs = (p0, p1, p2, p3)
        for chunk, ref in enumerate((g0, g1, g2, g3)):
            here = slice(chunk * each, (chunk + 1) * each)
            grad = dot_nt(ref[:, :half], down0[...]) + dot_nt(ref[:, half:], down1[...])
            gate = gate_ref[here, :].astype(f32)
            up = up_ref[here, :].astype(f32)
            sig = jax.nn.sigmoid(gate)
            grad_gate = (grad * up * sig * (1.0 + gate * (1.0 - sig))).astype(bf16)
            grad_up = (grad * gate * sig).astype(bf16)
            grad_gate_ref[here, :] = grad_gate
            grad_up_ref[here, :] = grad_up
            left = dot_nt(grad_gate, gate0[...]) + dot_nt(grad_up, up0[...])
            right = dot_nt(grad_gate, gate1[...]) + dot_nt(grad_up, up1[...])

            @pl.when(pid == 0)
            def _():
                acc[here, :half] = left
                acc[here, half:] = right

            @pl.when(pid != 0)
            def _():
                acc[here, :half] += left
                acc[here, half:] += right

        @pl.when(pid == last)
        def _():
            for chunk in range(4):
                outs[chunk][...] = acc[chunk * each : (chunk + 1) * each, :].astype(bf16)

    tall = pl.BlockSpec((TILE, half), lambda j: (j, 0))
    gate_spec = pl.BlockSpec((half, TILE), lambda j: (0, j))
    up_spec = pl.BlockSpec((half, TILE), lambda j: (0, tiles + j))
    wide = pl.BlockSpec((count, TILE), lambda j: (0, j))
    return run(
        "ffn_backward",
        body,
        (units // TILE,),
        [*chunks, *down_w, *both_w, *both_w, gate_proj, up_proj],
        [whole((each, width))] * 4 + [tall] * 2 + [gate_spec] * 2 + [up_spec] * 2 + [wide] * 2,
        [shape_of((count, units), bf16)] * 2 + [shape_of((each, width), bf16)] * 4,
        [wide] * 2 + [whole((each, width))] * 4,
        [pltpu.VMEM((count, width), f32)],
    )


def grad_rows_weight(chunks, right, side, first, size, got=None):
    each, width = chunks[0].shape
    half = width // 2
    at = first // size
    tiles = half // TILE

    def body(x0, x1, x2, x3, right_ref, *refs):
        total = 0.0 if got is None else refs[0][...].astype(f32)
        for chunk, ref in enumerate((x0, x1, x2, x3)):
            total = total + dot_tn(ref[...], right_ref[chunk * each : (chunk + 1) * each, :])
        refs[-1][...] = total.astype(bf16)

    spec = pl.BlockSpec((TILE, size), lambda j: (j, 0))
    return run(
        "grad_rows_weight",
        body,
        (tiles,),
        [*chunks, right] + ([] if got is None else [got]),
        [pl.BlockSpec((each, TILE), lambda j: (0, side * tiles + j))] * 4
        + [pl.BlockSpec((4 * each, size), lambda j: (0, at))]
        + ([] if got is None else [spec]),
        shape_of((half, size), bf16),
        spec,
    )


def grad_cols_weight(left, chunks, side, first, size, got=None):
    each, width = chunks[0].shape
    half = width // 2
    tile = TILE if size % TILE == 0 else 128
    at = first // tile

    def body(left_ref, x0, x1, x2, x3, *refs):
        total = 0.0 if got is None else refs[0][...].astype(f32)
        for chunk, ref in enumerate((x0, x1, x2, x3)):
            total = total + dot_tn(left_ref[chunk * each : (chunk + 1) * each, :], ref[...])
        refs[-1][...] = total.astype(bf16)

    spec = pl.BlockSpec((tile, half), lambda j: (j, 0))
    return run(
        "grad_cols_weight",
        body,
        (size // tile,),
        [left, *chunks] + ([] if got is None else [got]),
        [pl.BlockSpec((4 * each, tile), lambda j: (0, at + j))]
        + [pl.BlockSpec((each, half), lambda j: (0, side))] * 4
        + ([] if got is None else [spec]),
        shape_of((size, half), bf16),
        spec,
    )


def grad_forget(grad_logits, chunks):
    each, width = chunks[0].shape

    def body(log_ref, x0, x1, x2, x3, out_ref, bias_ref):
        total = 0.0
        low = log_ref[...].astype(bf16)
        for chunk, ref in enumerate((x0, x1, x2, x3)):
            total = total + dot_nn(low[:, chunk * each : (chunk + 1) * each], ref[...])
        out_ref[...] = total
        bias_ref[...] = jnp.broadcast_to(jnp.sum(low.astype(f32), axis=1, keepdims=True), (8, 128))

    return run(
        "grad_forget",
        body,
        (1,),
        [grad_logits, *chunks],
        [whole(grad_logits.shape)] + [whole((each, width))] * 4,
        [shape_of((8, width), f32), shape_of((8, 128), f32)],
        [whole((8, width)), whole((8, 128))],
    )


def chain_one(values):
    return add(values, lax.ppermute(values, "dp", [(0, 1), (3, 2)]))


def chain_two(values):
    return add(values, lax.ppermute(values, "dp", [(1, 2), (2, 1)]))


def chain_three(values):
    return lax.ppermute(values, "dp", [(1, 0), (2, 3)])


def settle(inner, outer, scalars, axis):
    shape = list(inner.shape)
    shape[axis] //= 2

    def body(s, inner_ref, outer_ref, out_ref):
        @pl.when(s[1] == 1)
        def _():
            out_ref[...] = inner_ref[...]

        @pl.when(s[1] != 1)
        def _():
            out_ref[...] = outer_ref[...]

    spec = pl.BlockSpec(tuple(shape), lambda i, s: (1 - s[0], 0) if axis == 0 else (0, 1 - s[0]))
    return run(
        "settle",
        body,
        (1,),
        [inner, outer],
        [spec] * 2,
        shape_of(tuple(shape), inner.dtype),
        whole(tuple(shape)),
        scalars=scalars,
    )


def put(target, shape, inner, outer, got, scalars, axis, piece, pieces):
    rows, cols = got.shape

    def body(s, *refs):
        inner_ref, outer_ref, got_ref = refs[-4:-1]
        out_ref = refs[-1]

        @pl.when((pl.program_id(0) == 0) & (s[1] == 1))
        def _():
            out_ref[...] = inner_ref[...].astype(f32)

        @pl.when((pl.program_id(0) == 0) & (s[1] != 1))
        def _():
            out_ref[...] = outer_ref[...].astype(f32)

        @pl.when(pl.program_id(0) == 1)
        def _():
            out_ref[...] = got_ref[...].astype(f32)

    spec = pl.BlockSpec((rows, cols), lambda i, s: (s[0], 0) if axis == 0 else (0, s[0]))

    def out_map(i, s):
        place = jnp.bitwise_xor(s[0], i) * pieces + piece
        return (0, place) if axis == 0 else (place, 0)

    first = target is None
    return run(
        "put",
        body,
        (2,),
        ([] if first else [target]) + [inner, outer, got],
        ([] if first else [pl.BlockSpec(memory_space=pl.ANY)]) + [spec] * 2 + [whole((rows, cols))],
        shape_of(shape, f32),
        pl.BlockSpec((rows, cols), out_map),
        scalars=scalars,
        alias=None if first else {1: 0},
    )


def shards(
    tokens,
    seq_lengths,
    seq_slots,
    w_attn,
    w_forget,
    b_forget,
    w_out,
    w_gate,
    w_up,
    w_down,
    gain_attn,
    gain_ffn,
    out_grad,
):
    count_seq = seq_slots.shape[0]
    piece_rows = tokens.shape[2]
    width = tokens.shape[3]
    groups = lax.axis_size("dp")
    row_index = lax.axis_index("row")
    pair, core = row_index // 2, row_index % 2
    col = lax.axis_index("col")
    group = lax.axis_index("dp")
    part_rows = out_grad.shape[2]
    own_heads = b_forget.shape[0] // 2
    all_heads = b_forget.shape[0] * lax.axis_size("col")
    head_size = w_out.shape[0] // (2 * own_heads)
    where = jnp.stack([core, col]).astype(jnp.int32)

    order = [None]

    def tie(values):
        return values if order[0] is None else after(values, order[0])

    def step(op, values, *others):
        out = op(tie(values), *others)
        order[0] = out[0] if isinstance(out, (list, tuple)) else out
        return out

    inverse = (
        jnp.zeros((count_seq,), jnp.int32).at[seq_slots].set(jnp.arange(count_seq, dtype=jnp.int32))
    )
    by_pair = inverse.reshape(groups, 2)
    my_length = seq_lengths[pick(by_pair[group], pair, 0)]
    scalars = jnp.stack([pair, core, col, my_length]).astype(jnp.int32)
    flat_tokens = tokens.reshape(count_seq, piece_rows, width)

    small = jnp.concatenate([w_forget.T, gain_attn[None], gain_ffn[None]], axis=0)
    small = joined(small, swap_core(small), core, 1)
    attn_got = swap_core(cut(w_attn, 1 - core, 1))
    sent = jnp.take(flat_tokens, pick(by_pair, 1 - pair, 1), axis=0)
    kept = jnp.take(flat_tokens, pick(by_pair, pair, 1), axis=0)
    arrived = swap_pair(sent)
    cots = out_grad.reshape(2, part_rows, width)
    tall = -(-small.shape[0] // 8) * 8
    payload = jnp.concatenate(
        [
            after(pick(cots, 1 - pair, 0), sent),
            jnp.pad(small, ((0, tall - small.shape[0]), (0, width // 2))),
        ],
        axis=0,
    )
    payload_got = swap_pair(payload)
    order[0] = payload

    attn_own = step(lay, attn_got, w_attn, core, 1)
    outgoing = step(arrange_tokens, arrived, kept, pair)
    outgoing = outgoing.reshape(2 * groups, piece_rows, width)
    rows = lax.all_to_all(outgoing, "dp", split_axis=0, concat_axis=1, tiled=True)
    rows = rows.reshape(2 * part_rows, width)
    attn_other = swap_pair(after(attn_own, payload_got, outgoing))
    attn_w = [attn_own, attn_other]
    order[0] = outgoing
    out_cut = step(cut, w_out, 1 - core, 0)
    gate_cut = step(cut, w_gate, 1 - core, 1)
    up_cut = step(cut, w_up, 1 - core, 1)
    down_cut = step(cut, w_down, 1 - core, 0)
    out_own = step(lay, swap_core(out_cut), w_out, core, 0)
    both_own = step(lay_two, swap_core(gate_cut), swap_core(up_cut), [w_gate, w_up], core)
    down_own = step(lay, swap_core(down_cut), w_down, core, 0)
    out_w = [out_own, swap_pair(out_own)]
    both_w = [both_own, swap_pair(both_own)]
    down_w = [down_own, swap_pair(down_own)]

    small_got = payload_got[part_rows : part_rows + small.shape[0], : width // 2]
    small = jnp.concatenate([small, small_got], axis=1)
    forget = pick(small[: 2 * own_heads].reshape(2, own_heads, width), core, 0)
    forget = jnp.pad(forget, ((0, 8 - own_heads), (0, 0)))
    gain_one = small[2 * own_heads : 2 * own_heads + 1].astype(f32)
    gain_two = small[2 * own_heads + 1 : 2 * own_heads + 2].astype(f32)
    bias = pick(b_forget.reshape(2, own_heads), core, 0).astype(f32)
    bias = jnp.broadcast_to(jnp.pad(bias, (0, 8 - own_heads))[:, None], (8, 128))

    normed_one = step(norm, rows, gain_one)
    wide_one = gather_quad(normed_one)
    grad_final = step(arrange_cotangent, cots, payload_got, scalars)
    wide_grad = gather_quad(grad_final)
    gated, *saved = step(
        attention_forward, wide_one, *attn_w, forget, bias, where, own_heads, head_size
    )
    part = step(to_width, gated, *out_w, "out_forward")
    sent_one = step(add, part[2], swap_core(part[3]))
    middle, normed_two = step(sum_norm, rows, part[0], swap_core(part[1]), swap_col(sent_one), gain_two)
    wide_two = gather_quad(normed_two)
    gate_proj, up_proj, hidden = step(ffn_forward, wide_two, both_w)

    inner = ((group == 1) | (group == 2)) if groups == 4 else (group >= 0)
    flags = jnp.stack([core, inner.astype(jnp.int32)]).astype(jnp.int32)
    shapes = {"down": w_down.shape, "gate": w_gate.shape, "up": w_up.shape, "out": w_out.shape, "attn": w_attn.shape}
    grads = {name: None for name in shapes}
    state = {}

    def unit(name, kind, left, right, piece=0, pieces=1):
        full = (right if kind is grad_rows_weight else left).shape[1]
        size = full // pieces
        first = piece * size
        away = step(lambda v: kind(v, right, 1, first, size), left)
        state[name, piece] = [kind, left, right, first, size, pieces, swap_pair(away)]

    def own(name, piece=0):
        kind, left, right, first, size, pieces, got = state[name, piece]
        mine = step(lambda v: kind(v, right, 0, first, size, got), left)
        if groups == 4:
            got = lax.ppermute(mine, "dp", [(0, 1), (3, 2)])
        state[name, piece] = [kind, pieces, mine, got]

    def one(name, piece=0):
        kind, pieces, mine, got = state[name, piece]
        if groups == 4:
            mine = step(add, mine, got)
            got = lax.ppermute(mine, "dp", [(1, 2), (2, 1)])
        state[name, piece] = [kind, pieces, mine, got]

    def two(name, piece=0):
        kind, pieces, mine, got = state[name, piece]
        if groups == 4:
            mine = step(add, mine, got)
            got = lax.ppermute(mine, "dp", [(1, 0), (2, 3)])
        else:
            mine = got = lax.psum(mine, "dp")
        state[name, piece] = [kind, pieces, mine, got]

    def three(name, piece=0):
        kind, pieces, mine, got = state[name, piece]
        axis = 0 if kind is grad_rows_weight else 1
        state[name, piece] += [axis, swap_core(step(settle, mine, got, flags, axis))]

    def four(name, piece=0):
        kind, pieces, mine, got, axis, beside = state[name, piece]
        grads[name] = step(
            lambda v: put(grads[name], shapes[name], mine, got, v, flags, axis, piece, pieces), beside
        )

    unit("down", grad_cols_weight, hidden, wide_grad)
    grad_gate, grad_up, *part = step(ffn_backward, wide_grad, down_w, both_w, gate_proj, up_proj)
    unit("gate", grad_rows_weight, wide_two, grad_gate)
    sent_three = step(add, part[2], swap_core(part[3]))
    unit("up", grad_rows_weight, wide_two, grad_up)
    own("down")
    grad_middle, grad_attn, gain_two_term = step(
        norm_backward, middle, part[0], swap_core(part[1]), swap_col(sent_three), grad_final, gain_two, "both"
    )
    wide_mid = gather_quad(grad_attn)
    part = step(to_width, hidden, *down_w, "down_forward")
    sent_two = step(add, part[2], swap_core(part[3]))
    final_parts = [part[0], swap_core(part[1]), swap_col(sent_two)]
    own("gate")
    unit("out", grad_cols_weight, gated, wide_mid)
    grad_projected, grad_logits, *part = step(
        attention_backward, wide_mid, out_w, attn_w, forget, saved, where, own_heads, head_size
    )
    one("down")
    own("up")
    unit("attn", grad_rows_weight, wide_one, grad_projected, 0, 3)
    unit("attn", grad_rows_weight, wide_one, grad_projected, 1, 3)
    sent_four = step(add, part[2], swap_core(part[3]))
    unit("attn", grad_rows_weight, wide_one, grad_projected, 2, 3)
    one("gate")
    own("out")
    final = step(final_rows, middle, *final_parts, scalars).reshape(2, part_rows, width)
    final_other = swap_pair(pick(final, 1 - pair, 0))
    two("down")
    grad_rows, gain_one_term = step(
        norm_backward, rows, part[0], swap_core(part[1]), swap_col(sent_four), grad_middle, gain_one, "rounded"
    )
    returned = lax.all_to_all(
        grad_rows.reshape(2, part_rows, width), "dp", split_axis=1, concat_axis=0, tiled=True
    )
    own("attn", 0)
    forget_term, bias_term = step(grad_forget, grad_logits, wide_one)
    one("up")
    own("attn", 1)
    two("gate")
    one("out")
    own("attn", 2)
    one("attn", 0)
    three("down")
    two("up")

    returned = step(turned, returned, pair).reshape(groups, 2, piece_rows, width)
    back = swap_pair(pick(returned, 1 - pair, 1))

    tall = -(-(all_heads + 3) // 8) * 8
    pack = jnp.zeros((tall, width), f32)
    first_head = (2 * col + core) * own_heads
    pack = lax.dynamic_update_slice(pack, tie(forget_term)[:own_heads], (first_head, 0))
    pack = pack.at[all_heads].set(gain_one_term[0]).at[all_heads + 1].set(gain_two_term[0])
    pack = turned(pack, pair)
    pack = lax.dynamic_update_slice(pack, bias_term[:own_heads, 0][None], (all_heads + 2, first_head))
    pack = pack + swap_core(pack)
    order[0] = pack
    four("down")
    two("out")
    one("attn", 1)
    pack = tie(pack) + swap_col(pack)
    two("attn", 0)
    one("attn", 2)
    three("gate")
    pack = tie(pack) + swap_pair(pack)
    order[0] = pack
    four("gate")
    if groups == 4:
        pack = tie(pack) + lax.ppermute(pack, "dp", [(0, 1), (3, 2)])
        order[0] = pack
    two("attn", 1)
    three("up")
    two("attn", 2)
    four("up")
    if groups == 4:
        pack = tie(pack) + lax.ppermute(pack, "dp", [(1, 2), (2, 1)])
        pack_got = lax.ppermute(pack, "dp", [(1, 0), (2, 3)])
        order[0] = pack
    stay = tie(pick(returned, pair, 1))
    by_slot = jnp.stack([jnp.where(pair == 0, stay, back), jnp.where(pair == 0, back, stay)], 1)
    tokens_grad = jnp.take(by_slot.reshape(count_seq, piece_rows, width), seq_slots, axis=0)
    order[0] = tokens_grad
    block_out = joined(tie(pick(final, pair, 0))[None], final_other[None], pair, 0)
    order[0] = block_out
    three("out")
    three("attn", 0)
    four("out")
    three("attn", 1)
    four("attn", 0)
    three("attn", 2)
    four("attn", 1)
    four("attn", 2)
    if groups == 4:
        pack = jnp.where(inner, tie(pack), pack_got)
    else:
        pack = lax.psum(pack, "dp")
    block = gain_attn.shape[0]
    mine = lax.dynamic_slice_in_dim(pack, row_index * block, block, 1)
    forget_grad = lax.dynamic_slice_in_dim(mine, col * 2 * own_heads, 2 * own_heads, 0).T
    bias_grad = lax.dynamic_slice_in_dim(pack[all_heads + 2], col * 2 * own_heads, 2 * own_heads)
    return (
        block_out[:, None],
        tokens_grad[:, None],
        grads["attn"],
        forget_grad,
        bias_grad,
        grads["out"],
        grads["gate"],
        grads["up"],
        grads["down"],
        mine[all_heads],
        mine[all_heads + 1],
    )


def solution(mesh):
    return jax.shard_map(
        shards,
        mesh=mesh,
        in_specs=(
            P(None, ("row", "col"), "dp", None),
            P(),
            P(),
            P("row", "col"),
            P("row", "col"),
            P("col"),
            P("col", "row"),
            P("row", "col"),
            P("row", "col"),
            P("col", "row"),
            P("row"),
            P("row"),
            P("dp", ("row", "col"), None, None),
        ),
        out_specs=(
            P("dp", ("row", "col"), None, None),
            P(None, ("row", "col"), "dp", None),
            P("row", "col"),
            P("row", "col"),
            P("col"),
            P("col", "row"),
            P("row", "col"),
            P("row", "col"),
            P("col", "row"),
            P("row"),
            P("row"),
        ),
        check_vma=False,
    )
```

```python
import jax
import jax.numpy as jnp
from jax import lax
from jax.experimental import pallas as pl
from jax.experimental.pallas import tpu as pltpu
from jax.sharding import PartitionSpec as P

bf16 = jnp.bfloat16
f32 = jnp.float32
norm_epsilon = 1e-06
masked_score = -1e30
STEP = 256


def after(values, *others):
    return lax.optimization_barrier((values, *others))[0]


def swap_pair(values):
    count = lax.axis_size("row")
    return lax.ppermute(values, "row", [(r, r ^ 2) for r in range(count)])


def swap_core(values):
    count = lax.axis_size("row")
    return lax.ppermute(values, "row", [(r, r ^ 1) for r in range(count)])


def swap_col(values):
    count = lax.axis_size("col")
    return lax.ppermute(values, "col", [(r, r ^ 1) for r in range(count)])


def pick(values, index, axis):
    return lax.dynamic_index_in_dim(values, index, axis, keepdims=False)


def joined(own, other, index, axis):
    return jnp.where(
        index == 0, jnp.concatenate([own, other], axis), jnp.concatenate([other, own], axis)
    )


def turned(values, pair):
    half = values.shape[-1] // 2
    swapped = jnp.concatenate([values[..., half:], values[..., :half]], axis=-1)
    return jnp.where(pair == 0, values, swapped)


def gather_quad(values):
    across = swap_col(values)
    return [values, swap_core(values), across, swap_core(across)]


def dot_nt(left, right):
    return lax.dot_general(left, right, (((1,), (1,)), ((), ())), preferred_element_type=f32)


def dot_nn(left, right):
    return lax.dot_general(left, right, (((1,), (0,)), ((), ())), preferred_element_type=f32)


def dot_tn(left, right):
    return lax.dot_general(left, right, (((0,), (0,)), ((), ())), preferred_element_type=f32)


def shape_of(shape, dtype):
    return jax.ShapeDtypeStruct(shape, dtype)


VMEM = pl.BlockSpec(memory_space=pltpu.VMEM)
SMEM = pl.BlockSpec(memory_space=pltpu.SMEM)


def near(name, body, ins, out_shape, scratch=(), scalars=None, grid=(), limit=6, in_specs=None, out_specs=None, alias=None):
    specs = in_specs or [VMEM] * len(ins)
    if out_specs is None:
        out_specs = [VMEM] * len(out_shape) if isinstance(out_shape, list) else VMEM
    return pl.pallas_call(
        body,
        grid=grid,
        in_specs=specs if scalars is None else [SMEM, *specs],
        out_specs=out_specs,
        out_shape=out_shape,
        scratch_shapes=list(scratch),
        input_output_aliases=alias or {},
        compiler_params=pltpu.CompilerParams(vmem_limit_bytes=limit << 20),
        name=name,
    )(*(() if scalars is None else (scalars,)), *ins)


def add(left, right):
    def body(left_ref, right_ref, out_ref):
        out_ref[...] = (left_ref[...].astype(f32) + right_ref[...].astype(f32)).astype(out_ref.dtype)

    return near("add", body, [left, right], shape_of(left.shape, left.dtype))


def cut(shard, index, axis, pieces=2):
    shape = list(shard.shape)
    shape[axis] //= pieces

    def body(_, in_ref, out_ref):
        out_ref[...] = in_ref[...]

    return pl.pallas_call(
        body,
        grid_spec=pltpu.PrefetchScalarGridSpec(
            num_scalar_prefetch=1,
            grid=(1,),
            in_specs=[pl.BlockSpec(tuple(shape), lambda i, s: (s[0], 0) if axis == 0 else (0, s[0]))],
            out_specs=VMEM,
        ),
        out_shape=shape_of(tuple(shape), shard.dtype),
        compiler_params=pltpu.CompilerParams(vmem_limit_bytes=8 << 20),
        name="cut",
    )(index.reshape(1).astype(jnp.int32), shard)


def lay(got, shard, core, axis):
    rows, cols = got.shape
    out = (2 * rows, cols) if axis == 1 else (rows, 2 * cols)

    def body(s, got_ref, shard_ref, out_ref):
        for place in range(2):

            @pl.when(s[0] == place)
            def _():
                if axis == 1:
                    out_ref[place * rows : (place + 1) * rows, :] = shard_ref[...]
                    out_ref[(1 - place) * rows : (2 - place) * rows, :] = got_ref[...]
                else:
                    out_ref[:, place * cols : (place + 1) * cols] = shard_ref[...]
                    out_ref[:, (1 - place) * cols : (2 - place) * cols] = got_ref[...]

    return pl.pallas_call(
        body,
        grid_spec=pltpu.PrefetchScalarGridSpec(
            num_scalar_prefetch=1,
            grid=(1,),
            in_specs=[
                VMEM,
                pl.BlockSpec((rows, cols), lambda i, s: (0, s[0]) if axis == 1 else (s[0], 0)),
            ],
            out_specs=VMEM,
        ),
        out_shape=shape_of(out, shard.dtype),
        compiler_params=pltpu.CompilerParams(vmem_limit_bytes=8 << 20),
        name="lay",
    )(core.reshape(1).astype(jnp.int32), got, shard)


def inverse_scale(values):
    return lax.rsqrt(jnp.mean(values * values, axis=-1, keepdims=True) + norm_epsilon)


def turn_block(values, pair):
    half = values.shape[-1] // 2
    return jnp.where(
        pair == 0, values, jnp.concatenate([values[..., half:], values[..., :half]], axis=-1)
    )


SLAB = 64


def slabs(count):
    return [slice(at, at + SLAB) for at in range(0, count, SLAB)]


def norm(rows, gain):
    def body(rows_ref, gain_ref, out_ref):
        for here in slabs(rows.shape[0]):
            values = rows_ref[here, :].astype(f32)
            out_ref[here, :] = (values * inverse_scale(values) * gain_ref[...]).astype(bf16)

    return near("norm", body, [rows, gain], shape_of(rows.shape, bf16))


def sum_norm(rows, own, beside, across, gain):
    def body(rows_ref, own_ref, beside_ref, across_ref, gain_ref, middle_ref, out_ref):
        for here in slabs(rows.shape[0]):
            total = own_ref[here, :].astype(f32) + beside_ref[here, :].astype(f32)
            values = rows_ref[here, :].astype(f32) + (total + across_ref[here, :].astype(f32))
            middle_ref[here, :] = values
            out_ref[here, :] = (values * inverse_scale(values) * gain_ref[...]).astype(bf16)

    return near(
        "sum_norm",
        body,
        [rows, own, beside, across, gain],
        [shape_of(rows.shape, f32), shape_of(rows.shape, bf16)],
    )


def norm_backward(values, own, beside, across, base, gain, pair=None, groups=None):
    count, width = values.shape
    size = count // 2
    piece = size // (groups or 1)

    def body(s, values_ref, own_ref, beside_ref, across_ref, base_ref, gain_ref, *out_refs):
        term = jnp.zeros((1, width), f32)
        for here in slabs(count):
            grad = own_ref[here, :].astype(f32) + beside_ref[here, :].astype(f32) + across_ref[here, :].astype(f32)
            vals = values_ref[here, :].astype(f32)
            scale = inverse_scale(vals)
            weighted = grad * gain_ref[...]
            inner = jnp.mean(weighted * vals, axis=-1, keepdims=True)
            total = scale * weighted - vals * (scale * scale * scale) * inner
            total = base_ref[here, :].astype(f32) + total
            if groups is None:
                out_refs[0][here, :] = total
                out_refs[1][here, :] = total.astype(bf16)
            else:
                total = turn_block(total, s[0])
                step = min(piece, SLAB)
                for at in range(here.start, here.stop, step):
                    side, rest = at // size, at % size
                    group, first = rest // piece, rest % piece
                    rows = total[at - here.start : at - here.start + step]
                    out_refs[0][group, side, first : first + step, :] = rows.astype(bf16)
            term = term + jnp.sum(grad * vals * scale, axis=0, keepdims=True)
        out_refs[-1][...] = term

    if groups is None:
        shapes = [shape_of((count, width), f32), shape_of((count, width), bf16)]
    else:
        shapes = [shape_of((groups, 2, piece, width), bf16)]
    return near(
        "norm_backward",
        body,
        [values, own, beside, across, base, gain],
        [*shapes, shape_of((1, width), f32)],
        scalars=jnp.zeros((1,), jnp.int32) if pair is None else pair.reshape(1),
    )


def arrange_tokens(arrived, kept, pair):
    groups, size, width = kept.shape

    def body(s, arrived_ref, kept_ref, out_ref):
        for place in range(2):

            @pl.when(s[0] == place)
            def _():
                for group in range(groups):
                    out_ref[group, place] = turn_block(kept_ref[group], s[0])
                    out_ref[group, 1 - place] = turn_block(arrived_ref[group], s[0])

    return near(
        "arrange_tokens",
        body,
        [arrived, kept],
        shape_of((groups, 2, size, width), bf16),
        scalars=pair.reshape(1),
    )


def is_valid(s, half, size):
    first = (half * 4 + 2 * s[1] + s[2]) * size
    return first + lax.broadcasted_iota(jnp.int32, (size, 1), 0) < s[3]


def arrange_cotangent(cots, other, scalars):
    _, size, width = cots.shape

    def body(s, own_ref, other_ref, out_ref):
        for half in range(2):
            good = is_valid(s, half, size)

            @pl.when(half == s[0])
            def _():
                rows = turn_block(own_ref[half].astype(f32), s[0])
                out_ref[half * size : (half + 1) * size, :] = jnp.where(good, rows, 0.0).astype(bf16)

            @pl.when(half != s[0])
            def _():
                rows = turn_block(other_ref[0:size, :].astype(f32), s[0])
                out_ref[half * size : (half + 1) * size, :] = jnp.where(good, rows, 0.0).astype(bf16)

    return near(
        "arrange_cotangent",
        body,
        [cots, other],
        shape_of((2 * size, width), bf16),
        scalars=scalars,
    )


def final_rows(middle, own, beside, across, scalars):
    count, width = middle.shape
    size = count // 2

    def body(s, middle_ref, own_ref, beside_ref, across_ref, out_ref, away_ref):
        for half in range(2):
            good = is_valid(s, half, size)
            here = slice(half * size, (half + 1) * size)
            total = own_ref[here, :].astype(f32) + beside_ref[here, :].astype(f32)
            total = middle_ref[here, :] + (total + across_ref[here, :].astype(f32))
            rows = turn_block(jnp.where(good, total, 0.0), s[0]).astype(bf16)

            @pl.when(half == s[0])
            def _():
                out_ref[...] = rows

            @pl.when(half != s[0])
            def _():
                away_ref[...] = rows

    return near(
        "final_rows",
        body,
        [middle, own, beside, across],
        [shape_of((size, width), bf16)] * 2,
        scalars=scalars,
    )


def part_of(where_ref, chunk, half):
    core = jnp.bitwise_xor(where_ref[0], chunk % 2)
    col = jnp.bitwise_xor(where_ref[1], chunk // 2)
    return half * 4 + core * 2 + col


def scan_lanes(values, backwards):
    count = values.shape[1]
    lane = lax.broadcasted_iota(jnp.int32, values.shape, 1)
    step = 1
    while step < count:
        if backwards:
            moved = pltpu.roll(values, count - step, 1)
            values = values + jnp.where(lane < count - step, moved, 0.0)
        else:
            moved = pltpu.roll(values, step, 1)
            values = values + jnp.where(lane >= step, moved, 0.0)
        step *= 2
    return values


def log_sigmoid(values):
    return jnp.minimum(values, 0.0) - jnp.log1p(jnp.exp(-jnp.abs(values)))


def attention_forward(chunks, own_w, other_w, forget, bias, where, heads, head_size):
    each, width = chunks[0].shape
    count, half = 4 * each, width // 2
    size = count // 8
    pairs = heads // 2
    per = 4 * head_size
    step = min(STEP, count)

    def body(where_ref, x0, x1, x2, x3, own_ref, other_ref, forget_ref, bias_ref,
             gated_ref, proj_ref, mixed_ref, logit_ref, prefix_ref, base_ref, rows, cols):
        pid = pl.program_id(0)
        lanes = pl.multiple_of(pid * 2 * per, 2 * per)
        pair_lanes = pl.multiple_of(pid * 2 * head_size, 2 * head_size)
        xs = (x0, x1, x2, x3)

        @pl.when(pid == 0)
        def _():
            for chunk in range(4):
                logits = dot_nt(forget_ref[...], xs[chunk][...]) + bias_ref[:, 0:1]
                for side in range(2):
                    start = pl.multiple_of(part_of(where_ref, chunk, side) * size, size)
                    logit_ref[:, pl.ds(start, size)] = logits[:, side * size : (side + 1) * size]
            sums = scan_lanes(log_sigmoid(logit_ref[...]), False)
            prefix_ref[...] = sums
            for part in range(8):
                block = sums[:, part * size : (part + 1) * size]
                tall = jnp.concatenate([block, jnp.zeros((128 - 8, size), f32)], axis=0)
                cols[part * size : (part + 1) * size, :] = tall.T

        for chunk in range(4):
            made = dot_nn(xs[chunk][:, :half], own_ref[:, pl.ds(lanes, 2 * per)])
            made = (made + dot_nn(xs[chunk][:, half:], other_ref[:, pl.ds(lanes, 2 * per)])).astype(bf16)
            for side in range(2):
                start = pl.multiple_of(part_of(where_ref, chunk, side) * size, size)
                rows[pl.ds(start, size), :] = made[side * size : (side + 1) * size]
        proj_ref[:, pl.ds(lanes, 2 * per)] = rows[...]
        lane = lax.broadcasted_iota(jnp.int32, (step, 128), 1)
        apart = lax.broadcasted_iota(jnp.int32, (step, step), 1) <= lax.broadcasted_iota(
            jnp.int32, (step, step), 0
        )
        for first in range(0, count, step):
            last = first + step
            mixed_two, gated_two, base_two = [], [], []
            for side in range(2):
                at = side * per
                head = pid * 2 + side
                query = rows[first:last, at : at + head_size]
                key = rows[0:last, at + head_size : at + 2 * head_size]
                value = rows[0:last, at + 2 * head_size : at + 3 * head_size]
                gate = rows[first:last, at + 3 * head_size : at + 4 * head_size].astype(f32)
                own = jnp.sum(jnp.where(lane == head, cols[first:last, :], 0.0), axis=1, keepdims=True)
                allp = prefix_ref[pl.ds(head, 1), 0:last]
                score = dot_nt(query, key) * head_size ** (-0.5) + own - allp
                tail = jnp.where(apart, score[:, first:last], masked_score)
                score = tail if first == 0 else jnp.concatenate([score[:, :first], tail], axis=1)
                top = jnp.max(score, axis=1, keepdims=True)
                weight = jnp.exp(score - top)
                total = jnp.sum(weight, axis=1, keepdims=True)
                mixed = dot_nn(weight.astype(bf16), value) / total
                mixed_two.append(mixed)
                gated_two.append(mixed * jax.nn.sigmoid(gate))
                base_two.append(own - top - jnp.log(total))
            mixed_ref[first:last, pl.ds(pair_lanes, 2 * head_size)] = jnp.concatenate(mixed_two, axis=1)
            gated = jnp.concatenate(gated_two, axis=1).astype(bf16)
            base_ref[pid, first:last, :] = jnp.where(lane == 0, base_two[0], base_two[1])
            for part in range(first // size, last // size):
                core = jnp.bitwise_xor(where_ref[0], (part // 2) % 2)
                col = jnp.bitwise_xor(where_ref[1], part % 2)
                start = pl.multiple_of(((col * 2 + core) * 2 + part // 4) * size, size)
                off = part * size - first
                gated_ref[pl.ds(start, size), pl.ds(pair_lanes, 2 * head_size)] = gated[off : off + size]

    return near(
        "attention_forward",
        body,
        [*chunks, own_w, other_w, forget, bias],
        [
            shape_of((count, heads * head_size), bf16),
            shape_of((count, heads * per), bf16),
            shape_of((count, heads * head_size), f32),
            shape_of((8, count), f32),
            shape_of((8, count), f32),
            shape_of((pairs, count, 128), f32),
        ],
        [pltpu.VMEM((count, 2 * per), bf16), pltpu.VMEM((count, 128), f32)],
        where,
        grid=(pairs,),
        limit=12,
    )


def attention_backward(chunks, out_w, saved, where, pid, head_size):
    projected, mixed, logits, prefix, base = saved
    each, width = chunks[0].shape
    count, own_half = 4 * each, width // 2
    size = count // 8
    per = 4 * head_size
    step = min(STEP, count)
    scale = head_size ** (-0.5)

    def body(where_ref, m0, m1, m2, m3, out0_ref, out1_ref, saved_ref, mixes_ref, prefix_ref, base_ref,
             proj_ref, places_ref, rows, grads, key_sum, value_sum, query_out):
        for chunk, ref in enumerate((m0, m1, m2, m3)):
            here = slice(pid * 2 * head_size, (pid + 1) * 2 * head_size)
            made = dot_nt(ref[:, :own_half], out0_ref[here, :])
            made = made + dot_nt(ref[:, own_half:], out1_ref[here, :])
            for side in range(2):
                start = pl.multiple_of(part_of(where_ref, chunk, side) * size, size)
                grads[pl.ds(start, size), :] = made[side * size : (side + 1) * size]
        rows[...] = saved_ref[:, pid * 2 * per : (pid + 1) * 2 * per]
        lane_all = lax.broadcasted_iota(jnp.int32, (count, 128), 1)
        apart = lax.broadcasted_iota(jnp.int32, (step, step), 1) <= lax.broadcasted_iota(
            jnp.int32, (step, step), 0
        )
        sums = []
        outs = []
        one = jnp.ones((count, 1), bf16)
        pad = jnp.zeros((count, 128 - head_size - 1), bf16)
        for side in range(2):
            at = side * per
            head = pid * 2 + side
            query = rows[:, at : at + head_size]
            key = rows[:, at + head_size : at + 2 * head_size]
            value = rows[:, at + 2 * head_size : at + 3 * head_size]
            gate = jax.nn.sigmoid(rows[:, at + 3 * head_size : at + 4 * head_size].astype(f32))
            grad = grads[:, side * head_size : (side + 1) * head_size]
            mix = mixes_ref[:, (pid * 2 + side) * head_size : (pid * 2 + side + 1) * head_size]
            grad_mix = (grad * gate).astype(bf16)
            inner = jnp.sum(grad_mix.astype(f32) * mix, axis=1, keepdims=True)
            grad_gate = grad * mix * gate * (1.0 - gate)
            query_one = jnp.concatenate([query, one, pad], axis=1)
            key_one = jnp.concatenate([key, one, pad], axis=1)
            key_sum[...] = jnp.zeros((count, 128), f32)
            value_sum[...] = jnp.zeros((count, head_size), f32)
            for first in range(0, count, step):
                last = first + step
                own = base_ref[pid, first:last, side : side + 1]
                allp = prefix_ref[head : head + 1, 0:last]
                score = dot_nt(query[first:last], key[0:last]) * scale + own - allp
                tail = jnp.where(apart, score[:, first:last], masked_score)
                score = tail if first == 0 else jnp.concatenate([score[:, :first], tail], axis=1)
                probs = jnp.exp(score)
                grad_probs = dot_nt(grad_mix[first:last], value[0:last])
                grad_score = (probs * (grad_probs - inner[first:last])).astype(bf16)
                query_out[first:last, :] = dot_nn(grad_score, key_one[0:last])
                key_sum[0:last, :] += dot_tn(grad_score, query_one[first:last])
                value_sum[0:last, :] += dot_tn(probs.astype(bf16), grad_mix[first:last])
            dq = query_out[...]
            dk = key_sum[...]
            sums.append(dq[:, head_size : head_size + 1] - dk[:, head_size : head_size + 1])
            outs += [dq[:, :head_size] * scale, dk[:, :head_size] * scale, value_sum[...], grad_gate]
        full = jnp.concatenate(outs, axis=1).astype(bf16)
        for part in range(8):
            core = jnp.bitwise_xor(where_ref[0], (part // 2) % 2)
            col = jnp.bitwise_xor(where_ref[1], part % 2)
            start = pl.multiple_of(((col * 2 + core) * 2 + part // 4) * size, size)
            proj_ref[pl.ds(start, size), :] = full[part * size : (part + 1) * size]
        both = jnp.where(lane_all == 0, sums[0], jnp.where(lane_all == 1, sums[1], 0.0))
        for part in range(8):
            here = slice(part * size, (part + 1) * size)
            places_ref[:, here] = both[here].T[0:8, :]

    return near(
        "attention_backward",
        body,
        [*chunks, *out_w, projected, mixed, prefix, base],
        [shape_of((count, 2 * per), bf16), shape_of((8, count), f32)],
        [
            pltpu.VMEM((count, 2 * per), bf16),
            pltpu.VMEM((count, 2 * head_size), f32),
            pltpu.VMEM((count, 128), f32),
            pltpu.VMEM((count, head_size), f32),
            pltpu.VMEM((count, 128), f32),
        ],
        where,
        limit=16,
    )


def grad_log(places, logits, where, each):
    count = logits.shape[1]
    size = count // 8

    def body(where_ref, *refs):
        parts, logit_ref, out_ref, rows = refs[:-3], refs[-3], refs[-2], refs[-1]
        rows[...] = jnp.zeros((8, count), f32)
        for k, ref in enumerate(parts):
            rows[2 * k : 2 * k + 2, :] = ref[0:2, :]
        rows[...] = scan_lanes(rows[...], True) * jax.nn.sigmoid(-logit_ref[...])
        for chunk in range(4):
            for side in range(2):
                start = pl.multiple_of(part_of(where_ref, chunk, side) * size, size)
                at = chunk * each + side * size
                out_ref[:, at : at + size] = rows[:, pl.ds(start, size)]

    return near(
        "grad_log",
        body,
        [*places, logits],
        shape_of((8, count), f32),
        [pltpu.VMEM((8, count), f32)],
        where,
    )


WIDE = 256


def spread(terms, name, extra=None):
    count = terms[0][0].shape[0]
    half = terms[0][1].shape[1] if terms[0][3] is None else terms[0][1].shape[0]
    each = count // 4
    ins = [array for term in terms for array in term[:3]] + list(extra or ())

    def body(*refs):
        out_refs = refs[-4:]
        for chunk in (2, 3, 0, 1):
            rows = slice(chunk * each, (chunk + 1) * each)
            for at in range(0, 2 * half, WIDE):
                side, here = at // half, slice(at % half, at % half + WIDE)
                total = 0.0
                for k, (left, _, _, kind) in enumerate(terms):
                    left_ref, weight_ref = refs[3 * k], refs[3 * k + 1 + side]
                    if kind is None:
                        total = total + dot_nn(left_ref[rows, :], weight_ref[:, here])
                    else:
                        inner = left.shape[1]
                        weight = weight_ref[here, kind * inner : (kind + 1) * inner]
                        total = total + dot_nt(left_ref[rows, :], weight)
                if extra is not None:
                    log_ref, forget_ref = refs[3 * len(terms)], refs[3 * len(terms) + 1]
                    total = total + dot_tn(log_ref[:, rows].astype(bf16), forget_ref[:, at : at + WIDE])
                out_refs[chunk][:, at : at + WIDE] = total.astype(bf16)

    return near(name, body, ins, [shape_of((each, 2 * half), bf16)] * 4, limit=12)


TILE = 256


def ffn_forward(chunks, gate_w, up_w):
    each, width = chunks[0].shape
    count, half = 4 * each, width // 2
    units = gate_w[0].shape[1]

    def body(x0, x1, x2, x3, gate0, gate1, up0, up1, gate_ref, up_ref, hidden_ref):
        for chunk, ref in enumerate((x0, x1, x2, x3)):
            here = slice(chunk * each, (chunk + 1) * each)
            for at in range(0, units, TILE):
                cols = slice(at, at + TILE)
                gate = dot_nn(ref[:, :half], gate0[:, cols]) + dot_nn(ref[:, half:], gate1[:, cols])
                up = dot_nn(ref[:, :half], up0[:, cols]) + dot_nn(ref[:, half:], up1[:, cols])
                gate_ref[here, cols] = gate.astype(bf16)
                up_ref[here, cols] = up.astype(bf16)
                hidden_ref[here, cols] = (gate * jax.nn.sigmoid(gate) * up).astype(bf16)

    return near(
        "ffn_forward", body, [*chunks, *gate_w, *up_w], [shape_of((count, units), bf16)] * 3
    )


def ffn_backward(chunks, down_w, gate_proj, up_proj):
    each, width = chunks[0].shape
    count, half = 4 * each, width // 2
    units = gate_proj.shape[1]

    def body(g0, g1, g2, g3, down0, down1, gate_ref, up_ref, grad_gate_ref, grad_up_ref):
        for chunk, ref in enumerate((g0, g1, g2, g3)):
            here = slice(chunk * each, (chunk + 1) * each)
            for at in range(0, units, TILE):
                cols = slice(at, at + TILE)
                grad = dot_nt(ref[:, :half], down0[cols, :]) + dot_nt(ref[:, half:], down1[cols, :])
                gate = gate_ref[here, cols].astype(f32)
                up = up_ref[here, cols].astype(f32)
                sig = jax.nn.sigmoid(gate)
                slope = sig * (1.0 + gate * (1.0 - sig))
                grad_gate_ref[here, cols] = (grad * up * slope).astype(bf16)
                grad_up_ref[here, cols] = (grad * gate * sig).astype(bf16)

    return near(
        "ffn_backward",
        body,
        [*chunks, *down_w, gate_proj, up_proj],
        [shape_of((count, units), bf16)] * 2,
    )


def grad_rows_weight(chunks, right, side, first, size, got=None):
    each, width = chunks[0].shape
    half = width // 2

    def body(x0, x1, x2, x3, right_ref, *refs):
        for at in range(0, half, TILE):
            total = 0.0 if got is None else refs[0][at : at + TILE, :].astype(f32)
            cols = slice(side * half + at, side * half + at + TILE)
            for chunk, ref in enumerate((x0, x1, x2, x3)):
                rows = slice(chunk * each, (chunk + 1) * each)
                total = total + dot_tn(ref[:, cols], right_ref[rows, first : first + size])
            refs[-1][at : at + TILE, :] = total.astype(bf16)

    return near(
        "grad_rows_weight",
        body,
        [*chunks, right] + ([] if got is None else [got]),
        shape_of((half, size), bf16),
    )


def grad_cols_weight(left, chunks, side, first, size, got=None):
    each, width = chunks[0].shape
    half = width // 2
    tile = TILE if size % TILE == 0 else 128

    def body(left_ref, x0, x1, x2, x3, *refs):
        for at in range(0, size, tile):
            total = 0.0 if got is None else refs[0][at : at + tile, :].astype(f32)
            for chunk, ref in enumerate((x0, x1, x2, x3)):
                rows = slice(chunk * each, (chunk + 1) * each)
                left_block = left_ref[rows, first + at : first + at + tile]
                total = total + dot_tn(left_block, ref[:, side * half : (side + 1) * half])
            refs[-1][at : at + tile, :] = total.astype(bf16)

    return near(
        "grad_cols_weight",
        body,
        [left, *chunks] + ([] if got is None else [got]),
        shape_of((size, half), bf16),
    )


def small_grads(grad_logits, chunks, gain_one, gain_two, scalars, heads, own_heads):
    each, width = chunks[0].shape
    tall = -(-(heads + 3) // 8) * 8

    def body(s, log_ref, x0, x1, x2, x3, one_ref, two_ref, out_ref):
        low = log_ref[...].astype(bf16)
        total = 0.0
        for chunk, ref in enumerate((x0, x1, x2, x3)):
            total = total + dot_nn(low[:, chunk * each : (chunk + 1) * each], ref[...])
        total = turn_block(total, s[0])
        place = 2 * s[2] + s[1]
        out_ref[...] = jnp.zeros((tall, width), f32)
        for k in range(heads // own_heads):

            @pl.when(place == k)
            def _():
                out_ref[k * own_heads : (k + 1) * own_heads, :] = total[0:own_heads, :]

        out_ref[heads : heads + 1, :] = turn_block(one_ref[...], s[0])
        out_ref[heads + 1 : heads + 2, :] = turn_block(two_ref[...], s[0])
        bias = jnp.sum(low.astype(f32), axis=1, keepdims=True)
        lane = lax.broadcasted_iota(jnp.int32, (8, 128), 1)
        head = lax.broadcasted_iota(jnp.int32, (8, 128), 0)
        good = (lane == place * own_heads + head) & (head < own_heads)
        out_ref[heads + 2 : heads + 3, 0:128] = jnp.sum(jnp.where(good, bias, 0.0), axis=0, keepdims=True)

    return near(
        "small_grads",
        body,
        [grad_logits, *chunks, gain_one, gain_two],
        shape_of((tall, width), f32),
        scalars=scalars,
    )


def line_rows(own, before, behind, place):
    rows, cols = own.shape

    def body(s, *refs):
        out_ref = refs[-1]
        for at in range(4):
            for k in range(-3, 4):

                @pl.when(at - s[0] == k)
                def _():
                    out_ref[at * rows : (at + 1) * rows, :] = refs[k + 3][...]

    return near(
        "line_rows",
        body,
        [*reversed(before), own, *behind],
        shape_of((4 * rows, cols), own.dtype),
        scalars=place.reshape(1).astype(jnp.int32),
    )


def halves(ref, index, axis):
    half = ref.shape[axis] // 2
    here = slice(index * half, (index + 1) * half)
    return ref[here, :] if axis == 0 else ref[:, here]


def settle(inner, outer, scalars, axis):
    shape = list(inner.shape)
    shape[axis] //= 2

    def body(s, inner_ref, outer_ref, out_ref):
        for core in range(2):

            @pl.when((s[1] == 1) & (s[0] == core))
            def _():
                out_ref[...] = halves(inner_ref, 1 - core, axis)

            @pl.when((s[1] != 1) & (s[0] == core))
            def _():
                out_ref[...] = halves(outer_ref, 1 - core, axis)

    return near("settle", body, [inner, outer], shape_of(tuple(shape), inner.dtype), scalars=scalars)


def put(target, shape, inner, outer, got, scalars, axis, piece, pieces):
    rows, cols = got.shape

    def body(s, *refs):
        inner_ref, outer_ref, got_ref = refs[-4:-1]
        out_ref = refs[-1]
        for core in range(2):

            @pl.when((pl.program_id(0) == 0) & (s[1] == 1) & (s[0] == core))
            def _():
                out_ref[...] = halves(inner_ref, core, axis).astype(f32)

            @pl.when((pl.program_id(0) == 0) & (s[1] != 1) & (s[0] == core))
            def _():
                out_ref[...] = halves(outer_ref, core, axis).astype(f32)

        @pl.when(pl.program_id(0) == 1)
        def _():
            out_ref[...] = got_ref[...].astype(f32)

    def out_map(i, s):
        place = jnp.bitwise_xor(s[0], i) * pieces + piece
        return (0, place) if axis == 0 else (place, 0)

    first = target is None
    ins = ([] if first else [target]) + [inner, outer, got]
    return pl.pallas_call(
        body,
        grid_spec=pltpu.PrefetchScalarGridSpec(
            num_scalar_prefetch=1,
            grid=(2,),
            in_specs=([] if first else [pl.BlockSpec(memory_space=pl.ANY)]) + [VMEM] * 3,
            out_specs=pl.BlockSpec((rows, cols), out_map),
        ),
        out_shape=shape_of(shape, f32),
        input_output_aliases={} if first else {1: 0},
        compiler_params=pltpu.CompilerParams(vmem_limit_bytes=12 << 20),
        name="put",
    )(scalars, *ins)


def chain_inward(values):
    return lax.ppermute(values, "dp", [(0, 1), (3, 2)])


def chain_middle(values):
    return lax.ppermute(values, "dp", [(1, 2), (2, 1)])


def chain_outward(values):
    return lax.ppermute(values, "dp", [(1, 0), (2, 3)])


ORDER = (
    "away down 0",
    "away down 1",
    "ffn_back",
    "away gate 0",
    "away up 1",
    "down_fwd",
    "own down 0",
    "sum_two",
    "away gate 1",
    "ffn_nffn",
    "own down 1",
    "sum_three",
    "one down 0",
    "final",
    "away up 0",
    "own gate 0",
    "one down 1",
    "norm_three",
    "two down 0",
    "own up 1",
    "one gate 0",
    "two down 1",
    "own gate 1",
    "three down 0",
    "att 1",
    "one up 1",
    "att 0",
    "away attn 0",
    "own up 0",
    "three down 1",
    "one gate 1",
    "two up 1",
    "four down 1",
    "away attn 1",
    "att 2",
    "one up 0",
    "own attn 0",
    "two gate 1",
    "log",
    "three up 1",
    "four down 0",
    "away attn 2",
    "four up 1",
    "own attn 1",
    "two up 0",
    "away out 0",
    "one attn 0",
    "three gate 1",
    "two gate 0",
    "nattn",
    "one attn 1",
    "own attn 2",
    "sum_four",
    "own out 0",
    "three up 0",
    "two attn 0",
    "four gate 1",
    "four up 0",
    "three gate 0",
    "two attn 1",
    "one attn 2",
    "four gate 0",
    "norm_four",
    "small",
    "three attn 0",
    "one out 0",
    "small 1",
    "four attn 0",
    "two attn 2",
    "small 2",
    "three attn 1",
    "small 3",
    "four attn 1",
    "back",
    "small 4",
    "two out 0",
    "tokens",
    "three attn 2",
    "small 5",
    "four attn 2",
    "three out 0",
    "four out 0",
)
PIECES = {"down": 2, "gate": 2, "up": 2, "out": 1, "attn": 3}


def shards(
    tokens,
    seq_lengths,
    seq_slots,
    w_attn,
    w_forget,
    b_forget,
    w_out,
    w_gate,
    w_up,
    w_down,
    gain_attn,
    gain_ffn,
    out_grad,
):
    count_seq = seq_slots.shape[0]
    piece_rows = tokens.shape[2]
    width = tokens.shape[3]
    groups = lax.axis_size("dp")
    row_index = lax.axis_index("row")
    pair, core = row_index // 2, row_index % 2
    col = lax.axis_index("col")
    group = lax.axis_index("dp")
    part_rows = out_grad.shape[2]
    own_heads = b_forget.shape[0] // 2
    all_heads = b_forget.shape[0] * lax.axis_size("col")
    head_size = w_out.shape[0] // (2 * own_heads)
    where = jnp.stack([core, col]).astype(jnp.int32)

    order = [None]

    def tie(values):
        return values if order[0] is None else after(values, order[0])

    def step(op, values, *others):
        out = op(tie(values), *others)
        order[0] = out[0] if isinstance(out, (list, tuple)) else out
        return out

    inverse = (
        jnp.zeros((count_seq,), jnp.int32).at[seq_slots].set(jnp.arange(count_seq, dtype=jnp.int32))
    )
    by_pair = inverse.reshape(groups, 2)
    my_length = seq_lengths[pick(by_pair[group], pair, 0)]
    scalars = jnp.stack([pair, core, col, my_length]).astype(jnp.int32)
    flat_tokens = tokens.reshape(count_seq, piece_rows, width)

    small = jnp.concatenate([w_forget.T, gain_attn[None], gain_ffn[None]], axis=0)
    small = joined(small, swap_core(small), core, 1)
    attn_got = swap_core(cut(w_attn, 1 - core, 1))
    sent = jnp.take(flat_tokens, pick(by_pair, 1 - pair, 1), axis=0)
    kept = jnp.take(flat_tokens, pick(by_pair, pair, 1), axis=0)
    tall = -(-small.shape[0] // 8) * 8
    payload = jnp.concatenate(
        [
            sent.reshape(groups * piece_rows, width),
            jnp.pad(small, ((0, tall - small.shape[0]), (0, width // 2))),
        ],
        axis=0,
    )
    payload_got = swap_pair(payload)
    arrived = payload_got[: groups * piece_rows].reshape(kept.shape)
    cots = out_grad.reshape(2, part_rows, width)
    order[0] = payload

    out_cut = step(cut, w_out, 1 - core, 0)
    gate_cut = step(cut, w_gate, 1 - core, 1)
    up_cut = step(cut, w_up, 1 - core, 1)
    down_cut = step(cut, w_down, 1 - core, 0)
    attn_own = step(lay, attn_got, w_attn, core, 1)
    outgoing = step(arrange_tokens, arrived, kept, pair)
    outgoing = outgoing.reshape(2 * groups, piece_rows, width)
    rows = lax.all_to_all(outgoing, "dp", split_axis=0, concat_axis=1, tiled=True)
    rows = rows.reshape(2 * part_rows, width)
    attn_own = after(attn_own, payload_got, outgoing)
    attn_w = [attn_own, swap_pair(attn_own)]
    order[0] = attn_own
    cots_got = swap_pair(tie(pick(cots, 1 - pair, 0)))
    out_own = step(lay, swap_core(out_cut), w_out, core, 0)
    gate_own = step(lay, swap_core(gate_cut), w_gate, core, 1)
    up_own = step(lay, swap_core(up_cut), w_up, core, 1)
    down_own = step(lay, swap_core(down_cut), w_down, core, 0)
    out_w = [out_own, swap_pair(out_own)]
    gate_w = [gate_own, swap_pair(gate_own)]
    up_w = [up_own, swap_pair(up_own)]
    down_w = [down_own, swap_pair(down_own)]

    small_got = payload_got[groups * piece_rows :][: small.shape[0], : width // 2]
    small = jnp.concatenate([small, small_got], axis=1)
    forget = pick(small[: 2 * own_heads].reshape(2, own_heads, width), core, 0)
    forget = jnp.pad(forget, ((0, 8 - own_heads), (0, 0)))
    gain_one = small[2 * own_heads : 2 * own_heads + 1].astype(f32)
    gain_two = small[2 * own_heads + 1 : 2 * own_heads + 2].astype(f32)
    bias = pick(b_forget.reshape(2, own_heads), core, 0).astype(f32)
    bias = jnp.broadcast_to(jnp.pad(bias, (0, 8 - own_heads))[:, None], (8, 128))

    normed_one = step(norm, rows, gain_one)
    wide_one = gather_quad(normed_one)
    first_tied = [tie(wide_one[0]), *wide_one[1:]]
    gated, *saved = attention_forward(
        first_tied, *attn_w, forget, bias, where, own_heads, head_size
    )
    order[0] = gated
    grad_final = step(arrange_cotangent, cots, cots_got, scalars)
    wide_grad = gather_quad(grad_final)
    part = step(lambda v: spread([(v, *out_w, None)], "out_forward"), gated)
    sent_one = step(add, part[2], swap_core(part[3]))
    middle, normed_two = step(sum_norm, after(rows, gate_w[1]), part[0], swap_core(part[1]), swap_col(sent_one), gain_two)
    wide_two = gather_quad(normed_two)
    gate_proj, up_proj, hidden = step(ffn_forward, wide_two, gate_w, up_w)

    inner = ((group == 1) | (group == 2)) if groups == 4 else (group >= 0)
    flags = jnp.stack([core, inner.astype(jnp.int32)]).astype(jnp.int32)
    shapes = {
        "down": w_down.shape,
        "gate": w_gate.shape,
        "up": w_up.shape,
        "out": w_out.shape,
        "attn": w_attn.shape,
    }
    grads = {name: None for name in shapes}
    put_so_far = {name: 0 for name in shapes}
    have = {}

    def operands(name, piece):
        pieces = PIECES[name]
        if name == "attn":
            return grad_rows_weight, wide_one, have["grad_projected"][piece], 0, w_attn.shape[1] // (2 * pieces)
        size = shapes[name][0 if name in ("down", "out") else 1] // (2 * pieces)
        if name == "down":
            return grad_cols_weight, hidden, wide_grad, piece * size, size
        if name == "out":
            return grad_cols_weight, gated, have["wide_mid"], piece * size, size
        return grad_rows_weight, wide_two, have["grad_" + name], piece * size, size

    def product(name, piece, side, got=None):
        kind, left, right, first, size = operands(name, piece)
        if kind is grad_rows_weight:
            return step(lambda v: kind(left, v, side, first, size, got), right)
        return step(lambda v: kind(v, right, side, first, size, got), left)

    def away(name, piece):
        have[name, piece] = swap_pair(product(name, piece, 1))

    def own(name, piece):
        mine = product(name, piece, 0, have[name, piece])
        have[name, piece] = (mine, chain_inward(mine) if groups == 4 else None)

    def one(name, piece):
        mine, got = have[name, piece]
        if groups == 4:
            mine = step(add, mine, got)
            got = chain_middle(mine)
        have[name, piece] = (mine, got)

    def two(name, piece):
        mine, got = have[name, piece]
        if groups == 4:
            mine = step(add, mine, got)
            got = chain_outward(mine)
        else:
            mine = got = lax.psum(mine, "dp")
        have[name, piece] = (mine, got)

    def three(name, piece):
        mine, got = have[name, piece]
        axis = 0 if operands(name, piece)[0] is grad_rows_weight else 1
        have[name, piece] = (mine, got, axis, swap_core(step(settle, mine, got, flags, axis)))

    def four(name, piece):
        mine, got, axis, beside = have[name, piece]
        grads[name] = step(
            lambda v: put(grads[name], shapes[name], mine, got, v, flags, axis, piece, PIECES[name]), beside
        )

    def ffn_back():
        have["grad_gate"], have["grad_up"] = step(ffn_backward, wide_grad, down_w, gate_proj, up_proj)

    def ffn_nffn():
        terms = [(have["grad_up"], *up_w, 0)]
        part = step(lambda v: spread([(v, *gate_w, 0), *terms], "ffn_nffn"), have["grad_gate"])
        have["part_three"] = [*part, swap_core(part[3]), swap_core(part[1])]

    def down_fwd():
        part = step(lambda v: spread([(v, *down_w, None)], "down_forward"), hidden)
        have["part_two"] = [*part, swap_core(part[3]), swap_core(part[1])]

    def sums(name):
        part = have["part_" + name]
        have["across_" + name] = swap_col(step(add, part[2], part[4]))

    def norm_three():
        part = have["part_three"]
        have["grad_middle"], grad_attn, have["gain_two"] = step(
            norm_backward, middle, part[0], part[5], have["across_three"], grad_final, gain_two
        )
        have["wide_mid"] = gather_quad(grad_attn)

    def final():
        part = have["part_two"]
        kept, away = step(final_rows, middle, part[0], part[5], have["across_two"], scalars)
        have["final"] = (kept, swap_pair(away))

    def att(piece):
        have.setdefault("grad_projected", {})
        have.setdefault("places", {})
        have["grad_projected"][piece], have["places"][piece] = step(
            attention_backward, have["wide_mid"], out_w, saved, where, piece, head_size
        )

    def log():
        places = [have["places"][k] for k in range(own_heads // 2)]
        have["grad_logits"] = step(lambda v: grad_log([v, *places[1:]], saved[2], where, 2 * part_rows), places[0])

    def nattn():
        grad = [have["grad_projected"][k] for k in range(own_heads // 2)]
        part = step(
            lambda v: spread(
                [(v, *attn_w, 0)] + [(grad[k], *attn_w, k) for k in range(1, len(grad))],
                "attn_nattn",
                (have["grad_logits"], forget),
            ),
            grad[0],
        )
        have["part_four"] = [*part, swap_core(part[3]), swap_core(part[1])]

    def norm_four():
        part = have["part_four"]
        grad_rows, have["gain_one"] = step(
            norm_backward, rows, part[0], part[5], have["across_four"], have["grad_middle"], gain_one, pair, groups
        )
        have["returned"] = lax.all_to_all(grad_rows, "dp", split_axis=0, concat_axis=0, tiled=True)

    def back():
        returned = tie(have["returned"])
        sent = pick(returned, 1 - pair, 1)
        have["back"] = (pick(returned, pair, 1), swap_pair(sent))
        order[0] = sent

    def tokens_last():
        stay, got = have["back"]
        stay = tie(stay)
        by_slot = jnp.stack([jnp.where(pair == 0, stay, got), jnp.where(pair == 0, got, stay)], 1)
        have["tokens"] = jnp.take(by_slot.reshape(count_seq, piece_rows, width), seq_slots, axis=0)
        order[0] = have["tokens"]

    def small_first():
        pack = step(
            small_grads, have["grad_logits"], wide_one, have["gain_one"], have["gain_two"], scalars, all_heads, own_heads
        )
        have["small"] = (pack, swap_core(pack))

    def small_next(stage):
        pack, got = have["small"]
        if stage >= 3 and groups != 4:
            have["small"] = (pack if stage > 3 else lax.psum(step(add, pack, got), "dp"), None)
            return
        pack = step(add, pack, got)
        swap = (swap_col, swap_pair, chain_inward, chain_middle, chain_outward)[stage - 1]
        if stage == 2 and groups != 4:
            swap = swap_pair
        have["small"] = (pack, swap(pack))

    named = {
        "ffn_back": ffn_back,
        "ffn_nffn": ffn_nffn,
        "down_fwd": down_fwd,
        "sum_two": lambda: sums("two"),
        "sum_three": lambda: sums("three"),
        "sum_four": lambda: sums("four"),
        "norm_three": norm_three,
        "norm_four": norm_four,
        "final": final,
        "log": log,
        "nattn": nattn,
        "back": back,
        "tokens": tokens_last,
        "small": small_first,
    }
    staged = {"away": away, "own": own, "one": one, "two": two, "three": three, "four": four}
    for entry in ORDER:
        words = entry.split()
        if len(words) == 1:
            named[entry]()
        elif words[0] == "att":
            att(int(words[1]))
        elif words[0] == "small":
            small_next(int(words[1]))
        else:
            staged[words[0]](words[1], int(words[2]))

    kept, got = have["final"]
    block_out = joined(tie(kept)[None], got[None], pair, 0)
    pack, got = have["small"]
    if groups == 4:
        pack = jnp.where(inner, tie(pack), got)
    block = gain_attn.shape[0]
    mine = lax.dynamic_slice_in_dim(pack, row_index * block, block, 1)
    forget_grad = lax.dynamic_slice_in_dim(mine, col * 2 * own_heads, 2 * own_heads, 0).T
    bias_grad = lax.dynamic_slice_in_dim(pack[all_heads + 2], col * 2 * own_heads, 2 * own_heads)
    return (
        block_out[:, None],
        have["tokens"][:, None],
        grads["attn"],
        forget_grad,
        bias_grad,
        grads["out"],
        grads["gate"],
        grads["up"],
        grads["down"],
        mine[all_heads],
        mine[all_heads + 1],
    )


def solution(mesh):
    return jax.shard_map(
        shards,
        mesh=mesh,
        in_specs=(
            P(None, ("row", "col"), "dp", None),
            P(),
            P(),
            P("row", "col"),
            P("row", "col"),
            P("col"),
            P("col", "row"),
            P("row", "col"),
            P("row", "col"),
            P("col", "row"),
            P("row"),
            P("row"),
            P("dp", ("row", "col"), None, None),
        ),
        out_specs=(
            P("dp", ("row", "col"), None, None),
            P(None, ("row", "col"), "dp", None),
            P("row", "col"),
            P("row", "col"),
            P("col"),
            P("col", "row"),
            P("row", "col"),
            P("row", "col"),
            P("col", "row"),
            P("row"),
            P("row"),
        ),
        check_vma=False,
    )
```

```python
import jax
import jax.numpy as jnp
from jax import lax
from jax.experimental import pallas as pl
from jax.experimental.pallas import tpu as pltpu
from jax.sharding import PartitionSpec as P

bf16 = jnp.bfloat16
f32 = jnp.float32
norm_epsilon = 1e-06
masked_score = -1e30
STEP = 256


def after(values, *others):
    return lax.optimization_barrier((values, *others))[0]


def swap_pair(values):
    count = lax.axis_size("row")
    return lax.ppermute(values, "row", [(r, r ^ 2) for r in range(count)])


def swap_core(values):
    count = lax.axis_size("row")
    return lax.ppermute(values, "row", [(r, r ^ 1) for r in range(count)])


def swap_col(values):
    count = lax.axis_size("col")
    return lax.ppermute(values, "col", [(r, r ^ 1) for r in range(count)])


def pick(values, index, axis):
    return lax.dynamic_index_in_dim(values, index, axis, keepdims=False)


def joined(own, other, index, axis):
    return jnp.where(
        index == 0, jnp.concatenate([own, other], axis), jnp.concatenate([other, own], axis)
    )


def turned(values, pair):
    half = values.shape[-1] // 2
    swapped = jnp.concatenate([values[..., half:], values[..., :half]], axis=-1)
    return jnp.where(pair == 0, values, swapped)


def gather_quad(values):
    across = swap_col(values)
    return [values, swap_core(values), across, swap_core(across)]


def dot_nt(left, right):
    return lax.dot_general(left, right, (((1,), (1,)), ((), ())), preferred_element_type=f32)


def dot_nn(left, right):
    return lax.dot_general(left, right, (((1,), (0,)), ((), ())), preferred_element_type=f32)


def dot_tn(left, right):
    return lax.dot_general(left, right, (((0,), (0,)), ((), ())), preferred_element_type=f32)


def shape_of(shape, dtype):
    return jax.ShapeDtypeStruct(shape, dtype)


VMEM = pl.BlockSpec(memory_space=pltpu.VMEM)
SMEM = pl.BlockSpec(memory_space=pltpu.SMEM)


def near(name, body, ins, out_shape, scratch=(), scalars=None, grid=(), limit=8, in_specs=None, out_specs=None, alias=None):
    specs = in_specs or [VMEM] * len(ins)
    if out_specs is None:
        out_specs = [VMEM] * len(out_shape) if isinstance(out_shape, list) else VMEM
    return pl.pallas_call(
        body,
        grid=grid,
        in_specs=specs if scalars is None else [SMEM, *specs],
        out_specs=out_specs,
        out_shape=out_shape,
        scratch_shapes=list(scratch),
        input_output_aliases=alias or {},
        compiler_params=pltpu.CompilerParams(vmem_limit_bytes=limit << 20),
        name=name,
    )(*(() if scalars is None else (scalars,)), *ins)


def slot_owner(slots_ref, slot, count):
    found = 0
    for k in range(count):
        found = found + jnp.where(slots_ref[k] == slot, k, 0)
    return found


def take_slots(tokens, slots, pair, extra=None):
    count, size, width = tokens.shape
    groups = count // 2
    more = 0 if extra is None else extra.shape[0]

    def body(slots_ref, pair_ref, tokens_ref, *refs):
        @pl.when(pl.program_id(0) < groups)
        def _():
            refs[-1][...] = tokens_ref[...]

        if more:

            @pl.when(pl.program_id(0) >= groups)
            def _():
                refs[-1][...] = refs[0][...]

    def source(g, slots_ref, pair_ref):
        slot = 2 * jnp.minimum(g, groups - 1) + pair_ref[0]
        return slot_owner(slots_ref, slot, count), 0, 0

    specs = [pl.BlockSpec((1, size, width), source)]
    if more:
        specs.append(pl.BlockSpec((1, size, width), lambda g, *_: (jnp.maximum(g - groups, 0), 0, 0)))
    return pl.pallas_call(
        body,
        grid_spec=pltpu.PrefetchScalarGridSpec(
            num_scalar_prefetch=2,
            grid=(groups + more,),
            in_specs=specs,
            out_specs=pl.BlockSpec((1, size, width), lambda g, *_: (g, 0, 0)),
        ),
        out_shape=shape_of((groups + more, size, width), tokens.dtype),
        compiler_params=pltpu.CompilerParams(vmem_limit_bytes=6 << 20),
        name="take_slots",
    )(slots, pair.reshape(1).astype(jnp.int32), tokens, *([extra] if more else []))


def add(left, right):
    def body(left_ref, right_ref, out_ref):
        out_ref[...] = (left_ref[...].astype(f32) + right_ref[...].astype(f32)).astype(out_ref.dtype)

    return near("add", body, [left, right], shape_of(left.shape, left.dtype))


def cut(shard, index, axis, pieces=2):
    shape = list(shard.shape)
    shape[axis] //= pieces

    def body(_, in_ref, out_ref):
        out_ref[...] = in_ref[...]

    return pl.pallas_call(
        body,
        grid_spec=pltpu.PrefetchScalarGridSpec(
            num_scalar_prefetch=1,
            grid=(1,),
            in_specs=[pl.BlockSpec(tuple(shape), lambda i, s: (s[0], 0) if axis == 0 else (0, s[0]))],
            out_specs=VMEM,
        ),
        out_shape=shape_of(tuple(shape), shard.dtype),
        compiler_params=pltpu.CompilerParams(vmem_limit_bytes=8 << 20),
        name="cut",
    )(index.reshape(1).astype(jnp.int32), shard)


def lay(got, shard, core, axis):
    rows, cols = got.shape
    out = (2 * rows, cols) if axis == 1 else (rows, 2 * cols)

    def body(s, got_ref, shard_ref, out_ref):
        for place in range(2):

            @pl.when(s[0] == place)
            def _():
                if axis == 1:
                    out_ref[place * rows : (place + 1) * rows, :] = shard_ref[...]
                    out_ref[(1 - place) * rows : (2 - place) * rows, :] = got_ref[...]
                else:
                    out_ref[:, place * cols : (place + 1) * cols] = shard_ref[...]
                    out_ref[:, (1 - place) * cols : (2 - place) * cols] = got_ref[...]

    return pl.pallas_call(
        body,
        grid_spec=pltpu.PrefetchScalarGridSpec(
            num_scalar_prefetch=1,
            grid=(1,),
            in_specs=[
                VMEM,
                pl.BlockSpec((rows, cols), lambda i, s: (0, s[0]) if axis == 1 else (s[0], 0)),
            ],
            out_specs=VMEM,
        ),
        out_shape=shape_of(out, shard.dtype),
        compiler_params=pltpu.CompilerParams(vmem_limit_bytes=8 << 20),
        name="lay",
    )(core.reshape(1).astype(jnp.int32), got, shard)


def inverse_scale(values):
    return lax.rsqrt(jnp.mean(values * values, axis=-1, keepdims=True) + norm_epsilon)


def turn_block(values, pair):
    half = values.shape[-1] // 2
    return jnp.where(
        pair == 0, values, jnp.concatenate([values[..., half:], values[..., :half]], axis=-1)
    )


SLAB = 64


def slabs(count):
    return [slice(at, at + SLAB) for at in range(0, count, SLAB)]


def norm(rows, gain):
    def body(rows_ref, gain_ref, out_ref):
        for here in slabs(rows.shape[0]):
            values = rows_ref[here, :].astype(f32)
            out_ref[here, :] = (values * inverse_scale(values) * gain_ref[...]).astype(bf16)

    return near("norm", body, [rows, gain], shape_of(rows.shape, bf16))


def sum_norm(rows, own, beside, across, gain):
    def body(rows_ref, own_ref, beside_ref, across_ref, gain_ref, middle_ref, out_ref):
        for here in slabs(rows.shape[0]):
            total = own_ref[here, :].astype(f32) + beside_ref[here, :].astype(f32)
            values = rows_ref[here, :].astype(f32) + (total + across_ref[here, :].astype(f32))
            middle_ref[here, :] = values
            out_ref[here, :] = (values * inverse_scale(values) * gain_ref[...]).astype(bf16)

    return near(
        "sum_norm",
        body,
        [rows, own, beside, across, gain],
        [shape_of(rows.shape, f32), shape_of(rows.shape, bf16)],
    )


def norm_backward(values, own, beside, across, base, gain, pair=None, groups=None):
    count, width = values.shape
    size = count // 2
    piece = size // (groups or 1)

    def body(s, values_ref, own_ref, beside_ref, across_ref, base_ref, gain_ref, *out_refs):
        term = jnp.zeros((1, width), f32)
        for here in slabs(count):
            grad = own_ref[here, :].astype(f32) + beside_ref[here, :].astype(f32) + across_ref[here, :].astype(f32)
            vals = values_ref[here, :].astype(f32)
            scale = inverse_scale(vals)
            weighted = grad * gain_ref[...]
            inner = jnp.mean(weighted * vals, axis=-1, keepdims=True)
            total = scale * weighted - vals * (scale * scale * scale) * inner
            total = base_ref[here, :].astype(f32) + total
            if groups is None:
                out_refs[0][here, :] = total
                out_refs[1][here, :] = total.astype(bf16)
            else:
                total = turn_block(total, s[0])
                step = min(piece, SLAB)
                for at in range(here.start, here.stop, step):
                    side, rest = at // size, at % size
                    group, first = rest // piece, rest % piece
                    rows = total[at - here.start : at - here.start + step]
                    out_refs[0][group, side, first : first + step, :] = rows.astype(bf16)
            term = term + jnp.sum(grad * vals * scale, axis=0, keepdims=True)
        out_refs[-1][...] = term

    if groups is None:
        shapes = [shape_of((count, width), f32), shape_of((count, width), bf16)]
    else:
        shapes = [shape_of((groups, 2, piece, width), bf16)]
    return near(
        "norm_backward",
        body,
        [values, own, beside, across, base, gain],
        [*shapes, shape_of((1, width), f32)],
        scalars=jnp.zeros((1,), jnp.int32) if pair is None else pair.reshape(1),
    )


def arrange_tokens(arrived, kept, pair):
    groups, size, width = kept.shape

    def body(s, arrived_ref, kept_ref, out_ref):
        for place in range(2):

            @pl.when(s[0] == place)
            def _():
                for group in range(groups):
                    out_ref[group, place] = turn_block(kept_ref[group], s[0])
                    out_ref[group, 1 - place] = turn_block(arrived_ref[group], s[0])

    return near(
        "arrange_tokens",
        body,
        [arrived, kept],
        shape_of((groups, 2, size, width), bf16),
        scalars=pair.reshape(1),
    )


def is_valid(s, half, size):
    first = (half * 4 + 2 * s[1] + s[2]) * size
    return first + lax.broadcasted_iota(jnp.int32, (size, 1), 0) < s[3]


def arrange_cotangent(cots, other, scalars):
    _, size, width = cots.shape

    def body(s, own_ref, other_ref, out_ref):
        for half in range(2):
            good = is_valid(s, half, size)

            @pl.when(half == s[0])
            def _():
                rows = turn_block(own_ref[half].astype(f32), s[0])
                out_ref[half * size : (half + 1) * size, :] = jnp.where(good, rows, 0.0).astype(bf16)

            @pl.when(half != s[0])
            def _():
                rows = turn_block(other_ref[0:size, :].astype(f32), s[0])
                out_ref[half * size : (half + 1) * size, :] = jnp.where(good, rows, 0.0).astype(bf16)

    return near(
        "arrange_cotangent",
        body,
        [cots, other],
        shape_of((2 * size, width), bf16),
        scalars=scalars,
    )


def final_rows(middle, own, beside, across, scalars):
    count, width = middle.shape
    size = count // 2

    def body(s, middle_ref, own_ref, beside_ref, across_ref, out_ref, away_ref):
        for half in range(2):
            good = is_valid(s, half, size)
            here = slice(half * size, (half + 1) * size)
            total = own_ref[here, :].astype(f32) + beside_ref[here, :].astype(f32)
            total = middle_ref[here, :] + (total + across_ref[here, :].astype(f32))
            rows = turn_block(jnp.where(good, total, 0.0), s[0]).astype(bf16)

            @pl.when(half == s[0])
            def _():
                out_ref[...] = rows

            @pl.when(half != s[0])
            def _():
                away_ref[...] = rows

    return near(
        "final_rows",
        body,
        [middle, own, beside, across],
        [shape_of((size, width), bf16)] * 2,
        scalars=scalars,
    )


def part_of(where_ref, chunk, half):
    core = jnp.bitwise_xor(where_ref[0], chunk % 2)
    col = jnp.bitwise_xor(where_ref[1], chunk // 2)
    return half * 4 + core * 2 + col


def scan_lanes(values, backwards):
    count = values.shape[1]
    lane = lax.broadcasted_iota(jnp.int32, values.shape, 1)
    step = 1
    while step < count:
        if backwards:
            moved = pltpu.roll(values, count - step, 1)
            values = values + jnp.where(lane < count - step, moved, 0.0)
        else:
            moved = pltpu.roll(values, step, 1)
            values = values + jnp.where(lane >= step, moved, 0.0)
        step *= 2
    return values


def log_sigmoid(values):
    return jnp.minimum(values, 0.0) - jnp.log1p(jnp.exp(-jnp.abs(values)))


def attention_forward(chunks, own_w, other_w, forget, bias, where, heads, head_size):
    each, width = chunks[0].shape
    count, half = 4 * each, width // 2
    size = count // 8
    pairs = heads // 2
    per = 4 * head_size
    step = min(STEP, count)

    def body(where_ref, x0, x1, x2, x3, own_ref, other_ref, forget_ref, bias_ref,
             gated_ref, proj_ref, mixed_ref, logit_ref, prefix_ref, base_ref, rows, cols):
        pid = pl.program_id(0)
        lanes = pl.multiple_of(pid * 2 * per, 2 * per)
        pair_lanes = pl.multiple_of(pid * 2 * head_size, 2 * head_size)
        xs = (x0, x1, x2, x3)

        @pl.when(pid == 0)
        def _():
            for chunk in range(4):
                logits = dot_nt(forget_ref[...], xs[chunk][...]) + bias_ref[:, 0:1]
                for side in range(2):
                    start = pl.multiple_of(part_of(where_ref, chunk, side) * size, size)
                    logit_ref[:, pl.ds(start, size)] = logits[:, side * size : (side + 1) * size]
            sums = scan_lanes(log_sigmoid(logit_ref[...]), False)
            prefix_ref[...] = sums
            for part in range(8):
                block = sums[:, part * size : (part + 1) * size]
                tall = jnp.concatenate([block, jnp.zeros((128 - 8, size), f32)], axis=0)
                cols[part * size : (part + 1) * size, :] = tall.T

        for chunk in range(4):
            made = dot_nn(xs[chunk][:, :half], own_ref[:, pl.ds(lanes, 2 * per)])
            made = (made + dot_nn(xs[chunk][:, half:], other_ref[:, pl.ds(lanes, 2 * per)])).astype(bf16)
            for side in range(2):
                start = pl.multiple_of(part_of(where_ref, chunk, side) * size, size)
                rows[pl.ds(start, size), :] = made[side * size : (side + 1) * size]
        proj_ref[:, pl.ds(lanes, 2 * per)] = rows[...]
        lane = lax.broadcasted_iota(jnp.int32, (step, 128), 1)
        apart = lax.broadcasted_iota(jnp.int32, (step, step), 1) <= lax.broadcasted_iota(
            jnp.int32, (step, step), 0
        )
        for first in range(0, count, step):
            last = first + step
            mixed_two, gated_two, base_two = [], [], []
            for side in range(2):
                at = side * per
                head = pid * 2 + side
                query = rows[first:last, at : at + head_size]
                key = rows[0:last, at + head_size : at + 2 * head_size]
                value = rows[0:last, at + 2 * head_size : at + 3 * head_size]
                gate = rows[first:last, at + 3 * head_size : at + 4 * head_size].astype(f32)
                own = jnp.sum(jnp.where(lane == head, cols[first:last, :], 0.0), axis=1, keepdims=True)
                allp = prefix_ref[pl.ds(head, 1), 0:last]
                score = dot_nt(query, key) * head_size ** (-0.5) + own - allp
                tail = jnp.where(apart, score[:, first:last], masked_score)
                score = tail if first == 0 else jnp.concatenate([score[:, :first], tail], axis=1)
                top = jnp.max(score, axis=1, keepdims=True)
                weight = jnp.exp(score - top)
                total = jnp.sum(weight, axis=1, keepdims=True)
                mixed = dot_nn(weight.astype(bf16), value) / total
                mixed_two.append(mixed)
                gated_two.append(mixed * jax.nn.sigmoid(gate))
                base_two.append(own - top - jnp.log(total))
            mixed_ref[first:last, pl.ds(pair_lanes, 2 * head_size)] = jnp.concatenate(mixed_two, axis=1)
            gated = jnp.concatenate(gated_two, axis=1).astype(bf16)
            base_ref[pid, first:last, :] = jnp.where(lane == 0, base_two[0], base_two[1])
            for part in range(first // size, last // size):
                core = jnp.bitwise_xor(where_ref[0], (part // 2) % 2)
                col = jnp.bitwise_xor(where_ref[1], part % 2)
                start = pl.multiple_of(((col * 2 + core) * 2 + part // 4) * size, size)
                off = part * size - first
                gated_ref[pl.ds(start, size), pl.ds(pair_lanes, 2 * head_size)] = gated[off : off + size]

    return near(
        "attention_forward",
        body,
        [*chunks, own_w, other_w, forget, bias],
        [
            shape_of((count, heads * head_size), bf16),
            shape_of((count, heads * per), bf16),
            shape_of((count, heads * head_size), f32),
            shape_of((8, count), f32),
            shape_of((8, count), f32),
            shape_of((pairs, count, 128), f32),
        ],
        [pltpu.VMEM((count, 2 * per), bf16), pltpu.VMEM((count, 128), f32)],
        where,
        grid=(pairs,),
        limit=12,
    )


def attention_backward(chunks, out_w, saved, where, pid, head_size):
    projected, mixed, logits, prefix, base = saved
    each, width = chunks[0].shape
    count, own_half = 4 * each, width // 2
    size = count // 8
    per = 4 * head_size
    step = min(STEP, count)
    scale = head_size ** (-0.5)

    def body(where_ref, m0, m1, m2, m3, out0_ref, out1_ref, saved_ref, mixes_ref, prefix_ref, base_ref,
             proj_ref, places_ref, rows, grads, key_sum, value_sum, query_out):
        for chunk, ref in enumerate((m0, m1, m2, m3)):
            here = slice(pid * 2 * head_size, (pid + 1) * 2 * head_size)
            made = dot_nt(ref[:, :own_half], out0_ref[here, :])
            made = made + dot_nt(ref[:, own_half:], out1_ref[here, :])
            for side in range(2):
                start = pl.multiple_of(part_of(where_ref, chunk, side) * size, size)
                grads[pl.ds(start, size), :] = made[side * size : (side + 1) * size]
        rows[...] = saved_ref[:, pid * 2 * per : (pid + 1) * 2 * per]
        lane_all = lax.broadcasted_iota(jnp.int32, (count, 128), 1)
        apart = lax.broadcasted_iota(jnp.int32, (step, step), 1) <= lax.broadcasted_iota(
            jnp.int32, (step, step), 0
        )
        sums = []
        outs = []
        one = jnp.ones((count, 1), bf16)
        pad = jnp.zeros((count, 128 - head_size - 1), bf16)
        for side in range(2):
            at = side * per
            head = pid * 2 + side
            query = rows[:, at : at + head_size]
            key = rows[:, at + head_size : at + 2 * head_size]
            value = rows[:, at + 2 * head_size : at + 3 * head_size]
            gate = jax.nn.sigmoid(rows[:, at + 3 * head_size : at + 4 * head_size].astype(f32))
            grad = grads[:, side * head_size : (side + 1) * head_size]
            mix = mixes_ref[:, (pid * 2 + side) * head_size : (pid * 2 + side + 1) * head_size]
            grad_mix = (grad * gate).astype(bf16)
            inner = jnp.sum(grad_mix.astype(f32) * mix, axis=1, keepdims=True)
            grad_gate = grad * mix * gate * (1.0 - gate)
            query_one = jnp.concatenate([query, one, pad], axis=1)
            key_one = jnp.concatenate([key, one, pad], axis=1)
            key_sum[...] = jnp.zeros((count, 128), f32)
            value_sum[...] = jnp.zeros((count, head_size), f32)
            for first in range(0, count, step):
                last = first + step
                own = base_ref[pid, first:last, side : side + 1]
                allp = prefix_ref[head : head + 1, 0:last]
                score = dot_nt(query[first:last], key[0:last]) * scale + own - allp
                tail = jnp.where(apart, score[:, first:last], masked_score)
                score = tail if first == 0 else jnp.concatenate([score[:, :first], tail], axis=1)
                probs = jnp.exp(score)
                grad_probs = dot_nt(grad_mix[first:last], value[0:last])
                grad_score = (probs * (grad_probs - inner[first:last])).astype(bf16)
                query_out[first:last, :] = dot_nn(grad_score, key_one[0:last])
                key_sum[0:last, :] += dot_tn(grad_score, query_one[first:last])
                value_sum[0:last, :] += dot_tn(probs.astype(bf16), grad_mix[first:last])
            dq = query_out[...]
            dk = key_sum[...]
            sums.append(dq[:, head_size : head_size + 1] - dk[:, head_size : head_size + 1])
            outs += [dq[:, :head_size] * scale, dk[:, :head_size] * scale, value_sum[...], grad_gate]
        full = jnp.concatenate(outs, axis=1).astype(bf16)
        for part in range(8):
            core = jnp.bitwise_xor(where_ref[0], (part // 2) % 2)
            col = jnp.bitwise_xor(where_ref[1], part % 2)
            start = pl.multiple_of(((col * 2 + core) * 2 + part // 4) * size, size)
            proj_ref[pl.ds(start, size), :] = full[part * size : (part + 1) * size]
        both = jnp.where(lane_all == 0, sums[0], jnp.where(lane_all == 1, sums[1], 0.0))
        for part in range(8):
            here = slice(part * size, (part + 1) * size)
            places_ref[:, here] = both[here].T[0:8, :]

    return near(
        "attention_backward",
        body,
        [*chunks, *out_w, projected, mixed, prefix, base],
        [shape_of((count, 2 * per), bf16), shape_of((8, count), f32)],
        [
            pltpu.VMEM((count, 2 * per), bf16),
            pltpu.VMEM((count, 2 * head_size), f32),
            pltpu.VMEM((count, 128), f32),
            pltpu.VMEM((count, head_size), f32),
            pltpu.VMEM((count, 128), f32),
        ],
        where,
        limit=16,
    )


def grad_log(places, logits, where, each):
    count = logits.shape[1]
    size = count // 8

    def body(where_ref, *refs):
        parts, logit_ref, out_ref, rows = refs[:-3], refs[-3], refs[-2], refs[-1]
        rows[...] = jnp.zeros((8, count), f32)
        for k, ref in enumerate(parts):
            rows[2 * k : 2 * k + 2, :] = ref[0:2, :]
        rows[...] = scan_lanes(rows[...], True) * jax.nn.sigmoid(-logit_ref[...])
        for chunk in range(4):
            for side in range(2):
                start = pl.multiple_of(part_of(where_ref, chunk, side) * size, size)
                at = chunk * each + side * size
                out_ref[:, at : at + size] = rows[:, pl.ds(start, size)]

    return near(
        "grad_log",
        body,
        [*places, logits],
        shape_of((8, count), f32),
        [pltpu.VMEM((8, count), f32)],
        where,
    )


WIDE = 256


def spread(terms, name, extra=None):
    count = terms[0][0].shape[0]
    half = terms[0][1].shape[1] if terms[0][3] is None else terms[0][1].shape[0]
    each = count // 4
    ins = [array for term in terms for array in term[:3]] + list(extra or ())

    def body(*refs):
        out_refs = refs[-4:]
        for chunk in (2, 3, 0, 1):
            rows = slice(chunk * each, (chunk + 1) * each)
            for at in range(0, 2 * half, WIDE):
                side, here = at // half, slice(at % half, at % half + WIDE)
                total = 0.0
                for k, (left, _, _, kind) in enumerate(terms):
                    left_ref, weight_ref = refs[3 * k], refs[3 * k + 1 + side]
                    if kind is None:
                        total = total + dot_nn(left_ref[rows, :], weight_ref[:, here])
                    else:
                        inner = left.shape[1]
                        weight = weight_ref[here, kind * inner : (kind + 1) * inner]
                        total = total + dot_nt(left_ref[rows, :], weight)
                if extra is not None:
                    log_ref, forget_ref = refs[3 * len(terms)], refs[3 * len(terms) + 1]
                    total = total + dot_tn(log_ref[:, rows].astype(bf16), forget_ref[:, at : at + WIDE])
                out_refs[chunk][:, at : at + WIDE] = total.astype(bf16)

    return near(name, body, ins, [shape_of((each, 2 * half), bf16)] * 4, limit=12)


TILE = 256


def ffn_forward(chunks, gate_w, up_w):
    each, width = chunks[0].shape
    count, half = 4 * each, width // 2
    units = gate_w[0].shape[1]

    def body(x0, x1, x2, x3, gate0, gate1, up0, up1, gate_ref, up_ref, hidden_ref):
        for chunk, ref in enumerate((x0, x1, x2, x3)):
            here = slice(chunk * each, (chunk + 1) * each)
            for at in range(0, units, TILE):
                cols = slice(at, at + TILE)
                gate = dot_nn(ref[:, :half], gate0[:, cols]) + dot_nn(ref[:, half:], gate1[:, cols])
                up = dot_nn(ref[:, :half], up0[:, cols]) + dot_nn(ref[:, half:], up1[:, cols])
                gate_ref[here, cols] = gate.astype(bf16)
                up_ref[here, cols] = up.astype(bf16)
                hidden_ref[here, cols] = (gate * jax.nn.sigmoid(gate) * up).astype(bf16)

    return near(
        "ffn_forward", body, [*chunks, *gate_w, *up_w], [shape_of((count, units), bf16)] * 3
    )


def ffn_backward(chunks, down_w, gate_proj, up_proj):
    each, width = chunks[0].shape
    count, half = 4 * each, width // 2
    units = gate_proj.shape[1]

    def body(g0, g1, g2, g3, down0, down1, gate_ref, up_ref, grad_gate_ref, grad_up_ref):
        for chunk, ref in enumerate((g0, g1, g2, g3)):
            here = slice(chunk * each, (chunk + 1) * each)
            for at in range(0, units, TILE):
                cols = slice(at, at + TILE)
                grad = dot_nt(ref[:, :half], down0[cols, :]) + dot_nt(ref[:, half:], down1[cols, :])
                gate = gate_ref[here, cols].astype(f32)
                up = up_ref[here, cols].astype(f32)
                sig = jax.nn.sigmoid(gate)
                slope = sig * (1.0 + gate * (1.0 - sig))
                grad_gate_ref[here, cols] = (grad * up * slope).astype(bf16)
                grad_up_ref[here, cols] = (grad * gate * sig).astype(bf16)

    return near(
        "ffn_backward",
        body,
        [*chunks, *down_w, gate_proj, up_proj],
        [shape_of((count, units), bf16)] * 2,
    )


def grad_rows_weight(chunks, right, side, first, size, got=None):
    each, width = chunks[0].shape
    half = width // 2

    def body(x0, x1, x2, x3, right_ref, *refs):
        for at in range(0, half, TILE):
            total = 0.0 if got is None else refs[0][at : at + TILE, :].astype(f32)
            cols = slice(side * half + at, side * half + at + TILE)
            for chunk, ref in enumerate((x0, x1, x2, x3)):
                rows = slice(chunk * each, (chunk + 1) * each)
                total = total + dot_tn(ref[:, cols], right_ref[rows, first : first + size])
            refs[-1][at : at + TILE, :] = total.astype(bf16)

    return near(
        "grad_rows_weight",
        body,
        [*chunks, right] + ([] if got is None else [got]),
        shape_of((half, size), bf16),
    )


def grad_cols_weight(left, chunks, side, first, size, got=None):
    each, width = chunks[0].shape
    half = width // 2
    tile = TILE if size % TILE == 0 else 128

    def body(left_ref, x0, x1, x2, x3, *refs):
        for at in range(0, size, tile):
            total = 0.0 if got is None else refs[0][at : at + tile, :].astype(f32)
            for chunk, ref in enumerate((x0, x1, x2, x3)):
                rows = slice(chunk * each, (chunk + 1) * each)
                left_block = left_ref[rows, first + at : first + at + tile]
                total = total + dot_tn(left_block, ref[:, side * half : (side + 1) * half])
            refs[-1][at : at + tile, :] = total.astype(bf16)

    return near(
        "grad_cols_weight",
        body,
        [left, *chunks] + ([] if got is None else [got]),
        shape_of((size, half), bf16),
    )


def small_grads(grad_logits, chunks, gain_one, gain_two, scalars, heads, own_heads):
    each, width = chunks[0].shape
    tall = -(-(heads + 3) // 8) * 8

    def body(s, log_ref, x0, x1, x2, x3, one_ref, two_ref, out_ref):
        low = log_ref[...].astype(bf16)
        total = 0.0
        for chunk, ref in enumerate((x0, x1, x2, x3)):
            total = total + dot_nn(low[:, chunk * each : (chunk + 1) * each], ref[...])
        total = turn_block(total, s[0])
        place = 2 * s[2] + s[1]
        out_ref[...] = jnp.zeros((tall, width), f32)
        for k in range(heads // own_heads):

            @pl.when(place == k)
            def _():
                out_ref[k * own_heads : (k + 1) * own_heads, :] = total[0:own_heads, :]

        out_ref[heads : heads + 1, :] = turn_block(one_ref[...], s[0])
        out_ref[heads + 1 : heads + 2, :] = turn_block(two_ref[...], s[0])
        bias = jnp.sum(low.astype(f32), axis=1, keepdims=True)
        lane = lax.broadcasted_iota(jnp.int32, (8, 128), 1)
        head = lax.broadcasted_iota(jnp.int32, (8, 128), 0)
        good = (lane == place * own_heads + head) & (head < own_heads)
        out_ref[heads + 2 : heads + 3, 0:128] = jnp.sum(jnp.where(good, bias, 0.0), axis=0, keepdims=True)

    return near(
        "small_grads",
        body,
        [grad_logits, *chunks, gain_one, gain_two],
        shape_of((tall, width), f32),
        scalars=scalars,
    )


def line_rows(own, before, behind, place):
    rows, cols = own.shape

    def body(s, *refs):
        out_ref = refs[-1]
        for at in range(4):
            for k in range(-3, 4):

                @pl.when(at - s[0] == k)
                def _():
                    out_ref[at * rows : (at + 1) * rows, :] = refs[k + 3][...]

    return near(
        "line_rows",
        body,
        [*reversed(before), own, *behind],
        shape_of((4 * rows, cols), own.dtype),
        scalars=place.reshape(1).astype(jnp.int32),
    )


def halves(ref, index, axis):
    half = ref.shape[axis] // 2
    here = slice(index * half, (index + 1) * half)
    return ref[here, :] if axis == 0 else ref[:, here]


def settle(inner, outer, scalars, axis):
    shape = list(inner.shape)
    shape[axis] //= 2

    def body(s, inner_ref, outer_ref, out_ref):
        for core in range(2):

            @pl.when((s[1] == 1) & (s[0] == core))
            def _():
                out_ref[...] = halves(inner_ref, 1 - core, axis)

            @pl.when((s[1] != 1) & (s[0] == core))
            def _():
                out_ref[...] = halves(outer_ref, 1 - core, axis)

    return near("settle", body, [inner, outer], shape_of(tuple(shape), inner.dtype), scalars=scalars)


def put(target, shape, inner, outer, got, scalars, axis, piece, pieces):
    rows, cols = got.shape

    def body(s, *refs):
        inner_ref, outer_ref, got_ref = refs[-4:-1]
        out_ref = refs[-1]
        for core in range(2):

            @pl.when((pl.program_id(0) == 0) & (s[1] == 1) & (s[0] == core))
            def _():
                out_ref[...] = halves(inner_ref, core, axis).astype(f32)

            @pl.when((pl.program_id(0) == 0) & (s[1] != 1) & (s[0] == core))
            def _():
                out_ref[...] = halves(outer_ref, core, axis).astype(f32)

        @pl.when(pl.program_id(0) == 1)
        def _():
            out_ref[...] = got_ref[...].astype(f32)

    def out_map(i, s):
        place = jnp.bitwise_xor(s[0], i) * pieces + piece
        return (0, place) if axis == 0 else (place, 0)

    first = target is None
    ins = ([] if first else [target]) + [inner, outer, got]
    return pl.pallas_call(
        body,
        grid_spec=pltpu.PrefetchScalarGridSpec(
            num_scalar_prefetch=1,
            grid=(2,),
            in_specs=([] if first else [pl.BlockSpec(memory_space=pl.ANY)]) + [VMEM] * 3,
            out_specs=pl.BlockSpec((rows, cols), out_map),
        ),
        out_shape=shape_of(shape, f32),
        input_output_aliases={} if first else {1: 0},
        compiler_params=pltpu.CompilerParams(vmem_limit_bytes=12 << 20),
        name="put",
    )(scalars, *ins)


def line_gather(values):
    before, behind = [values], [values]
    for _ in range(3):
        before.append(lax.ppermute(before[-1], "dp", [(0, 1), (1, 2), (2, 3)]))
        behind.append(lax.ppermute(behind[-1], "dp", [(1, 0), (2, 1), (3, 2)]))
    return before[1:], behind[1:]


def chain_inward(values):
    return lax.ppermute(values, "dp", [(0, 1), (3, 2)])


def chain_middle(values):
    return lax.ppermute(values, "dp", [(1, 2), (2, 1)])


def chain_outward(values):
    return lax.ppermute(values, "dp", [(1, 0), (2, 3)])


AWAY, OWN, ONE, TWO, THREE, FOUR, ATT, SMALL_NEXT, SMALL, FFN_BACK, FFN_NFFN, DOWN_FWD = range(12)
SUM_TWO, SUM_THREE, SUM_FOUR, NORM_THREE, NORM_FOUR, FINAL, LOG, NATTN, BACK, TOKENS, REDUCE, BLOCK, PACK = range(12, 25)
DOWN, GATE, UP, OUT, ATTN = range(5)
ORDER = (
    (AWAY, DOWN, 0), (AWAY, DOWN, 1), (FFN_BACK,), (FFN_NFFN,),
    (AWAY, GATE, 0), (OWN, DOWN, 0), (SUM_THREE,), (AWAY, GATE, 1),
    (AWAY, UP, 0), (DOWN_FWD,), (OWN, DOWN, 1), (ONE, DOWN, 0),
    (NORM_THREE,), (SUM_TWO,), (OWN, GATE, 0), (ONE, DOWN, 1),
    (TWO, DOWN, 0), (OWN, GATE, 1), (ONE, GATE, 0), (TWO, DOWN, 1),
    (ATT, 0), (ATT, 1), (ONE, GATE, 1), (ATT, 2),
    (TWO, GATE, 0), (OWN, UP, 0), (LOG,), (NATTN,),
    (AWAY, OUT, 0), (TWO, GATE, 1), (SUM_FOUR,), (AWAY, ATTN, 0),
    (AWAY, ATTN, 1), (AWAY, ATTN, 2), (FINAL,), (THREE, DOWN, 0),
    (ONE, UP, 0), (OWN, ATTN, 0), (NORM_FOUR,), (SMALL,),
    (FOUR, DOWN, 0), (THREE, DOWN, 1), (SMALL_NEXT, 1), (OWN, ATTN, 1),
    (SMALL_NEXT, 2), (BACK,), (FOUR, DOWN, 1), (ONE, ATTN, 0),
    (THREE, GATE, 0), (THREE, GATE, 1), (TWO, UP, 0), (OWN, ATTN, 2),
    (FOUR, GATE, 0), (FOUR, GATE, 1), (OWN, OUT, 0), (ONE, ATTN, 1),
    (TWO, ATTN, 0), (SMALL_NEXT, 3), (ONE, ATTN, 2), (TOKENS,),
    (THREE, UP, 0), (ONE, OUT, 0), (TWO, ATTN, 1), (SMALL_NEXT, 4),
    (FOUR, UP, 0), (THREE, ATTN, 0), (TWO, ATTN, 2), (FOUR, ATTN, 0),
    (THREE, ATTN, 1), (TWO, OUT, 0), (SMALL_NEXT, 5), (FOUR, ATTN, 1),
    (THREE, ATTN, 2), (FOUR, ATTN, 2), (THREE, OUT, 0), (FOUR, OUT, 0),
    (BLOCK,), (PACK,),
)
PIECES = (2, 2, 1, 1, 3)
REDUCED = ()


class Store:
    pass


def shards(
    tokens,
    seq_lengths,
    seq_slots,
    w_attn,
    w_forget,
    b_forget,
    w_out,
    w_gate,
    w_up,
    w_down,
    gain_attn,
    gain_ffn,
    out_grad,
):
    count_seq = seq_slots.shape[0]
    piece_rows = tokens.shape[2]
    width = tokens.shape[3]
    groups = lax.axis_size("dp")
    row_index = lax.axis_index("row")
    pair, core = row_index // 2, row_index % 2
    col = lax.axis_index("col")
    group = lax.axis_index("dp")
    part_rows = out_grad.shape[2]
    own_heads = b_forget.shape[0] // 2
    all_heads = b_forget.shape[0] * lax.axis_size("col")
    head_size = w_out.shape[0] // (2 * own_heads)
    where = jnp.stack([core, col]).astype(jnp.int32)

    order = [None]

    def tie(values):
        return values if order[0] is None else after(values, order[0])

    def step(op, values, *others):
        out = op(tie(values), *others)
        order[0] = out[0] if isinstance(out, (list, tuple)) else out
        return out

    my_slot = 2 * group + pair
    my_length = jnp.sum(jnp.where(seq_slots == my_slot, seq_lengths, 0))
    scalars = jnp.stack([pair, core, col, my_length]).astype(jnp.int32)
    flat_tokens = tokens.reshape(count_seq, piece_rows, width)

    small = jnp.concatenate([w_forget.T, gain_attn[None], gain_ffn[None]], axis=0)
    small = joined(small, swap_core(small), core, 1)
    attn_cut = cut(w_attn, 1 - core, 1)
    order[0] = attn_cut
    gate_cut = step(cut, w_gate, 1 - core, 1)
    attn_got, gate_got = swap_core(attn_cut), swap_core(gate_cut)
    blocks = -(-small.shape[0] // piece_rows)
    extra = jnp.pad(small, ((0, blocks * piece_rows - small.shape[0]), (0, width // 2)))
    payload = take_slots(flat_tokens, seq_slots, 1 - pair, extra.reshape(blocks, piece_rows, width))
    payload_got = swap_pair(payload)
    arrived = payload_got
    order[0] = payload
    kept = step(lambda v: take_slots(v, seq_slots, pair), flat_tokens)

    cots = out_grad.reshape(2, part_rows, width)
    cots_sent = tie(pick(cots, 1 - pair, 0))
    cots_got = swap_pair(cots_sent)
    order[0] = cots_sent
    gate_own = step(lay, gate_got, w_gate, core, 1)
    if groups == 4:
        gate_quarter = step(cut, gate_own, group, 0, 4)
        gate_quarter = swap_pair(gate_quarter)
        before, behind = line_gather(gate_quarter)
        lines = [[before[k], behind[k]] for k in range(3)]
    else:
        lines = [[], [], []]
    out_cut = step(cut, w_out, 1 - core, 0)
    up_cut = step(cut, w_up, 1 - core, 1)
    down_cut = step(cut, w_down, 1 - core, 0)
    attn_own = step(lay, attn_got, w_attn, core, 1)
    outgoing = step(arrange_tokens, arrived, kept, pair)
    outgoing = outgoing.reshape(2 * groups, piece_rows, width)
    rows = lax.all_to_all(outgoing, "dp", split_axis=0, concat_axis=1, tiled=True)
    rows = rows.reshape(2 * part_rows, width)
    attn_own = after(attn_own, outgoing, *([gate_quarter] if groups == 4 else []))
    attn_w = [attn_own, swap_pair(attn_own)]
    order[0] = attn_own
    out_own = step(lay, swap_core(out_cut), w_out, core, 0)
    up_own = step(lay, swap_core(up_cut), w_up, core, 1)
    down_own = step(lay, swap_core(down_cut), w_down, core, 0)
    out_w = [out_own, swap_pair(out_own)]
    up_w = [up_own, swap_pair(up_own)]
    down_w = [down_own, swap_pair(down_own)]

    small_got = payload_got[groups:].reshape(-1, width)[: small.shape[0], : width // 2]
    small = jnp.concatenate([small, small_got], axis=1)
    forget = pick(small[: 2 * own_heads].reshape(2, own_heads, width), core, 0)
    forget = jnp.pad(forget, ((0, 8 - own_heads), (0, 0)))
    gain_one = small[2 * own_heads : 2 * own_heads + 1].astype(f32)
    gain_two = small[2 * own_heads + 1 : 2 * own_heads + 2].astype(f32)
    bias = pick(b_forget.reshape(2, own_heads), core, 0).astype(f32)
    bias = jnp.broadcast_to(jnp.pad(bias, (0, 8 - own_heads))[:, None], (8, 128))

    grad_final = step(arrange_cotangent, cots, cots_got, scalars)
    wide_grad = gather_quad(grad_final)
    normed_one = step(norm, after(rows, wide_grad[1]), gain_one)
    across = swap_col(normed_one)
    wide_one = [normed_one, swap_core(normed_one), across, swap_core(after(across, *lines[0]))]
    gated, *saved = attention_forward(
        [after(normed_one, order[0], wide_grad[2], *lines[1]), *wide_one[1:]],
        *attn_w, forget, bias, where, own_heads, head_size
    )
    order[0] = gated
    part = step(lambda v: spread([(v, *out_w, None)], "out_forward"), after(gated, *lines[2]))
    sent_one = step(add, part[2], swap_core(part[3]))
    across = swap_col(sent_one)
    if groups == 4:
        gate_w = [gate_own, step(line_rows, gate_quarter, before, behind, group)]
    else:
        gate_w = [gate_own, swap_pair(gate_own)]
    middle, normed_two = step(sum_norm, after(rows, up_w[1]), part[0], swap_core(part[1]), across, gain_two)
    across = swap_col(normed_two)
    wide_two = [normed_two, swap_core(normed_two), across, swap_core(across)]
    gate_proj, up_proj, hidden = step(ffn_forward, wide_two, gate_w, up_w)

    parts = own_heads // 2
    inner = ((group == 1) | (group == 2)) if groups == 4 else (group >= 0)
    flags = jnp.stack([core, inner.astype(jnp.int32)]).astype(jnp.int32)
    shapes = (w_down.shape, w_gate.shape, w_up.shape, w_out.shape, w_attn.shape)
    grads = [None] * 5
    have = Store()
    have.units, have.projected, have.places = {}, {}, {}

    def operands(name, piece):
        pieces = PIECES[name]
        if name == ATTN:
            return grad_rows_weight, wide_one, have.projected[piece], 0, w_attn.shape[1] // (2 * pieces)
        size = shapes[name][0 if name in (DOWN, OUT) else 1] // (2 * pieces)
        if name == DOWN:
            return grad_cols_weight, hidden, wide_grad, piece * size, size
        if name == OUT:
            return grad_cols_weight, gated, have.wide_mid, 0, size
        return grad_rows_weight, wide_two, have.grad_gate if name == GATE else have.grad_up, piece * size, size

    def product(name, piece, side, got=None):
        kind, left, right, first, size = operands(name, piece)
        if kind is grad_rows_weight:
            return step(lambda v: kind(left, v, side, first, size, got), right)
        if isinstance(left, list):
            return step(lambda v: kind([v, *left[1:]], right, side, first, size, got), left[0])
        return step(lambda v: kind(v, right, side, first, size, got), left)

    def away(name, piece):
        have.units[name, piece] = swap_pair(product(name, piece, 1))

    def own(name, piece):
        mine = product(name, piece, 0, have.units[name, piece])
        chained = groups == 4 and name not in REDUCED
        have.units[name, piece] = (mine, chain_inward(mine) if chained else None)

    def reduce(*names):
        keys = [key for key in have.units if key[0] in names]
        sums = lax.psum([have.units[key][0] for key in keys], "dp")
        for key, total in zip(keys, sums):
            have.units[key] = (total, total)

    def one(name, piece):
        mine, got = have.units[name, piece]
        if groups == 4:
            mine = step(add, mine, got)
            got = chain_middle(mine)
        have.units[name, piece] = (mine, got)

    def two(name, piece):
        mine, got = have.units[name, piece]
        if groups == 4:
            mine = step(add, mine, got)
            got = chain_outward(mine)
        else:
            mine = got = lax.psum(mine, "dp")
        have.units[name, piece] = (mine, got)

    def three(name, piece):
        mine, got = have.units[name, piece]
        axis = 0 if operands(name, piece)[0] is grad_rows_weight else 1
        have.units[name, piece] = (mine, got, axis, swap_core(step(settle, mine, got, flags, axis)))

    def four(name, piece):
        mine, got, axis, beside = have.units[name, piece]
        grads[name] = step(
            lambda v: put(grads[name], shapes[name], mine, got, v, flags, axis, piece, PIECES[name]), beside
        )

    def ffn_back():
        have.grad_gate, have.grad_up = step(ffn_backward, wide_grad, down_w, gate_proj, up_proj)

    def ffn_nffn():
        terms = [(have.grad_up, *up_w, 0)]
        part = step(lambda v: spread([(v, *gate_w, 0), *terms], "ffn_nffn"), have.grad_gate)
        have.part_three = [*part, swap_core(part[3]), swap_core(part[1])]

    def down_fwd():
        part = step(lambda v: spread([(v, *down_w, None)], "down_forward"), hidden)
        have.part_two = [*part, swap_core(part[3]), swap_core(part[1])]

    def sums(part):
        return swap_col(step(add, part[2], part[4]))

    def sum_two():
        have.across_two = sums(have.part_two)

    def sum_three():
        have.across_three = sums(have.part_three)

    def sum_four():
        have.across_four = sums(have.part_four)

    def norm_three():
        part = have.part_three
        have.grad_middle, grad_attn, have.gain_two = step(
            norm_backward, middle, part[0], part[5], have.across_three, grad_final, gain_two
        )
        have.wide_mid = gather_quad(grad_attn)

    def final():
        part = have.part_two
        kept, away = step(final_rows, middle, part[0], part[5], have.across_two, scalars)
        have.final = (kept, swap_pair(away))

    def att(piece):
        have.projected[piece], have.places[piece] = step(
            lambda v: attention_backward([v, *have.wide_mid[1:]], out_w, saved, where, piece, head_size),
            have.wide_mid[0],
        )

    def log():
        places = [have.places[k] for k in range(parts)]
        have.grad_logits = step(lambda v: grad_log([v, *places[1:]], saved[2], where, 2 * part_rows), places[0])

    def nattn():
        grad = have.projected
        part = step(
            lambda v: spread(
                [(grad[k] if k else v, *attn_w, k) for k in range(parts)],
                "attn_nattn",
                (have.grad_logits, forget),
            ),
            grad[0],
        )
        have.part_four = [*part, swap_core(part[3]), swap_core(part[1])]

    def norm_four():
        part = have.part_four
        grad_rows, have.gain_one = step(
            norm_backward, rows, part[0], part[5], have.across_four, have.grad_middle, gain_one, pair, groups
        )
        have.returned = lax.all_to_all(grad_rows, "dp", split_axis=0, concat_axis=0, tiled=True)

    def back():
        returned = tie(have.returned)
        sent = pick(returned, 1 - pair, 1)
        have.back = (pick(returned, pair, 1), swap_pair(sent))
        order[0] = sent

    def tokens_last():
        stay, got = have.back
        stay = tie(stay)
        by_slot = jnp.stack([jnp.where(pair == 0, stay, got), jnp.where(pair == 0, got, stay)], 1)
        have.tokens = jnp.take(by_slot.reshape(count_seq, piece_rows, width), seq_slots, axis=0, mode="clip")
        order[0] = have.tokens

    def small_first():
        pack = step(
            small_grads, have.grad_logits, wide_one, have.gain_one, have.gain_two, scalars, all_heads, own_heads
        )
        have.small = (pack, swap_core(pack))

    def small_next(stage):
        pack, got = have.small
        if stage >= 3 and groups != 4:
            have.small = (pack if stage > 3 else lax.psum(step(add, pack, got), "dp"), None)
            return
        pack = step(add, pack, got)
        swap = (swap_col, swap_pair, chain_inward, chain_middle, chain_outward)[stage - 1]
        if stage == 2 and groups != 4:
            swap = swap_pair
        have.small = (pack, swap(pack))

    def block():
        kept, got = have.final
        have.block_out = joined(tie(kept)[None], got[None], pair, 0)
        order[0] = have.block_out

    def pack_last():
        have.pack, got = have.small
        if groups == 4:
            have.pack = jnp.where(inner, tie(have.pack), got)
            order[0] = have.pack

    single = {
        BLOCK: block,
        PACK: pack_last,
        FFN_BACK: ffn_back,
        FFN_NFFN: ffn_nffn,
        DOWN_FWD: down_fwd,
        SUM_TWO: sum_two,
        SUM_THREE: sum_three,
        SUM_FOUR: sum_four,
        NORM_THREE: norm_three,
        NORM_FOUR: norm_four,
        FINAL: final,
        LOG: log,
        NATTN: nattn,
        BACK: back,
        TOKENS: tokens_last,
        SMALL: small_first,
        ATT: att,
        REDUCE: reduce,
        SMALL_NEXT: small_next,
        AWAY: away,
        OWN: own,
        ONE: one,
        TWO: two,
        THREE: three,
        FOUR: four,
    }
    for entry in ORDER:
        single[entry[0]](*entry[1:])

    block_out, pack = have.block_out, have.pack
    block_width = gain_attn.shape[0]
    mine = lax.dynamic_slice_in_dim(pack, row_index * block_width, block_width, 1)
    forget_grad = lax.dynamic_slice_in_dim(mine, col * 2 * own_heads, 2 * own_heads, 0).T
    bias_grad = lax.dynamic_slice_in_dim(pack[all_heads + 2], col * 2 * own_heads, 2 * own_heads)
    return (
        block_out[:, None],
        have.tokens[:, None],
        grads[ATTN],
        forget_grad,
        bias_grad,
        grads[OUT],
        grads[GATE],
        grads[UP],
        grads[DOWN],
        mine[all_heads],
        mine[all_heads + 1],
    )


def solution(mesh):
    return jax.shard_map(
        shards,
        mesh=mesh,
        in_specs=(
            P(None, ("row", "col"), "dp", None),
            P(),
            P(),
            P("row", "col"),
            P("row", "col"),
            P("col"),
            P("col", "row"),
            P("row", "col"),
            P("row", "col"),
            P("col", "row"),
            P("row"),
            P("row"),
            P("dp", ("row", "col"), None, None),
        ),
        out_specs=(
            P("dp", ("row", "col"), None, None),
            P(None, ("row", "col"), "dp", None),
            P("row", "col"),
            P("row", "col"),
            P("col"),
            P("col", "row"),
            P("row", "col"),
            P("row", "col"),
            P("col", "row"),
            P("row"),
            P("row"),
        ),
        check_vma=False,
    )
```

```python
import jax
import jax.numpy as jnp
from jax import lax
from jax.experimental import pallas as pl
from jax.experimental.pallas import tpu as pltpu
from jax.sharding import PartitionSpec as P

bf16 = jnp.bfloat16
f32 = jnp.float32
norm_epsilon = 1e-06
masked_score = -1e30
STEP = 256


def after(values, *others):
    return lax.optimization_barrier((values, *others))[0]


def swap_pair(values):
    count = lax.axis_size("row")
    return lax.ppermute(values, "row", [(r, r ^ 2) for r in range(count)])


def swap_core(values):
    count = lax.axis_size("row")
    return lax.ppermute(values, "row", [(r, r ^ 1) for r in range(count)])


def swap_col(values):
    count = lax.axis_size("col")
    return lax.ppermute(values, "col", [(r, r ^ 1) for r in range(count)])


def pick(values, index, axis):
    return lax.dynamic_index_in_dim(values, index, axis, keepdims=False)


def joined(own, other, index, axis):
    return jnp.where(
        index == 0, jnp.concatenate([own, other], axis), jnp.concatenate([other, own], axis)
    )


def turned(values, pair):
    half = values.shape[-1] // 2
    swapped = jnp.concatenate([values[..., half:], values[..., :half]], axis=-1)
    return jnp.where(pair == 0, values, swapped)


def gather_quad(values):
    across = swap_col(values)
    return [values, swap_core(values), across, swap_core(across)]


def dot_nt(left, right):
    return lax.dot_general(left, right, (((1,), (1,)), ((), ())), preferred_element_type=f32)


def dot_nn(left, right):
    return lax.dot_general(left, right, (((1,), (0,)), ((), ())), preferred_element_type=f32)


def dot_tn(left, right):
    return lax.dot_general(left, right, (((0,), (0,)), ((), ())), preferred_element_type=f32)


def shape_of(shape, dtype):
    return jax.ShapeDtypeStruct(shape, dtype)


VMEM = pl.BlockSpec(memory_space=pltpu.VMEM)
SMEM = pl.BlockSpec(memory_space=pltpu.SMEM)


def near(name, body, ins, out_shape, scratch=(), scalars=None, grid=(), limit=8, in_specs=None, out_specs=None, alias=None):
    specs = in_specs or [VMEM] * len(ins)
    if out_specs is None:
        out_specs = [VMEM] * len(out_shape) if isinstance(out_shape, list) else VMEM
    return pl.pallas_call(
        body,
        grid=grid,
        in_specs=specs if scalars is None else [SMEM, *specs],
        out_specs=out_specs,
        out_shape=out_shape,
        scratch_shapes=list(scratch),
        input_output_aliases=alias or {},
        compiler_params=pltpu.CompilerParams(vmem_limit_bytes=limit << 20),
        name=name,
    )(*(() if scalars is None else (scalars,)), *ins)


def slot_owner(slots_ref, slot, count):
    found = 0
    for k in range(count):
        found = found + jnp.where(slots_ref[k] == slot, k, 0)
    return found


def take_slots(tokens, slots, pair, extra=None):
    count, size, width = tokens.shape
    groups = count // 2
    more = 0 if extra is None else extra.shape[0]

    def body(slots_ref, pair_ref, tokens_ref, *refs):
        @pl.when(pl.program_id(0) < groups)
        def _():
            refs[-1][...] = tokens_ref[...]

        if more:

            @pl.when(pl.program_id(0) >= groups)
            def _():
                refs[-1][...] = refs[0][...]

    def source(g, slots_ref, pair_ref):
        slot = 2 * jnp.minimum(g, groups - 1) + pair_ref[0]
        return slot_owner(slots_ref, slot, count), 0, 0

    specs = [pl.BlockSpec((1, size, width), source)]
    if more:
        specs.append(pl.BlockSpec((1, size, width), lambda g, *_: (jnp.maximum(g - groups, 0), 0, 0)))
    return pl.pallas_call(
        body,
        grid_spec=pltpu.PrefetchScalarGridSpec(
            num_scalar_prefetch=2,
            grid=(groups + more,),
            in_specs=specs,
            out_specs=pl.BlockSpec((1, size, width), lambda g, *_: (g, 0, 0)),
        ),
        out_shape=shape_of((groups + more, size, width), tokens.dtype),
        compiler_params=pltpu.CompilerParams(vmem_limit_bytes=6 << 20),
        name="take_slots",
    )(slots, pair.reshape(1).astype(jnp.int32), tokens, *([extra] if more else []))


def add(left, right):
    def body(left_ref, right_ref, out_ref):
        out_ref[...] = (left_ref[...].astype(f32) + right_ref[...].astype(f32)).astype(out_ref.dtype)

    return near("add", body, [left, right], shape_of(left.shape, left.dtype))


def cut(shard, index, axis, pieces=2):
    shape = list(shard.shape)
    shape[axis] //= pieces

    def body(_, in_ref, out_ref):
        out_ref[...] = in_ref[...]

    return pl.pallas_call(
        body,
        grid_spec=pltpu.PrefetchScalarGridSpec(
            num_scalar_prefetch=1,
            grid=(1,),
            in_specs=[pl.BlockSpec(tuple(shape), lambda i, s: (s[0], 0) if axis == 0 else (0, s[0]))],
            out_specs=VMEM,
        ),
        out_shape=shape_of(tuple(shape), shard.dtype),
        compiler_params=pltpu.CompilerParams(vmem_limit_bytes=8 << 20),
        name="cut",
    )(index.reshape(1).astype(jnp.int32), shard)


def lay(got, shard, core, axis):
    rows, cols = got.shape
    out = (2 * rows, cols) if axis == 1 else (rows, 2 * cols)

    def body(s, got_ref, shard_ref, out_ref):
        for place in range(2):

            @pl.when(s[0] == place)
            def _():
                if axis == 1:
                    out_ref[place * rows : (place + 1) * rows, :] = shard_ref[...]
                    out_ref[(1 - place) * rows : (2 - place) * rows, :] = got_ref[...]
                else:
                    out_ref[:, place * cols : (place + 1) * cols] = shard_ref[...]
                    out_ref[:, (1 - place) * cols : (2 - place) * cols] = got_ref[...]

    return pl.pallas_call(
        body,
        grid_spec=pltpu.PrefetchScalarGridSpec(
            num_scalar_prefetch=1,
            grid=(1,),
            in_specs=[
                VMEM,
                pl.BlockSpec((rows, cols), lambda i, s: (0, s[0]) if axis == 1 else (s[0], 0)),
            ],
            out_specs=VMEM,
        ),
        out_shape=shape_of(out, shard.dtype),
        compiler_params=pltpu.CompilerParams(vmem_limit_bytes=8 << 20),
        name="lay",
    )(core.reshape(1).astype(jnp.int32), got, shard)


def inverse_scale(values):
    return lax.rsqrt(jnp.mean(values * values, axis=-1, keepdims=True) + norm_epsilon)


def turn_block(values, pair):
    half = values.shape[-1] // 2
    return jnp.where(
        pair == 0, values, jnp.concatenate([values[..., half:], values[..., :half]], axis=-1)
    )


SLAB = 64


def slabs(count):
    return [slice(at, at + SLAB) for at in range(0, count, SLAB)]


def norm(rows, gain):
    def body(rows_ref, gain_ref, out_ref):
        for here in slabs(rows.shape[0]):
            values = rows_ref[here, :].astype(f32)
            out_ref[here, :] = (values * inverse_scale(values) * gain_ref[...]).astype(bf16)

    return near("norm", body, [rows, gain], shape_of(rows.shape, bf16))


def sum_norm(rows, own, beside, across, gain):
    def body(rows_ref, own_ref, beside_ref, across_ref, gain_ref, middle_ref, out_ref):
        for here in slabs(rows.shape[0]):
            total = own_ref[here, :].astype(f32) + beside_ref[here, :].astype(f32)
            values = rows_ref[here, :].astype(f32) + (total + across_ref[here, :].astype(f32))
            middle_ref[here, :] = values
            out_ref[here, :] = (values * inverse_scale(values) * gain_ref[...]).astype(bf16)

    return near(
        "sum_norm",
        body,
        [rows, own, beside, across, gain],
        [shape_of(rows.shape, f32), shape_of(rows.shape, bf16)],
    )


def norm_backward(values, own, beside, across, base, gain, pair=None, groups=None):
    count, width = values.shape
    size = count // 2
    piece = size // (groups or 1)

    def body(s, values_ref, own_ref, beside_ref, across_ref, base_ref, gain_ref, *out_refs):
        term = jnp.zeros((1, width), f32)
        for here in slabs(count):
            grad = own_ref[here, :].astype(f32) + beside_ref[here, :].astype(f32) + across_ref[here, :].astype(f32)
            vals = values_ref[here, :].astype(f32)
            scale = inverse_scale(vals)
            weighted = grad * gain_ref[...]
            inner = jnp.mean(weighted * vals, axis=-1, keepdims=True)
            total = scale * weighted - vals * (scale * scale * scale) * inner
            total = base_ref[here, :].astype(f32) + total
            if groups is None:
                out_refs[0][here, :] = total
                out_refs[1][here, :] = total.astype(bf16)
            else:
                total = turn_block(total, s[0])
                step = min(piece, SLAB)
                for at in range(here.start, here.stop, step):
                    side, rest = at // size, at % size
                    group, first = rest // piece, rest % piece
                    rows = total[at - here.start : at - here.start + step]
                    out_refs[0][group, side, first : first + step, :] = rows.astype(bf16)
            term = term + jnp.sum(grad * vals * scale, axis=0, keepdims=True)
        out_refs[-1][...] = term

    if groups is None:
        shapes = [shape_of((count, width), f32), shape_of((count, width), bf16)]
    else:
        shapes = [shape_of((groups, 2, piece, width), bf16)]
    return near(
        "norm_backward",
        body,
        [values, own, beside, across, base, gain],
        [*shapes, shape_of((1, width), f32)],
        scalars=jnp.zeros((1,), jnp.int32) if pair is None else pair.reshape(1),
    )


def arrange_tokens(arrived, kept, pair):
    groups, size, width = kept.shape

    def body(s, arrived_ref, kept_ref, out_ref):
        for place in range(2):

            @pl.when(s[0] == place)
            def _():
                for group in range(groups):
                    out_ref[group, place] = turn_block(kept_ref[group], s[0])
                    out_ref[group, 1 - place] = turn_block(arrived_ref[group], s[0])

    return near(
        "arrange_tokens",
        body,
        [arrived, kept],
        shape_of((groups, 2, size, width), bf16),
        scalars=pair.reshape(1),
    )


def is_valid(s, half, size):
    first = (half * 4 + 2 * s[1] + s[2]) * size
    return first + lax.broadcasted_iota(jnp.int32, (size, 1), 0) < s[3]


def arrange_cotangent(cots, other, scalars):
    _, size, width = cots.shape

    def body(s, own_ref, other_ref, out_ref):
        for half in range(2):
            good = is_valid(s, half, size)

            @pl.when(half == s[0])
            def _():
                rows = turn_block(own_ref[half].astype(f32), s[0])
                out_ref[half * size : (half + 1) * size, :] = jnp.where(good, rows, 0.0).astype(bf16)

            @pl.when(half != s[0])
            def _():
                rows = turn_block(other_ref[0:size, :].astype(f32), s[0])
                out_ref[half * size : (half + 1) * size, :] = jnp.where(good, rows, 0.0).astype(bf16)

    return near(
        "arrange_cotangent",
        body,
        [cots, other],
        shape_of((2 * size, width), bf16),
        scalars=scalars,
    )


def final_rows(middle, own, beside, across, scalars):
    count, width = middle.shape
    size = count // 2

    def body(s, middle_ref, own_ref, beside_ref, across_ref, out_ref, away_ref):
        for half in range(2):
            good = is_valid(s, half, size)
            here = slice(half * size, (half + 1) * size)
            total = own_ref[here, :].astype(f32) + beside_ref[here, :].astype(f32)
            total = middle_ref[here, :] + (total + across_ref[here, :].astype(f32))
            rows = turn_block(jnp.where(good, total, 0.0), s[0]).astype(bf16)

            @pl.when(half == s[0])
            def _():
                out_ref[...] = rows

            @pl.when(half != s[0])
            def _():
                away_ref[...] = rows

    return near(
        "final_rows",
        body,
        [middle, own, beside, across],
        [shape_of((size, width), bf16)] * 2,
        scalars=scalars,
    )


def part_of(where_ref, chunk, half):
    core = jnp.bitwise_xor(where_ref[0], chunk % 2)
    col = jnp.bitwise_xor(where_ref[1], chunk // 2)
    return half * 4 + core * 2 + col


def scan_lanes(values, backwards):
    count = values.shape[1]
    lane = lax.broadcasted_iota(jnp.int32, values.shape, 1)
    step = 1
    while step < count:
        if backwards:
            moved = pltpu.roll(values, count - step, 1)
            values = values + jnp.where(lane < count - step, moved, 0.0)
        else:
            moved = pltpu.roll(values, step, 1)
            values = values + jnp.where(lane >= step, moved, 0.0)
        step *= 2
    return values


def log_sigmoid(values):
    return jnp.minimum(values, 0.0) - jnp.log1p(jnp.exp(-jnp.abs(values)))


def attention_forward(chunks, own_w, other_w, forget, bias, where, heads, head_size):
    each, width = chunks[0].shape
    count, half = 4 * each, width // 2
    size = count // 8
    pairs = heads // 2
    per = 4 * head_size
    step = min(STEP, count)

    def body(where_ref, x0, x1, x2, x3, own_ref, other_ref, forget_ref, bias_ref,
             gated_ref, proj_ref, mixed_ref, logit_ref, prefix_ref, base_ref, rows, cols):
        pid = pl.program_id(0)
        lanes = pl.multiple_of(pid * 2 * per, 2 * per)
        pair_lanes = pl.multiple_of(pid * 2 * head_size, 2 * head_size)
        xs = (x0, x1, x2, x3)

        @pl.when(pid == 0)
        def _():
            for chunk in range(4):
                logits = dot_nt(forget_ref[...], xs[chunk][...]) + bias_ref[:, 0:1]
                for side in range(2):
                    start = pl.multiple_of(part_of(where_ref, chunk, side) * size, size)
                    logit_ref[:, pl.ds(start, size)] = logits[:, side * size : (side + 1) * size]
            sums = scan_lanes(log_sigmoid(logit_ref[...]), False)
            prefix_ref[...] = sums
            for part in range(8):
                block = sums[:, part * size : (part + 1) * size]
                tall = jnp.concatenate([block, jnp.zeros((128 - 8, size), f32)], axis=0)
                cols[part * size : (part + 1) * size, :] = tall.T

        for chunk in range(4):
            made = dot_nn(xs[chunk][:, :half], own_ref[:, pl.ds(lanes, 2 * per)])
            made = (made + dot_nn(xs[chunk][:, half:], other_ref[:, pl.ds(lanes, 2 * per)])).astype(bf16)
            for side in range(2):
                start = pl.multiple_of(part_of(where_ref, chunk, side) * size, size)
                rows[pl.ds(start, size), :] = made[side * size : (side + 1) * size]
        proj_ref[:, pl.ds(lanes, 2 * per)] = rows[...]
        lane = lax.broadcasted_iota(jnp.int32, (step, 128), 1)
        apart = lax.broadcasted_iota(jnp.int32, (step, step), 1) <= lax.broadcasted_iota(
            jnp.int32, (step, step), 0
        )
        for first in range(0, count, step):
            last = first + step
            mixed_two, gated_two, base_two = [], [], []
            for side in range(2):
                at = side * per
                head = pid * 2 + side
                query = rows[first:last, at : at + head_size]
                key = rows[0:last, at + head_size : at + 2 * head_size]
                value = rows[0:last, at + 2 * head_size : at + 3 * head_size]
                gate = rows[first:last, at + 3 * head_size : at + 4 * head_size].astype(f32)
                own = jnp.sum(jnp.where(lane == head, cols[first:last, :], 0.0), axis=1, keepdims=True)
                allp = prefix_ref[pl.ds(head, 1), 0:last]
                score = dot_nt(query, key) * head_size ** (-0.5) + own - allp
                tail = jnp.where(apart, score[:, first:last], masked_score)
                score = tail if first == 0 else jnp.concatenate([score[:, :first], tail], axis=1)
                top = jnp.max(score, axis=1, keepdims=True)
                weight = jnp.exp(score - top)
                total = jnp.sum(weight, axis=1, keepdims=True)
                mixed = dot_nn(weight.astype(bf16), value) / total
                mixed_two.append(mixed)
                gated_two.append(mixed * jax.nn.sigmoid(gate))
                base_two.append(own - top - jnp.log(total))
            mixed_ref[first:last, pl.ds(pair_lanes, 2 * head_size)] = jnp.concatenate(mixed_two, axis=1)
            gated = jnp.concatenate(gated_two, axis=1).astype(bf16)
            base_ref[pid, first:last, :] = jnp.where(lane == 0, base_two[0], base_two[1])
            for part in range(first // size, last // size):
                core = jnp.bitwise_xor(where_ref[0], (part // 2) % 2)
                col = jnp.bitwise_xor(where_ref[1], part % 2)
                start = pl.multiple_of(((col * 2 + core) * 2 + part // 4) * size, size)
                off = part * size - first
                gated_ref[pl.ds(start, size), pl.ds(pair_lanes, 2 * head_size)] = gated[off : off + size]

    return near(
        "attention_forward",
        body,
        [*chunks, own_w, other_w, forget, bias],
        [
            shape_of((count, heads * head_size), bf16),
            shape_of((count, heads * per), bf16),
            shape_of((count, heads * head_size), f32),
            shape_of((8, count), f32),
            shape_of((8, count), f32),
            shape_of((pairs, count, 128), f32),
        ],
        [pltpu.VMEM((count, 2 * per), bf16), pltpu.VMEM((count, 128), f32)],
        where,
        grid=(pairs,),
        limit=12,
    )


def attention_backward(chunks, out_w, saved, where, pid, head_size):
    projected, mixed, logits, prefix, base = saved
    each, width = chunks[0].shape
    count, own_half = 4 * each, width // 2
    size = count // 8
    per = 4 * head_size
    step = min(STEP, count)
    scale = head_size ** (-0.5)

    def body(where_ref, m0, m1, m2, m3, out0_ref, out1_ref, saved_ref, mixes_ref, prefix_ref, base_ref,
             proj_ref, places_ref, rows, grads, key_sum, value_sum, query_out):
        for chunk, ref in enumerate((m0, m1, m2, m3)):
            here = slice(pid * 2 * head_size, (pid + 1) * 2 * head_size)
            made = dot_nt(ref[:, :own_half], out0_ref[here, :])
            made = made + dot_nt(ref[:, own_half:], out1_ref[here, :])
            for side in range(2):
                start = pl.multiple_of(part_of(where_ref, chunk, side) * size, size)
                grads[pl.ds(start, size), :] = made[side * size : (side + 1) * size]
        rows[...] = saved_ref[:, pid * 2 * per : (pid + 1) * 2 * per]
        lane_all = lax.broadcasted_iota(jnp.int32, (count, 128), 1)
        apart = lax.broadcasted_iota(jnp.int32, (step, step), 1) <= lax.broadcasted_iota(
            jnp.int32, (step, step), 0
        )
        sums = []
        outs = []
        one = jnp.ones((count, 1), bf16)
        pad = jnp.zeros((count, 128 - head_size - 1), bf16)
        for side in range(2):
            at = side * per
            head = pid * 2 + side
            query = rows[:, at : at + head_size]
            key = rows[:, at + head_size : at + 2 * head_size]
            value = rows[:, at + 2 * head_size : at + 3 * head_size]
            gate = jax.nn.sigmoid(rows[:, at + 3 * head_size : at + 4 * head_size].astype(f32))
            grad = grads[:, side * head_size : (side + 1) * head_size]
            mix = mixes_ref[:, (pid * 2 + side) * head_size : (pid * 2 + side + 1) * head_size]
            grad_mix = (grad * gate).astype(bf16)
            inner = jnp.sum(grad_mix.astype(f32) * mix, axis=1, keepdims=True)
            grad_gate = grad * mix * gate * (1.0 - gate)
            query_one = jnp.concatenate([query, one, pad], axis=1)
            key_one = jnp.concatenate([key, one, pad], axis=1)
            key_sum[...] = jnp.zeros((count, 128), f32)
            value_sum[...] = jnp.zeros((count, head_size), f32)
            for first in range(0, count, step):
                last = first + step
                own = base_ref[pid, first:last, side : side + 1]
                allp = prefix_ref[head : head + 1, 0:last]
                score = dot_nt(query[first:last], key[0:last]) * scale + own - allp
                tail = jnp.where(apart, score[:, first:last], masked_score)
                score = tail if first == 0 else jnp.concatenate([score[:, :first], tail], axis=1)
                probs = jnp.exp(score)
                grad_probs = dot_nt(grad_mix[first:last], value[0:last])
                grad_score = (probs * (grad_probs - inner[first:last])).astype(bf16)
                query_out[first:last, :] = dot_nn(grad_score, key_one[0:last])
                key_sum[0:last, :] += dot_tn(grad_score, query_one[first:last])
                value_sum[0:last, :] += dot_tn(probs.astype(bf16), grad_mix[first:last])
            dq = query_out[...]
            dk = key_sum[...]
            sums.append(dq[:, head_size : head_size + 1] - dk[:, head_size : head_size + 1])
            outs += [dq[:, :head_size] * scale, dk[:, :head_size] * scale, value_sum[...], grad_gate]
        full = jnp.concatenate(outs, axis=1).astype(bf16)
        for part in range(8):
            core = jnp.bitwise_xor(where_ref[0], (part // 2) % 2)
            col = jnp.bitwise_xor(where_ref[1], part % 2)
            start = pl.multiple_of(((col * 2 + core) * 2 + part // 4) * size, size)
            proj_ref[pl.ds(start, size), :] = full[part * size : (part + 1) * size]
        both = jnp.where(lane_all == 0, sums[0], jnp.where(lane_all == 1, sums[1], 0.0))
        for part in range(8):
            here = slice(part * size, (part + 1) * size)
            places_ref[:, here] = both[here].T[0:8, :]

    return near(
        "attention_backward",
        body,
        [*chunks, *out_w, projected, mixed, prefix, base],
        [shape_of((count, 2 * per), bf16), shape_of((8, count), f32)],
        [
            pltpu.VMEM((count, 2 * per), bf16),
            pltpu.VMEM((count, 2 * head_size), f32),
            pltpu.VMEM((count, 128), f32),
            pltpu.VMEM((count, head_size), f32),
            pltpu.VMEM((count, 128), f32),
        ],
        where,
        limit=16,
    )


def grad_log(places, logits, where, each):
    count = logits.shape[1]
    size = count // 8

    def body(where_ref, *refs):
        parts, logit_ref, out_ref, rows = refs[:-3], refs[-3], refs[-2], refs[-1]
        rows[...] = jnp.zeros((8, count), f32)
        for k, ref in enumerate(parts):
            rows[2 * k : 2 * k + 2, :] = ref[0:2, :]
        rows[...] = scan_lanes(rows[...], True) * jax.nn.sigmoid(-logit_ref[...])
        for chunk in range(4):
            for side in range(2):
                start = pl.multiple_of(part_of(where_ref, chunk, side) * size, size)
                at = chunk * each + side * size
                out_ref[:, at : at + size] = rows[:, pl.ds(start, size)]

    return near(
        "grad_log",
        body,
        [*places, logits],
        shape_of((8, count), f32),
        [pltpu.VMEM((8, count), f32)],
        where,
    )


WIDE = 256


def spread(terms, name, extra=None):
    count = terms[0][0].shape[0]
    half = terms[0][1].shape[1] if terms[0][3] is None else terms[0][1].shape[0]
    each = count // 4
    ins = [array for term in terms for array in term[:3]] + list(extra or ())

    def body(*refs):
        out_refs = refs[-4:]
        for chunk in (2, 3, 0, 1):
            rows = slice(chunk * each, (chunk + 1) * each)
            for at in range(0, 2 * half, WIDE):
                side, here = at // half, slice(at % half, at % half + WIDE)
                total = 0.0
                for k, (left, _, _, kind) in enumerate(terms):
                    left_ref, weight_ref = refs[3 * k], refs[3 * k + 1 + side]
                    if kind is None:
                        total = total + dot_nn(left_ref[rows, :], weight_ref[:, here])
                    else:
                        inner = left.shape[1]
                        weight = weight_ref[here, kind * inner : (kind + 1) * inner]
                        total = total + dot_nt(left_ref[rows, :], weight)
                if extra is not None:
                    log_ref, forget_ref = refs[3 * len(terms)], refs[3 * len(terms) + 1]
                    total = total + dot_tn(log_ref[:, rows].astype(bf16), forget_ref[:, at : at + WIDE])
                out_refs[chunk][:, at : at + WIDE] = total.astype(bf16)

    return near(name, body, ins, [shape_of((each, 2 * half), bf16)] * 4, limit=12)


TILE = 256


def ffn_forward(chunks, gate_w, up_w):
    each, width = chunks[0].shape
    count, half = 4 * each, width // 2
    units = gate_w[0].shape[1]

    def body(x0, x1, x2, x3, gate0, gate1, up0, up1, gate_ref, up_ref, hidden_ref):
        for chunk, ref in enumerate((x0, x1, x2, x3)):
            here = slice(chunk * each, (chunk + 1) * each)
            for at in range(0, units, TILE):
                cols = slice(at, at + TILE)
                gate = dot_nn(ref[:, :half], gate0[:, cols]) + dot_nn(ref[:, half:], gate1[:, cols])
                up = dot_nn(ref[:, :half], up0[:, cols]) + dot_nn(ref[:, half:], up1[:, cols])
                gate_ref[here, cols] = gate.astype(bf16)
                up_ref[here, cols] = up.astype(bf16)
                hidden_ref[here, cols] = (gate * jax.nn.sigmoid(gate) * up).astype(bf16)

    return near(
        "ffn_forward", body, [*chunks, *gate_w, *up_w], [shape_of((count, units), bf16)] * 3
    )


def ffn_backward(chunks, down_w, gate_proj, up_proj):
    each, width = chunks[0].shape
    count, half = 4 * each, width // 2
    units = gate_proj.shape[1]

    def body(g0, g1, g2, g3, down0, down1, gate_ref, up_ref, grad_gate_ref, grad_up_ref):
        for chunk, ref in enumerate((g0, g1, g2, g3)):
            here = slice(chunk * each, (chunk + 1) * each)
            for at in range(0, units, TILE):
                cols = slice(at, at + TILE)
                grad = dot_nt(ref[:, :half], down0[cols, :]) + dot_nt(ref[:, half:], down1[cols, :])
                gate = gate_ref[here, cols].astype(f32)
                up = up_ref[here, cols].astype(f32)
                sig = jax.nn.sigmoid(gate)
                slope = sig * (1.0 + gate * (1.0 - sig))
                grad_gate_ref[here, cols] = (grad * up * slope).astype(bf16)
                grad_up_ref[here, cols] = (grad * gate * sig).astype(bf16)

    return near(
        "ffn_backward",
        body,
        [*chunks, *down_w, gate_proj, up_proj],
        [shape_of((count, units), bf16)] * 2,
    )


def grad_rows_weight(chunks, right, side, first, size, got=None):
    each, width = chunks[0].shape
    half = width // 2

    def body(x0, x1, x2, x3, right_ref, *refs):
        for at in range(0, half, TILE):
            total = 0.0 if got is None else refs[0][at : at + TILE, :].astype(f32)
            cols = slice(side * half + at, side * half + at + TILE)
            for chunk, ref in enumerate((x0, x1, x2, x3)):
                rows = slice(chunk * each, (chunk + 1) * each)
                total = total + dot_tn(ref[:, cols], right_ref[rows, first : first + size])
            refs[-1][at : at + TILE, :] = total.astype(bf16)

    return near(
        "grad_rows_weight",
        body,
        [*chunks, right] + ([] if got is None else [got]),
        shape_of((half, size), bf16),
    )


def grad_cols_weight(left, chunks, side, first, size, got=None):
    each, width = chunks[0].shape
    half = width // 2
    tile = TILE if size % TILE == 0 else 128

    def body(left_ref, x0, x1, x2, x3, *refs):
        for at in range(0, size, tile):
            total = 0.0 if got is None else refs[0][at : at + tile, :].astype(f32)
            for chunk, ref in enumerate((x0, x1, x2, x3)):
                rows = slice(chunk * each, (chunk + 1) * each)
                left_block = left_ref[rows, first + at : first + at + tile]
                total = total + dot_tn(left_block, ref[:, side * half : (side + 1) * half])
            refs[-1][at : at + tile, :] = total.astype(bf16)

    return near(
        "grad_cols_weight",
        body,
        [left, *chunks] + ([] if got is None else [got]),
        shape_of((size, half), bf16),
    )


def small_grads(grad_logits, chunks, gain_one, gain_two, scalars, heads, own_heads):
    each, width = chunks[0].shape
    tall = -(-(heads + 3) // 8) * 8

    def body(s, log_ref, x0, x1, x2, x3, one_ref, two_ref, out_ref):
        low = log_ref[...].astype(bf16)
        total = 0.0
        for chunk, ref in enumerate((x0, x1, x2, x3)):
            total = total + dot_nn(low[:, chunk * each : (chunk + 1) * each], ref[...])
        total = turn_block(total, s[0])
        place = 2 * s[2] + s[1]
        out_ref[...] = jnp.zeros((tall, width), f32)
        for k in range(heads // own_heads):

            @pl.when(place == k)
            def _():
                out_ref[k * own_heads : (k + 1) * own_heads, :] = total[0:own_heads, :]

        out_ref[heads : heads + 1, :] = turn_block(one_ref[...], s[0])
        out_ref[heads + 1 : heads + 2, :] = turn_block(two_ref[...], s[0])
        bias = jnp.sum(low.astype(f32), axis=1, keepdims=True)
        lane = lax.broadcasted_iota(jnp.int32, (8, 128), 1)
        head = lax.broadcasted_iota(jnp.int32, (8, 128), 0)
        good = (lane == place * own_heads + head) & (head < own_heads)
        out_ref[heads + 2 : heads + 3, 0:128] = jnp.sum(jnp.where(good, bias, 0.0), axis=0, keepdims=True)

    return near(
        "small_grads",
        body,
        [grad_logits, *chunks, gain_one, gain_two],
        shape_of((tall, width), f32),
        scalars=scalars,
    )


def line_rows(own, before, behind, place):
    rows, cols = own.shape

    def body(s, *refs):
        out_ref = refs[-1]
        for at in range(4):
            for k in range(-3, 4):

                @pl.when(at - s[0] == k)
                def _():
                    out_ref[at * rows : (at + 1) * rows, :] = refs[k + 3][...]

    return near(
        "line_rows",
        body,
        [*reversed(before), own, *behind],
        shape_of((4 * rows, cols), own.dtype),
        scalars=place.reshape(1).astype(jnp.int32),
    )


def halves(ref, index, axis):
    half = ref.shape[axis] // 2
    here = slice(index * half, (index + 1) * half)
    return ref[here, :] if axis == 0 else ref[:, here]


def settle(inner, outer, scalars, axis):
    shape = list(inner.shape)
    shape[axis] //= 2

    def body(s, inner_ref, outer_ref, out_ref):
        for core in range(2):

            @pl.when((s[1] == 1) & (s[0] == core))
            def _():
                out_ref[...] = halves(inner_ref, 1 - core, axis)

            @pl.when((s[1] != 1) & (s[0] == core))
            def _():
                out_ref[...] = halves(outer_ref, 1 - core, axis)

    return near("settle", body, [inner, outer], shape_of(tuple(shape), inner.dtype), scalars=scalars)


def put(target, shape, inner, outer, got, scalars, axis, piece, pieces):
    rows, cols = got.shape

    def body(s, *refs):
        inner_ref, outer_ref, got_ref = refs[-4:-1]
        out_ref = refs[-1]
        for core in range(2):

            @pl.when((pl.program_id(0) == 0) & (s[1] == 1) & (s[0] == core))
            def _():
                out_ref[...] = halves(inner_ref, core, axis).astype(f32)

            @pl.when((pl.program_id(0) == 0) & (s[1] != 1) & (s[0] == core))
            def _():
                out_ref[...] = halves(outer_ref, core, axis).astype(f32)

        @pl.when(pl.program_id(0) == 1)
        def _():
            out_ref[...] = got_ref[...].astype(f32)

    def out_map(i, s):
        place = jnp.bitwise_xor(s[0], i) * pieces + piece
        return (0, place) if axis == 0 else (place, 0)

    first = target is None
    ins = ([] if first else [target]) + [inner, outer, got]
    return pl.pallas_call(
        body,
        grid_spec=pltpu.PrefetchScalarGridSpec(
            num_scalar_prefetch=1,
            grid=(2,),
            in_specs=([] if first else [pl.BlockSpec(memory_space=pl.ANY)]) + [VMEM] * 3,
            out_specs=pl.BlockSpec((rows, cols), out_map),
        ),
        out_shape=shape_of(shape, f32),
        input_output_aliases={} if first else {1: 0},
        compiler_params=pltpu.CompilerParams(vmem_limit_bytes=12 << 20),
        name="put",
    )(scalars, *ins)


def line_gather(values):
    before, behind = [values], [values]
    for _ in range(3):
        before.append(lax.ppermute(before[-1], "dp", [(0, 1), (1, 2), (2, 3)]))
        behind.append(lax.ppermute(behind[-1], "dp", [(1, 0), (2, 1), (3, 2)]))
    return before[1:], behind[1:]


def chain_inward(values):
    return lax.ppermute(values, "dp", [(0, 1), (3, 2)])


def chain_middle(values):
    return lax.ppermute(values, "dp", [(1, 2), (2, 1)])


def chain_outward(values):
    return lax.ppermute(values, "dp", [(1, 0), (2, 3)])


AWAY, OWN, ONE, TWO, THREE, FOUR, ATT, SMALL_NEXT, SMALL, FFN_BACK, FFN_NFFN, DOWN_FWD = range(12)
SUM_TWO, SUM_THREE, SUM_FOUR, NORM_THREE, NORM_FOUR, FINAL, LOG, NATTN, BACK, TOKENS, REDUCE, BLOCK, PACK = range(12, 25)
DOWN, GATE, UP, OUT, ATTN = range(5)
ORDER = (
    (AWAY, DOWN, 0), (AWAY, DOWN, 1), (FFN_BACK,), (FFN_NFFN,),
    (AWAY, GATE, 0), (OWN, DOWN, 0), (SUM_THREE,), (AWAY, GATE, 1),
    (AWAY, UP, 0), (DOWN_FWD,), (OWN, DOWN, 1), (ONE, DOWN, 0),
    (NORM_THREE,), (SUM_TWO,), (OWN, GATE, 0), (ONE, DOWN, 1),
    (TWO, DOWN, 0), (OWN, GATE, 1), (ONE, GATE, 0), (TWO, DOWN, 1),
    (ATT, 0), (ATT, 1), (ONE, GATE, 1), (ATT, 2),
    (TWO, GATE, 0), (OWN, UP, 0), (LOG,), (NATTN,),
    (AWAY, OUT, 0), (TWO, GATE, 1), (SUM_FOUR,), (AWAY, ATTN, 0),
    (AWAY, ATTN, 1), (AWAY, ATTN, 2), (FINAL,), (THREE, DOWN, 0),
    (ONE, UP, 0), (OWN, ATTN, 0), (NORM_FOUR,), (SMALL,),
    (FOUR, DOWN, 0), (THREE, DOWN, 1), (SMALL_NEXT, 1), (OWN, ATTN, 1),
    (SMALL_NEXT, 2), (BACK,), (FOUR, DOWN, 1), (ONE, ATTN, 0),
    (THREE, GATE, 0), (THREE, GATE, 1), (TWO, UP, 0), (OWN, ATTN, 2),
    (FOUR, GATE, 0), (FOUR, GATE, 1), (OWN, OUT, 0), (ONE, ATTN, 1),
    (TWO, ATTN, 0), (SMALL_NEXT, 3), (ONE, ATTN, 2), (TOKENS,),
    (THREE, UP, 0), (ONE, OUT, 0), (TWO, ATTN, 1), (SMALL_NEXT, 4),
    (FOUR, UP, 0), (BLOCK,), (THREE, ATTN, 0), (TWO, ATTN, 2),
    (FOUR, ATTN, 0), (THREE, ATTN, 1), (TWO, OUT, 0), (SMALL_NEXT, 5),
    (FOUR, ATTN, 1), (THREE, ATTN, 2), (FOUR, ATTN, 2), (THREE, OUT, 0),
    (PACK,), (FOUR, OUT, 0),
)
PIECES = (2, 2, 1, 1, 3)
REDUCED = ()


class Store:
    pass


def shards(
    tokens,
    seq_lengths,
    seq_slots,
    w_attn,
    w_forget,
    b_forget,
    w_out,
    w_gate,
    w_up,
    w_down,
    gain_attn,
    gain_ffn,
    out_grad,
):
    count_seq = seq_slots.shape[0]
    piece_rows = tokens.shape[2]
    width = tokens.shape[3]
    groups = lax.axis_size("dp")
    row_index = lax.axis_index("row")
    pair, core = row_index // 2, row_index % 2
    col = lax.axis_index("col")
    group = lax.axis_index("dp")
    part_rows = out_grad.shape[2]
    own_heads = b_forget.shape[0] // 2
    all_heads = b_forget.shape[0] * lax.axis_size("col")
    head_size = w_out.shape[0] // (2 * own_heads)
    where = jnp.stack([core, col]).astype(jnp.int32)

    order = [None]

    def tie(values):
        return values if order[0] is None else after(values, order[0])

    def step(op, values, *others):
        out = op(tie(values), *others)
        order[0] = out[0] if isinstance(out, (list, tuple)) else out
        return out

    my_slot = 2 * group + pair
    my_length = jnp.sum(jnp.where(seq_slots == my_slot, seq_lengths, 0))
    scalars = jnp.stack([pair, core, col, my_length]).astype(jnp.int32)
    flat_tokens = tokens.reshape(count_seq, piece_rows, width)

    small = jnp.concatenate([w_forget.T, gain_attn[None], gain_ffn[None]], axis=0)
    small = joined(small, swap_core(small), core, 1)
    attn_cut = cut(w_attn, 1 - core, 1)
    order[0] = attn_cut
    gate_cut = step(cut, w_gate, 1 - core, 1)
    attn_got, gate_got = swap_core(attn_cut), swap_core(gate_cut)
    blocks = -(-small.shape[0] // piece_rows)
    extra = jnp.pad(small, ((0, blocks * piece_rows - small.shape[0]), (0, width // 2)))
    payload = take_slots(flat_tokens, seq_slots, 1 - pair, extra.reshape(blocks, piece_rows, width))
    payload_got = swap_pair(payload)
    arrived = payload_got
    order[0] = payload
    kept = step(lambda v: take_slots(v, seq_slots, pair), flat_tokens)

    cots = out_grad.reshape(2, part_rows, width)
    cots_sent = tie(pick(cots, 1 - pair, 0))
    cots_got = swap_pair(cots_sent)
    order[0] = cots_sent
    gate_own = step(lay, gate_got, w_gate, core, 1)
    if groups == 4:
        gate_quarter = step(cut, gate_own, group, 0, 4)
        gate_quarter = swap_pair(gate_quarter)
        before, behind = line_gather(gate_quarter)
        lines = [[before[k], behind[k]] for k in range(3)]
    else:
        lines = [[], [], []]
    out_cut = step(cut, w_out, 1 - core, 0)
    up_cut = step(cut, w_up, 1 - core, 1)
    down_cut = step(cut, w_down, 1 - core, 0)
    attn_own = step(lay, attn_got, w_attn, core, 1)
    outgoing = step(arrange_tokens, arrived, kept, pair)
    outgoing = outgoing.reshape(2 * groups, piece_rows, width)
    rows = lax.all_to_all(outgoing, "dp", split_axis=0, concat_axis=1, tiled=True)
    rows = rows.reshape(2 * part_rows, width)
    attn_own = after(attn_own, outgoing, *([gate_quarter] if groups == 4 else []))
    attn_w = [attn_own, swap_pair(attn_own)]
    order[0] = attn_own
    out_own = step(lay, swap_core(out_cut), w_out, core, 0)
    up_own = step(lay, swap_core(up_cut), w_up, core, 1)
    down_own = step(lay, swap_core(down_cut), w_down, core, 0)
    out_w = [out_own, swap_pair(out_own)]
    up_w = [up_own, swap_pair(up_own)]
    down_w = [down_own, swap_pair(down_own)]

    small_got = payload_got[groups:].reshape(-1, width)[: small.shape[0], : width // 2]
    small = jnp.concatenate([small, small_got], axis=1)
    forget = pick(small[: 2 * own_heads].reshape(2, own_heads, width), core, 0)
    forget = jnp.pad(forget, ((0, 8 - own_heads), (0, 0)))
    gain_one = small[2 * own_heads : 2 * own_heads + 1].astype(f32)
    gain_two = small[2 * own_heads + 1 : 2 * own_heads + 2].astype(f32)
    bias = pick(b_forget.reshape(2, own_heads), core, 0).astype(f32)
    bias = jnp.broadcast_to(jnp.pad(bias, (0, 8 - own_heads))[:, None], (8, 128))

    grad_final = step(arrange_cotangent, cots, cots_got, scalars)
    wide_grad = gather_quad(grad_final)
    normed_one = step(norm, after(rows, wide_grad[1]), gain_one)
    across = swap_col(normed_one)
    wide_one = [normed_one, swap_core(normed_one), across, swap_core(after(across, *lines[0]))]
    gated, *saved = attention_forward(
        [after(normed_one, order[0], wide_grad[2], *lines[1]), *wide_one[1:]],
        *attn_w, forget, bias, where, own_heads, head_size
    )
    order[0] = gated
    part = step(lambda v: spread([(v, *out_w, None)], "out_forward"), after(gated, *lines[2]))
    sent_one = step(add, part[2], swap_core(part[3]))
    across = swap_col(sent_one)
    if groups == 4:
        gate_w = [gate_own, step(line_rows, gate_quarter, before, behind, group)]
    else:
        gate_w = [gate_own, swap_pair(gate_own)]
    middle, normed_two = step(sum_norm, after(rows, up_w[1]), part[0], swap_core(part[1]), across, gain_two)
    across = swap_col(normed_two)
    wide_two = [normed_two, swap_core(normed_two), across, swap_core(across)]
    gate_proj, up_proj, hidden = step(ffn_forward, wide_two, gate_w, up_w)

    parts = own_heads // 2
    inner = ((group == 1) | (group == 2)) if groups == 4 else (group >= 0)
    flags = jnp.stack([core, inner.astype(jnp.int32)]).astype(jnp.int32)
    shapes = (w_down.shape, w_gate.shape, w_up.shape, w_out.shape, w_attn.shape)
    grads = [None] * 5
    have = Store()
    have.units, have.projected, have.places = {}, {}, {}

    def operands(name, piece):
        pieces = PIECES[name]
        if name == ATTN:
            return grad_rows_weight, wide_one, have.projected[piece], 0, w_attn.shape[1] // (2 * pieces)
        size = shapes[name][0 if name in (DOWN, OUT) else 1] // (2 * pieces)
        if name == DOWN:
            return grad_cols_weight, hidden, wide_grad, piece * size, size
        if name == OUT:
            return grad_cols_weight, gated, have.wide_mid, 0, size
        return grad_rows_weight, wide_two, have.grad_gate if name == GATE else have.grad_up, piece * size, size

    def product(name, piece, side, got=None):
        kind, left, right, first, size = operands(name, piece)
        if kind is grad_rows_weight:
            return step(lambda v: kind(left, v, side, first, size, got), right)
        if isinstance(left, list):
            return step(lambda v: kind([v, *left[1:]], right, side, first, size, got), left[0])
        return step(lambda v: kind(v, right, side, first, size, got), left)

    def away(name, piece):
        have.units[name, piece] = swap_pair(product(name, piece, 1))

    def own(name, piece):
        mine = product(name, piece, 0, have.units[name, piece])
        chained = groups == 4 and name not in REDUCED
        have.units[name, piece] = (mine, chain_inward(mine) if chained else None)

    def reduce(*names):
        keys = [key for key in have.units if key[0] in names]
        sums = lax.psum([have.units[key][0] for key in keys], "dp")
        for key, total in zip(keys, sums):
            have.units[key] = (total, total)

    def one(name, piece):
        mine, got = have.units[name, piece]
        if groups == 4:
            mine = step(add, mine, got)
            got = chain_middle(mine)
        have.units[name, piece] = (mine, got)

    def two(name, piece):
        mine, got = have.units[name, piece]
        if groups == 4:
            mine = step(add, mine, got)
            got = chain_outward(mine)
        else:
            mine = got = lax.psum(mine, "dp")
        have.units[name, piece] = (mine, got)

    def three(name, piece):
        mine, got = have.units[name, piece]
        axis = 0 if operands(name, piece)[0] is grad_rows_weight else 1
        have.units[name, piece] = (mine, got, axis, swap_core(step(settle, mine, got, flags, axis)))

    def four(name, piece):
        mine, got, axis, beside = have.units[name, piece]
        grads[name] = step(
            lambda v: put(grads[name], shapes[name], mine, got, v, flags, axis, piece, PIECES[name]), beside
        )

    def ffn_back():
        have.grad_gate, have.grad_up = step(ffn_backward, wide_grad, down_w, gate_proj, up_proj)

    def ffn_nffn():
        terms = [(have.grad_up, *up_w, 0)]
        part = step(lambda v: spread([(v, *gate_w, 0), *terms], "ffn_nffn"), have.grad_gate)
        have.part_three = [*part, swap_core(part[3]), swap_core(part[1])]

    def down_fwd():
        part = step(lambda v: spread([(v, *down_w, None)], "down_forward"), hidden)
        have.part_two = [*part, swap_core(part[3]), swap_core(part[1])]

    def sums(part):
        return swap_col(step(add, part[2], part[4]))

    def sum_two():
        have.across_two = sums(have.part_two)

    def sum_three():
        have.across_three = sums(have.part_three)

    def sum_four():
        have.across_four = sums(have.part_four)

    def norm_three():
        part = have.part_three
        have.grad_middle, grad_attn, have.gain_two = step(
            norm_backward, middle, part[0], part[5], have.across_three, grad_final, gain_two
        )
        have.wide_mid = gather_quad(grad_attn)

    def final():
        part = have.part_two
        kept, away = step(final_rows, middle, part[0], part[5], have.across_two, scalars)
        have.final = (kept, swap_pair(away))

    def att(piece):
        have.projected[piece], have.places[piece] = step(
            lambda v: attention_backward([v, *have.wide_mid[1:]], out_w, saved, where, piece, head_size),
            have.wide_mid[0],
        )

    def log():
        places = [have.places[k] for k in range(parts)]
        have.grad_logits = step(lambda v: grad_log([v, *places[1:]], saved[2], where, 2 * part_rows), places[0])

    def nattn():
        grad = have.projected
        part = step(
            lambda v: spread(
                [(grad[k] if k else v, *attn_w, k) for k in range(parts)],
                "attn_nattn",
                (have.grad_logits, forget),
            ),
            grad[0],
        )
        have.part_four = [*part, swap_core(part[3]), swap_core(part[1])]

    def norm_four():
        part = have.part_four
        grad_rows, have.gain_one = step(
            norm_backward, rows, part[0], part[5], have.across_four, have.grad_middle, gain_one, pair, groups
        )
        have.returned = lax.all_to_all(grad_rows, "dp", split_axis=0, concat_axis=0, tiled=True)

    def back():
        returned = tie(have.returned)
        sent = pick(returned, 1 - pair, 1)
        have.back = (pick(returned, pair, 1), swap_pair(sent))
        order[0] = sent

    def tokens_last():
        stay, got = have.back
        stay = tie(stay)
        by_slot = jnp.stack([jnp.where(pair == 0, stay, got), jnp.where(pair == 0, got, stay)], 1)
        have.tokens = jnp.take(by_slot.reshape(count_seq, piece_rows, width), seq_slots, axis=0, mode="clip")
        order[0] = have.tokens

    def small_first():
        pack = step(
            small_grads, have.grad_logits, wide_one, have.gain_one, have.gain_two, scalars, all_heads, own_heads
        )
        have.small = (pack, swap_core(pack))

    def small_next(stage):
        pack, got = have.small
        if stage >= 3 and groups != 4:
            have.small = (pack if stage > 3 else lax.psum(step(add, pack, got), "dp"), None)
            return
        pack = step(add, pack, got)
        swap = (swap_col, swap_pair, chain_inward, chain_middle, chain_outward)[stage - 1]
        if stage == 2 and groups != 4:
            swap = swap_pair
        have.small = (pack, swap(pack))

    def block():
        kept, got = have.final
        have.block_out = joined(tie(kept)[None], got[None], pair, 0)
        order[0] = have.block_out

    def pack_last():
        have.pack, got = have.small
        if groups == 4:
            have.pack = jnp.where(inner, tie(have.pack), got)
            order[0] = have.pack

    single = {
        BLOCK: block,
        PACK: pack_last,
        FFN_BACK: ffn_back,
        FFN_NFFN: ffn_nffn,
        DOWN_FWD: down_fwd,
        SUM_TWO: sum_two,
        SUM_THREE: sum_three,
        SUM_FOUR: sum_four,
        NORM_THREE: norm_three,
        NORM_FOUR: norm_four,
        FINAL: final,
        LOG: log,
        NATTN: nattn,
        BACK: back,
        TOKENS: tokens_last,
        SMALL: small_first,
        ATT: att,
        REDUCE: reduce,
        SMALL_NEXT: small_next,
        AWAY: away,
        OWN: own,
        ONE: one,
        TWO: two,
        THREE: three,
        FOUR: four,
    }
    for entry in ORDER:
        single[entry[0]](*entry[1:])

    block_out, pack = have.block_out, have.pack
    block_width = gain_attn.shape[0]
    mine = lax.dynamic_slice_in_dim(pack, row_index * block_width, block_width, 1)
    forget_grad = lax.dynamic_slice_in_dim(mine, col * 2 * own_heads, 2 * own_heads, 0).T
    bias_grad = lax.dynamic_slice_in_dim(pack[all_heads + 2], col * 2 * own_heads, 2 * own_heads)
    return (
        block_out[:, None],
        have.tokens[:, None],
        grads[ATTN],
        forget_grad,
        bias_grad,
        grads[OUT],
        grads[GATE],
        grads[UP],
        grads[DOWN],
        mine[all_heads],
        mine[all_heads + 1],
    )


def solution(mesh):
    return jax.shard_map(
        shards,
        mesh=mesh,
        in_specs=(
            P(None, ("row", "col"), "dp", None),
            P(),
            P(),
            P("row", "col"),
            P("row", "col"),
            P("col"),
            P("col", "row"),
            P("row", "col"),
            P("row", "col"),
            P("col", "row"),
            P("row"),
            P("row"),
            P("dp", ("row", "col"), None, None),
        ),
        out_specs=(
            P("dp", ("row", "col"), None, None),
            P(None, ("row", "col"), "dp", None),
            P("row", "col"),
            P("row", "col"),
            P("col"),
            P("col", "row"),
            P("row", "col"),
            P("row", "col"),
            P("col", "row"),
            P("row"),
            P("row"),
        ),
        check_vma=False,
    )
```

```python
import jax
import jax.numpy as jnp
from jax import lax
from jax.experimental import pallas as pl
from jax.experimental.pallas import tpu as pltpu
from jax.sharding import PartitionSpec as P

bf16 = jnp.bfloat16
f32 = jnp.float32
norm_epsilon = 1e-06
masked_score = -1e30
STEP = 256


def after(values, *others):
    return lax.optimization_barrier((values, *others))[0]


def swap_pair(values):
    count = lax.axis_size("row")
    return lax.ppermute(values, "row", [(r, r ^ 2) for r in range(count)])


def swap_core(values):
    count = lax.axis_size("row")
    return lax.ppermute(values, "row", [(r, r ^ 1) for r in range(count)])


def swap_col(values):
    count = lax.axis_size("col")
    return lax.ppermute(values, "col", [(r, r ^ 1) for r in range(count)])


def pick(values, index, axis):
    return lax.dynamic_index_in_dim(values, index, axis, keepdims=False)


def joined(own, other, index, axis):
    return jnp.where(
        index == 0, jnp.concatenate([own, other], axis), jnp.concatenate([other, own], axis)
    )


def turned(values, pair):
    half = values.shape[-1] // 2
    swapped = jnp.concatenate([values[..., half:], values[..., :half]], axis=-1)
    return jnp.where(pair == 0, values, swapped)


def gather_quad(values):
    across = swap_col(values)
    return [values, swap_core(values), across, swap_core(across)]


def dot_nt(left, right):
    return lax.dot_general(left, right, (((1,), (1,)), ((), ())), preferred_element_type=f32)


def dot_nn(left, right):
    return lax.dot_general(left, right, (((1,), (0,)), ((), ())), preferred_element_type=f32)


def dot_tn(left, right):
    return lax.dot_general(left, right, (((0,), (0,)), ((), ())), preferred_element_type=f32)


def shape_of(shape, dtype):
    return jax.ShapeDtypeStruct(shape, dtype)


VMEM = pl.BlockSpec(memory_space=pltpu.VMEM)
SMEM = pl.BlockSpec(memory_space=pltpu.SMEM)


def near(name, body, ins, out_shape, scratch=(), scalars=None, grid=(), limit=8, in_specs=None, out_specs=None, alias=None):
    specs = in_specs or [VMEM] * len(ins)
    if out_specs is None:
        out_specs = [VMEM] * len(out_shape) if isinstance(out_shape, list) else VMEM
    return pl.pallas_call(
        body,
        grid=grid,
        in_specs=specs if scalars is None else [SMEM, *specs],
        out_specs=out_specs,
        out_shape=out_shape,
        scratch_shapes=list(scratch),
        input_output_aliases=alias or {},
        compiler_params=pltpu.CompilerParams(vmem_limit_bytes=limit << 20),
        name=name,
    )(*(() if scalars is None else (scalars,)), *ins)


def slot_owner(slots_ref, slot, count):
    found = 0
    for k in range(count):
        found = found + jnp.where(slots_ref[k] == slot, k, 0)
    return found


def take_slots(tokens, slots, pair, extra=None):
    count, size, width = tokens.shape
    groups = count // 2
    more = 0 if extra is None else extra.shape[0]

    def body(slots_ref, pair_ref, tokens_ref, *refs):
        @pl.when(pl.program_id(0) < groups)
        def _():
            refs[-1][...] = tokens_ref[...]

        if more:

            @pl.when(pl.program_id(0) >= groups)
            def _():
                refs[-1][...] = refs[0][...]

    def source(g, slots_ref, pair_ref):
        slot = 2 * jnp.minimum(g, groups - 1) + pair_ref[0]
        return slot_owner(slots_ref, slot, count), 0, 0

    specs = [pl.BlockSpec((1, size, width), source)]
    if more:
        specs.append(pl.BlockSpec((1, size, width), lambda g, *_: (jnp.maximum(g - groups, 0), 0, 0)))
    return pl.pallas_call(
        body,
        grid_spec=pltpu.PrefetchScalarGridSpec(
            num_scalar_prefetch=2,
            grid=(groups + more,),
            in_specs=specs,
            out_specs=pl.BlockSpec((1, size, width), lambda g, *_: (g, 0, 0)),
        ),
        out_shape=shape_of((groups + more, size, width), tokens.dtype),
        compiler_params=pltpu.CompilerParams(vmem_limit_bytes=6 << 20),
        name="take_slots",
    )(slots, pair.reshape(1).astype(jnp.int32), tokens, *([extra] if more else []))


def add(left, right):
    def body(left_ref, right_ref, out_ref):
        out_ref[...] = (left_ref[...].astype(f32) + right_ref[...].astype(f32)).astype(out_ref.dtype)

    return near("add", body, [left, right], shape_of(left.shape, left.dtype))


def cut(shard, index, axis, pieces=2):
    shape = list(shard.shape)
    shape[axis] //= pieces

    def body(_, in_ref, out_ref):
        out_ref[...] = in_ref[...]

    return pl.pallas_call(
        body,
        grid_spec=pltpu.PrefetchScalarGridSpec(
            num_scalar_prefetch=1,
            grid=(1,),
            in_specs=[pl.BlockSpec(tuple(shape), lambda i, s: (s[0], 0) if axis == 0 else (0, s[0]))],
            out_specs=VMEM,
        ),
        out_shape=shape_of(tuple(shape), shard.dtype),
        compiler_params=pltpu.CompilerParams(vmem_limit_bytes=8 << 20),
        name="cut",
    )(index.reshape(1).astype(jnp.int32), shard)


def lay(got, shard, core, axis):
    rows, cols = got.shape
    out = (2 * rows, cols) if axis == 1 else (rows, 2 * cols)

    def body(s, got_ref, shard_ref, out_ref):
        for place in range(2):

            @pl.when(s[0] == place)
            def _():
                if axis == 1:
                    out_ref[place * rows : (place + 1) * rows, :] = shard_ref[...]
                    out_ref[(1 - place) * rows : (2 - place) * rows, :] = got_ref[...]
                else:
                    out_ref[:, place * cols : (place + 1) * cols] = shard_ref[...]
                    out_ref[:, (1 - place) * cols : (2 - place) * cols] = got_ref[...]

    return pl.pallas_call(
        body,
        grid_spec=pltpu.PrefetchScalarGridSpec(
            num_scalar_prefetch=1,
            grid=(1,),
            in_specs=[
                VMEM,
                pl.BlockSpec((rows, cols), lambda i, s: (0, s[0]) if axis == 1 else (s[0], 0)),
            ],
            out_specs=VMEM,
        ),
        out_shape=shape_of(out, shard.dtype),
        compiler_params=pltpu.CompilerParams(vmem_limit_bytes=8 << 20),
        name="lay",
    )(core.reshape(1).astype(jnp.int32), got, shard)


def inverse_scale(values):
    return lax.rsqrt(jnp.mean(values * values, axis=-1, keepdims=True) + norm_epsilon)


def turn_block(values, pair):
    half = values.shape[-1] // 2
    return jnp.where(
        pair == 0, values, jnp.concatenate([values[..., half:], values[..., :half]], axis=-1)
    )


SLAB = 64


def slabs(count):
    return [slice(at, at + SLAB) for at in range(0, count, SLAB)]


def norm(rows, gain):
    def body(rows_ref, gain_ref, out_ref):
        for here in slabs(rows.shape[0]):
            values = rows_ref[here, :].astype(f32)
            out_ref[here, :] = (values * inverse_scale(values) * gain_ref[...]).astype(bf16)

    return near("norm", body, [rows, gain], shape_of(rows.shape, bf16))


def sum_norm(rows, own, beside, across, gain):
    def body(rows_ref, own_ref, beside_ref, across_ref, gain_ref, middle_ref, out_ref):
        for here in slabs(rows.shape[0]):
            total = own_ref[here, :].astype(f32) + beside_ref[here, :].astype(f32)
            values = rows_ref[here, :].astype(f32) + (total + across_ref[here, :].astype(f32))
            middle_ref[here, :] = values
            out_ref[here, :] = (values * inverse_scale(values) * gain_ref[...]).astype(bf16)

    return near(
        "sum_norm",
        body,
        [rows, own, beside, across, gain],
        [shape_of(rows.shape, f32), shape_of(rows.shape, bf16)],
    )


def norm_backward(values, own, beside, across, base, gain, pair=None, groups=None):
    count, width = values.shape
    size = count // 2
    piece = size // (groups or 1)

    def body(s, values_ref, own_ref, beside_ref, across_ref, base_ref, gain_ref, *out_refs):
        term = jnp.zeros((1, width), f32)
        for here in slabs(count):
            grad = own_ref[here, :].astype(f32) + beside_ref[here, :].astype(f32) + across_ref[here, :].astype(f32)
            vals = values_ref[here, :].astype(f32)
            scale = inverse_scale(vals)
            weighted = grad * gain_ref[...]
            inner = jnp.mean(weighted * vals, axis=-1, keepdims=True)
            total = scale * weighted - vals * (scale * scale * scale) * inner
            total = base_ref[here, :].astype(f32) + total
            if groups is None:
                out_refs[0][here, :] = total
                out_refs[1][here, :] = total.astype(bf16)
            else:
                total = turn_block(total, s[0])
                step = min(piece, SLAB)
                for at in range(here.start, here.stop, step):
                    side, rest = at // size, at % size
                    group, first = rest // piece, rest % piece
                    rows = total[at - here.start : at - here.start + step]
                    out_refs[0][group, side, first : first + step, :] = rows.astype(bf16)
            term = term + jnp.sum(grad * vals * scale, axis=0, keepdims=True)
        out_refs[-1][...] = term

    if groups is None:
        shapes = [shape_of((count, width), f32), shape_of((count, width), bf16)]
    else:
        shapes = [shape_of((groups, 2, piece, width), bf16)]
    return near(
        "norm_backward",
        body,
        [values, own, beside, across, base, gain],
        [*shapes, shape_of((1, width), f32)],
        scalars=jnp.zeros((1,), jnp.int32) if pair is None else pair.reshape(1),
    )


def arrange_tokens(arrived, kept, pair):
    groups, size, width = kept.shape

    def body(s, arrived_ref, kept_ref, out_ref):
        for place in range(2):

            @pl.when(s[0] == place)
            def _():
                for group in range(groups):
                    out_ref[group, place] = turn_block(kept_ref[group], s[0])
                    out_ref[group, 1 - place] = turn_block(arrived_ref[group], s[0])

    return near(
        "arrange_tokens",
        body,
        [arrived, kept],
        shape_of((groups, 2, size, width), bf16),
        scalars=pair.reshape(1),
    )


def is_valid(s, half, size):
    first = (half * 4 + 2 * s[1] + s[2]) * size
    return first + lax.broadcasted_iota(jnp.int32, (size, 1), 0) < s[3]


def arrange_cotangent(cots, other, scalars):
    _, size, width = cots.shape

    def body(s, own_ref, other_ref, out_ref):
        for half in range(2):
            good = is_valid(s, half, size)

            @pl.when(half == s[0])
            def _():
                rows = turn_block(own_ref[half].astype(f32), s[0])
                out_ref[half * size : (half + 1) * size, :] = jnp.where(good, rows, 0.0).astype(bf16)

            @pl.when(half != s[0])
            def _():
                rows = turn_block(other_ref[0:size, :].astype(f32), s[0])
                out_ref[half * size : (half + 1) * size, :] = jnp.where(good, rows, 0.0).astype(bf16)

    return near(
        "arrange_cotangent",
        body,
        [cots, other],
        shape_of((2 * size, width), bf16),
        scalars=scalars,
    )


def final_rows(middle, own, beside, across, scalars):
    count, width = middle.shape
    size = count // 2

    def body(s, middle_ref, own_ref, beside_ref, across_ref, out_ref, away_ref):
        for half in range(2):
            good = is_valid(s, half, size)
            here = slice(half * size, (half + 1) * size)
            total = own_ref[here, :].astype(f32) + beside_ref[here, :].astype(f32)
            total = middle_ref[here, :] + (total + across_ref[here, :].astype(f32))
            rows = turn_block(jnp.where(good, total, 0.0), s[0]).astype(bf16)

            @pl.when(half == s[0])
            def _():
                out_ref[...] = rows

            @pl.when(half != s[0])
            def _():
                away_ref[...] = rows

    return near(
        "final_rows",
        body,
        [middle, own, beside, across],
        [shape_of((size, width), bf16)] * 2,
        scalars=scalars,
    )


def part_of(where_ref, chunk, half):
    core = jnp.bitwise_xor(where_ref[0], chunk % 2)
    col = jnp.bitwise_xor(where_ref[1], chunk // 2)
    return half * 4 + core * 2 + col


def scan_lanes(values, backwards):
    count = values.shape[1]
    lane = lax.broadcasted_iota(jnp.int32, values.shape, 1)
    step = 1
    while step < count:
        if backwards:
            moved = pltpu.roll(values, count - step, 1)
            values = values + jnp.where(lane < count - step, moved, 0.0)
        else:
            moved = pltpu.roll(values, step, 1)
            values = values + jnp.where(lane >= step, moved, 0.0)
        step *= 2
    return values


def log_sigmoid(values):
    return jnp.minimum(values, 0.0) - jnp.log1p(jnp.exp(-jnp.abs(values)))


def attention_forward(chunks, own_w, other_w, forget, bias, where, heads, head_size):
    each, width = chunks[0].shape
    count, half = 4 * each, width // 2
    size = count // 8
    pairs = heads // 2
    per = 4 * head_size
    step = min(STEP, count)

    def body(where_ref, x0, x1, x2, x3, own_ref, other_ref, forget_ref, bias_ref,
             gated_ref, proj_ref, mixed_ref, logit_ref, prefix_ref, base_ref, rows, cols):
        pid = pl.program_id(0)
        lanes = pl.multiple_of(pid * 2 * per, 2 * per)
        pair_lanes = pl.multiple_of(pid * 2 * head_size, 2 * head_size)
        xs = (x0, x1, x2, x3)

        @pl.when(pid == 0)
        def _():
            for chunk in range(4):
                logits = dot_nt(forget_ref[...], xs[chunk][...]) + bias_ref[:, 0:1]
                for side in range(2):
                    start = pl.multiple_of(part_of(where_ref, chunk, side) * size, size)
                    logit_ref[:, pl.ds(start, size)] = logits[:, side * size : (side + 1) * size]
            sums = scan_lanes(log_sigmoid(logit_ref[...]), False)
            prefix_ref[...] = sums
            for part in range(8):
                block = sums[:, part * size : (part + 1) * size]
                tall = jnp.concatenate([block, jnp.zeros((128 - 8, size), f32)], axis=0)
                cols[part * size : (part + 1) * size, :] = tall.T

        for chunk in range(4):
            made = dot_nn(xs[chunk][:, :half], own_ref[:, pl.ds(lanes, 2 * per)])
            made = (made + dot_nn(xs[chunk][:, half:], other_ref[:, pl.ds(lanes, 2 * per)])).astype(bf16)
            for side in range(2):
                start = pl.multiple_of(part_of(where_ref, chunk, side) * size, size)
                rows[pl.ds(start, size), :] = made[side * size : (side + 1) * size]
        proj_ref[:, pl.ds(lanes, 2 * per)] = rows[...]
        lane = lax.broadcasted_iota(jnp.int32, (step, 128), 1)
        apart = lax.broadcasted_iota(jnp.int32, (step, step), 1) <= lax.broadcasted_iota(
            jnp.int32, (step, step), 0
        )
        for first in range(0, count, step):
            last = first + step
            mixed_two, gated_two, base_two = [], [], []
            for side in range(2):
                at = side * per
                head = pid * 2 + side
                query = rows[first:last, at : at + head_size]
                key = rows[0:last, at + head_size : at + 2 * head_size]
                value = rows[0:last, at + 2 * head_size : at + 3 * head_size]
                gate = rows[first:last, at + 3 * head_size : at + 4 * head_size].astype(f32)
                own = jnp.sum(jnp.where(lane == head, cols[first:last, :], 0.0), axis=1, keepdims=True)
                allp = prefix_ref[pl.ds(head, 1), 0:last]
                score = dot_nt(query, key) * head_size ** (-0.5) + own - allp
                tail = jnp.where(apart, score[:, first:last], masked_score)
                score = tail if first == 0 else jnp.concatenate([score[:, :first], tail], axis=1)
                top = jnp.max(score, axis=1, keepdims=True)
                weight = jnp.exp(score - top)
                total = jnp.sum(weight, axis=1, keepdims=True)
                mixed = dot_nn(weight.astype(bf16), value) / total
                mixed_two.append(mixed)
                gated_two.append(mixed * jax.nn.sigmoid(gate))
                base_two.append(own - top - jnp.log(total))
            mixed_ref[first:last, pl.ds(pair_lanes, 2 * head_size)] = jnp.concatenate(mixed_two, axis=1)
            gated = jnp.concatenate(gated_two, axis=1).astype(bf16)
            base_ref[pid, first:last, :] = jnp.where(lane == 0, base_two[0], base_two[1])
            for part in range(first // size, last // size):
                core = jnp.bitwise_xor(where_ref[0], (part // 2) % 2)
                col = jnp.bitwise_xor(where_ref[1], part % 2)
                start = pl.multiple_of(((col * 2 + core) * 2 + part // 4) * size, size)
                off = part * size - first
                gated_ref[pl.ds(start, size), pl.ds(pair_lanes, 2 * head_size)] = gated[off : off + size]

    return near(
        "attention_forward",
        body,
        [*chunks, own_w, other_w, forget, bias],
        [
            shape_of((count, heads * head_size), bf16),
            shape_of((count, heads * per), bf16),
            shape_of((count, heads * head_size), f32),
            shape_of((8, count), f32),
            shape_of((8, count), f32),
            shape_of((pairs, count, 128), f32),
        ],
        [pltpu.VMEM((count, 2 * per), bf16), pltpu.VMEM((count, 128), f32)],
        where,
        grid=(pairs,),
        limit=12,
    )


def attention_backward(chunks, out_w, saved, where, pid, head_size):
    projected, mixed, logits, prefix, base = saved
    each, width = chunks[0].shape
    count, own_half = 4 * each, width // 2
    size = count // 8
    per = 4 * head_size
    step = min(STEP, count)
    scale = head_size ** (-0.5)

    def body(where_ref, m0, m1, m2, m3, out0_ref, out1_ref, saved_ref, mixes_ref, prefix_ref, base_ref,
             proj_ref, places_ref, rows, grads, key_sum, value_sum, query_out):
        for chunk, ref in enumerate((m0, m1, m2, m3)):
            here = slice(pid * 2 * head_size, (pid + 1) * 2 * head_size)
            made = dot_nt(ref[:, :own_half], out0_ref[here, :])
            made = made + dot_nt(ref[:, own_half:], out1_ref[here, :])
            for side in range(2):
                start = pl.multiple_of(part_of(where_ref, chunk, side) * size, size)
                grads[pl.ds(start, size), :] = made[side * size : (side + 1) * size]
        rows[...] = saved_ref[:, pid * 2 * per : (pid + 1) * 2 * per]
        lane_all = lax.broadcasted_iota(jnp.int32, (count, 128), 1)
        apart = lax.broadcasted_iota(jnp.int32, (step, step), 1) <= lax.broadcasted_iota(
            jnp.int32, (step, step), 0
        )
        sums = []
        outs = []
        one = jnp.ones((count, 1), bf16)
        pad = jnp.zeros((count, 128 - head_size - 1), bf16)
        for side in range(2):
            at = side * per
            head = pid * 2 + side
            query = rows[:, at : at + head_size]
            key = rows[:, at + head_size : at + 2 * head_size]
            value = rows[:, at + 2 * head_size : at + 3 * head_size]
            gate = jax.nn.sigmoid(rows[:, at + 3 * head_size : at + 4 * head_size].astype(f32))
            grad = grads[:, side * head_size : (side + 1) * head_size]
            mix = mixes_ref[:, (pid * 2 + side) * head_size : (pid * 2 + side + 1) * head_size]
            grad_mix = (grad * gate).astype(bf16)
            inner = jnp.sum(grad_mix.astype(f32) * mix, axis=1, keepdims=True)
            grad_gate = grad * mix * gate * (1.0 - gate)
            query_one = jnp.concatenate([query, one, pad], axis=1)
            key_one = jnp.concatenate([key, one, pad], axis=1)
            key_sum[...] = jnp.zeros((count, 128), f32)
            value_sum[...] = jnp.zeros((count, head_size), f32)
            for first in range(0, count, step):
                last = first + step
                own = base_ref[pid, first:last, side : side + 1]
                allp = prefix_ref[head : head + 1, 0:last]
                score = dot_nt(query[first:last], key[0:last]) * scale + own - allp
                tail = jnp.where(apart, score[:, first:last], masked_score)
                score = tail if first == 0 else jnp.concatenate([score[:, :first], tail], axis=1)
                probs = jnp.exp(score)
                grad_probs = dot_nt(grad_mix[first:last], value[0:last])
                grad_score = (probs * (grad_probs - inner[first:last])).astype(bf16)
                query_out[first:last, :] = dot_nn(grad_score, key_one[0:last])
                key_sum[0:last, :] += dot_tn(grad_score, query_one[first:last])
                value_sum[0:last, :] += dot_tn(probs.astype(bf16), grad_mix[first:last])
            dq = query_out[...]
            dk = key_sum[...]
            sums.append(dq[:, head_size : head_size + 1] - dk[:, head_size : head_size + 1])
            outs += [dq[:, :head_size] * scale, dk[:, :head_size] * scale, value_sum[...], grad_gate]
        full = jnp.concatenate(outs, axis=1).astype(bf16)
        for part in range(8):
            core = jnp.bitwise_xor(where_ref[0], (part // 2) % 2)
            col = jnp.bitwise_xor(where_ref[1], part % 2)
            start = pl.multiple_of(((col * 2 + core) * 2 + part // 4) * size, size)
            proj_ref[pl.ds(start, size), :] = full[part * size : (part + 1) * size]
        both = jnp.where(lane_all == 0, sums[0], jnp.where(lane_all == 1, sums[1], 0.0))
        for part in range(8):
            here = slice(part * size, (part + 1) * size)
            places_ref[:, here] = both[here].T[0:8, :]

    return near(
        "attention_backward",
        body,
        [*chunks, *out_w, projected, mixed, prefix, base],
        [shape_of((count, 2 * per), bf16), shape_of((8, count), f32)],
        [
            pltpu.VMEM((count, 2 * per), bf16),
            pltpu.VMEM((count, 2 * head_size), f32),
            pltpu.VMEM((count, 128), f32),
            pltpu.VMEM((count, head_size), f32),
            pltpu.VMEM((count, 128), f32),
        ],
        where,
        limit=16,
    )


def grad_log(places, logits, where, each):
    count = logits.shape[1]
    size = count // 8

    def body(where_ref, *refs):
        parts, logit_ref, out_ref, rows = refs[:-3], refs[-3], refs[-2], refs[-1]
        rows[...] = jnp.zeros((8, count), f32)
        for k, ref in enumerate(parts):
            rows[2 * k : 2 * k + 2, :] = ref[0:2, :]
        rows[...] = scan_lanes(rows[...], True) * jax.nn.sigmoid(-logit_ref[...])
        for chunk in range(4):
            for side in range(2):
                start = pl.multiple_of(part_of(where_ref, chunk, side) * size, size)
                at = chunk * each + side * size
                out_ref[:, at : at + size] = rows[:, pl.ds(start, size)]

    return near(
        "grad_log",
        body,
        [*places, logits],
        shape_of((8, count), f32),
        [pltpu.VMEM((8, count), f32)],
        where,
    )


WIDE = 256


def spread(terms, name, extra=None):
    count = terms[0][0].shape[0]
    half = terms[0][1].shape[1] if terms[0][3] is None else terms[0][1].shape[0]
    each = count // 4
    ins = [array for term in terms for array in term[:3]] + list(extra or ())

    def body(*refs):
        out_refs = refs[-4:]
        for chunk in (2, 3, 0, 1):
            rows = slice(chunk * each, (chunk + 1) * each)
            for at in range(0, 2 * half, WIDE):
                side, here = at // half, slice(at % half, at % half + WIDE)
                total = 0.0
                for k, (left, _, _, kind) in enumerate(terms):
                    left_ref, weight_ref = refs[3 * k], refs[3 * k + 1 + side]
                    if kind is None:
                        total = total + dot_nn(left_ref[rows, :], weight_ref[:, here])
                    else:
                        inner = left.shape[1]
                        weight = weight_ref[here, kind * inner : (kind + 1) * inner]
                        total = total + dot_nt(left_ref[rows, :], weight)
                if extra is not None:
                    log_ref, forget_ref = refs[3 * len(terms)], refs[3 * len(terms) + 1]
                    total = total + dot_tn(log_ref[:, rows].astype(bf16), forget_ref[:, at : at + WIDE])
                out_refs[chunk][:, at : at + WIDE] = total.astype(bf16)

    return near(name, body, ins, [shape_of((each, 2 * half), bf16)] * 4, limit=12)


TILE = 256


def ffn_forward(chunks, gate_w, up_w):
    each, width = chunks[0].shape
    count, half = 4 * each, width // 2
    units = gate_w[0].shape[1]

    def body(x0, x1, x2, x3, gate0, gate1, up0, up1, gate_ref, up_ref, hidden_ref):
        for chunk, ref in enumerate((x0, x1, x2, x3)):
            here = slice(chunk * each, (chunk + 1) * each)
            for at in range(0, units, TILE):
                cols = slice(at, at + TILE)
                gate = dot_nn(ref[:, :half], gate0[:, cols]) + dot_nn(ref[:, half:], gate1[:, cols])
                up = dot_nn(ref[:, :half], up0[:, cols]) + dot_nn(ref[:, half:], up1[:, cols])
                gate_ref[here, cols] = gate.astype(bf16)
                up_ref[here, cols] = up.astype(bf16)
                hidden_ref[here, cols] = (gate * jax.nn.sigmoid(gate) * up).astype(bf16)

    return near(
        "ffn_forward", body, [*chunks, *gate_w, *up_w], [shape_of((count, units), bf16)] * 3
    )


def ffn_backward(chunks, down_w, gate_proj, up_proj):
    each, width = chunks[0].shape
    count, half = 4 * each, width // 2
    units = gate_proj.shape[1]

    def body(g0, g1, g2, g3, down0, down1, gate_ref, up_ref, grad_gate_ref, grad_up_ref):
        for chunk, ref in enumerate((g0, g1, g2, g3)):
            here = slice(chunk * each, (chunk + 1) * each)
            for at in range(0, units, TILE):
                cols = slice(at, at + TILE)
                grad = dot_nt(ref[:, :half], down0[cols, :]) + dot_nt(ref[:, half:], down1[cols, :])
                gate = gate_ref[here, cols].astype(f32)
                up = up_ref[here, cols].astype(f32)
                sig = jax.nn.sigmoid(gate)
                slope = sig * (1.0 + gate * (1.0 - sig))
                grad_gate_ref[here, cols] = (grad * up * slope).astype(bf16)
                grad_up_ref[here, cols] = (grad * gate * sig).astype(bf16)

    return near(
        "ffn_backward",
        body,
        [*chunks, *down_w, gate_proj, up_proj],
        [shape_of((count, units), bf16)] * 2,
    )


def grad_rows_weight(chunks, right, side, first, size, got=None):
    each, width = chunks[0].shape
    half = width // 2

    def body(x0, x1, x2, x3, right_ref, *refs):
        for at in range(0, half, TILE):
            total = 0.0 if got is None else refs[0][at : at + TILE, :].astype(f32)
            cols = slice(side * half + at, side * half + at + TILE)
            for chunk, ref in enumerate((x0, x1, x2, x3)):
                rows = slice(chunk * each, (chunk + 1) * each)
                total = total + dot_tn(ref[:, cols], right_ref[rows, first : first + size])
            refs[-1][at : at + TILE, :] = total.astype(bf16)

    return near(
        "grad_rows_weight",
        body,
        [*chunks, right] + ([] if got is None else [got]),
        shape_of((half, size), bf16),
    )


def grad_cols_weight(left, chunks, side, first, size, got=None):
    each, width = chunks[0].shape
    half = width // 2
    tile = TILE if size % TILE == 0 else 128

    def body(left_ref, x0, x1, x2, x3, *refs):
        for at in range(0, size, tile):
            total = 0.0 if got is None else refs[0][at : at + tile, :].astype(f32)
            for chunk, ref in enumerate((x0, x1, x2, x3)):
                rows = slice(chunk * each, (chunk + 1) * each)
                left_block = left_ref[rows, first + at : first + at + tile]
                total = total + dot_tn(left_block, ref[:, side * half : (side + 1) * half])
            refs[-1][at : at + tile, :] = total.astype(bf16)

    return near(
        "grad_cols_weight",
        body,
        [left, *chunks] + ([] if got is None else [got]),
        shape_of((size, half), bf16),
    )


def small_grads(grad_logits, chunks, gain_one, gain_two, scalars, heads, own_heads):
    each, width = chunks[0].shape
    tall = -(-(heads + 3) // 8) * 8

    def body(s, log_ref, x0, x1, x2, x3, one_ref, two_ref, out_ref):
        low = log_ref[...].astype(bf16)
        total = 0.0
        for chunk, ref in enumerate((x0, x1, x2, x3)):
            total = total + dot_nn(low[:, chunk * each : (chunk + 1) * each], ref[...])
        total = turn_block(total, s[0])
        place = 2 * s[2] + s[1]
        out_ref[...] = jnp.zeros((tall, width), f32)
        for k in range(heads // own_heads):

            @pl.when(place == k)
            def _():
                out_ref[k * own_heads : (k + 1) * own_heads, :] = total[0:own_heads, :]

        out_ref[heads : heads + 1, :] = turn_block(one_ref[...], s[0])
        out_ref[heads + 1 : heads + 2, :] = turn_block(two_ref[...], s[0])
        bias = jnp.sum(low.astype(f32), axis=1, keepdims=True)
        lane = lax.broadcasted_iota(jnp.int32, (8, 128), 1)
        head = lax.broadcasted_iota(jnp.int32, (8, 128), 0)
        good = (lane == place * own_heads + head) & (head < own_heads)
        out_ref[heads + 2 : heads + 3, 0:128] = jnp.sum(jnp.where(good, bias, 0.0), axis=0, keepdims=True)

    return near(
        "small_grads",
        body,
        [grad_logits, *chunks, gain_one, gain_two],
        shape_of((tall, width), f32),
        scalars=scalars,
    )


def line_rows(own, before, behind, place):
    rows, cols = own.shape

    def body(s, *refs):
        out_ref = refs[-1]
        for at in range(4):
            for k in range(-3, 4):

                @pl.when(at - s[0] == k)
                def _():
                    out_ref[at * rows : (at + 1) * rows, :] = refs[k + 3][...]

    return near(
        "line_rows",
        body,
        [*reversed(before), own, *behind],
        shape_of((4 * rows, cols), own.dtype),
        scalars=place.reshape(1).astype(jnp.int32),
    )


def halves(ref, index, axis):
    half = ref.shape[axis] // 2
    here = slice(index * half, (index + 1) * half)
    return ref[here, :] if axis == 0 else ref[:, here]


def settle(inner, outer, scalars, axis):
    shape = list(inner.shape)
    shape[axis] //= 2

    def body(s, inner_ref, outer_ref, out_ref):
        for core in range(2):

            @pl.when((s[1] == 1) & (s[0] == core))
            def _():
                out_ref[...] = halves(inner_ref, 1 - core, axis)

            @pl.when((s[1] != 1) & (s[0] == core))
            def _():
                out_ref[...] = halves(outer_ref, 1 - core, axis)

    return near("settle", body, [inner, outer], shape_of(tuple(shape), inner.dtype), scalars=scalars)


def put(target, shape, inner, outer, got, scalars, axis, piece, pieces):
    rows, cols = got.shape

    def body(s, *refs):
        inner_ref, outer_ref, got_ref = refs[-4:-1]
        out_ref = refs[-1]
        for core in range(2):

            @pl.when((pl.program_id(0) == 0) & (s[1] == 1) & (s[0] == core))
            def _():
                out_ref[...] = halves(inner_ref, core, axis).astype(f32)

            @pl.when((pl.program_id(0) == 0) & (s[1] != 1) & (s[0] == core))
            def _():
                out_ref[...] = halves(outer_ref, core, axis).astype(f32)

        @pl.when(pl.program_id(0) == 1)
        def _():
            out_ref[...] = got_ref[...].astype(f32)

    def out_map(i, s):
        place = jnp.bitwise_xor(s[0], i) * pieces + piece
        return (0, place) if axis == 0 else (place, 0)

    first = target is None
    ins = ([] if first else [target]) + [inner, outer, got]
    return pl.pallas_call(
        body,
        grid_spec=pltpu.PrefetchScalarGridSpec(
            num_scalar_prefetch=1,
            grid=(2,),
            in_specs=([] if first else [pl.BlockSpec(memory_space=pl.ANY)]) + [VMEM] * 3,
            out_specs=pl.BlockSpec((rows, cols), out_map),
        ),
        out_shape=shape_of(shape, f32),
        input_output_aliases={} if first else {1: 0},
        compiler_params=pltpu.CompilerParams(vmem_limit_bytes=12 << 20),
        name="put",
    )(scalars, *ins)


def line_gather(values):
    before, behind = [values], [values]
    for _ in range(3):
        before.append(lax.ppermute(before[-1], "dp", [(0, 1), (1, 2), (2, 3)]))
        behind.append(lax.ppermute(behind[-1], "dp", [(1, 0), (2, 1), (3, 2)]))
    return before[1:], behind[1:]


def chain_inward(values):
    return lax.ppermute(values, "dp", [(0, 1), (3, 2)])


def chain_middle(values):
    return lax.ppermute(values, "dp", [(1, 2), (2, 1)])


def chain_outward(values):
    return lax.ppermute(values, "dp", [(1, 0), (2, 3)])


AWAY, OWN, ONE, TWO, THREE, FOUR, ATT, SMALL_NEXT, SMALL, FFN_BACK, FFN_NFFN, DOWN_FWD = range(12)
SUM_TWO, SUM_THREE, SUM_FOUR, NORM_THREE, NORM_FOUR, FINAL, LOG, NATTN, BACK, TOKENS, REDUCE, BLOCK, PACK = range(12, 25)
DOWN, GATE, UP, OUT, ATTN = range(5)
ORDER = (
    (AWAY, DOWN, 0), (AWAY, DOWN, 1), (FFN_BACK,), (FFN_NFFN,),
    (AWAY, GATE, 0), (OWN, DOWN, 0), (SUM_THREE,), (AWAY, GATE, 1),
    (AWAY, UP, 0), (DOWN_FWD,), (OWN, DOWN, 1), (ONE, DOWN, 0),
    (NORM_THREE,), (SUM_TWO,), (OWN, GATE, 0), (ONE, DOWN, 1),
    (TWO, DOWN, 0), (OWN, GATE, 1), (ONE, GATE, 0), (TWO, DOWN, 1),
    (ATT, 0), (ATT, 1), (ONE, GATE, 1), (ATT, 2),
    (TWO, GATE, 0), (OWN, UP, 0), (LOG,), (NATTN,),
    (AWAY, OUT, 0), (TWO, GATE, 1), (SUM_FOUR,), (AWAY, ATTN, 0),
    (AWAY, ATTN, 1), (AWAY, ATTN, 2), (FINAL,), (THREE, DOWN, 0),
    (ONE, UP, 0), (OWN, ATTN, 0), (NORM_FOUR,), (SMALL,),
    (FOUR, DOWN, 0), (THREE, DOWN, 1), (SMALL_NEXT, 1), (OWN, ATTN, 1),
    (SMALL_NEXT, 2), (BACK,), (FOUR, DOWN, 1), (ONE, ATTN, 0),
    (THREE, GATE, 0), (THREE, GATE, 1), (TWO, UP, 0), (OWN, ATTN, 2),
    (FOUR, GATE, 0), (FOUR, GATE, 1), (OWN, OUT, 0), (ONE, ATTN, 1),
    (TWO, ATTN, 0), (SMALL_NEXT, 3), (ONE, ATTN, 2), (TOKENS,),
    (THREE, UP, 0), (ONE, OUT, 0), (TWO, ATTN, 1), (SMALL_NEXT, 4),
    (BLOCK,), (THREE, ATTN, 0), (TWO, ATTN, 2), (FOUR, ATTN, 0),
    (THREE, ATTN, 1), (FOUR, UP, 0), (TWO, OUT, 0), (SMALL_NEXT, 5),
    (FOUR, ATTN, 1), (THREE, ATTN, 2), (FOUR, ATTN, 2), (THREE, OUT, 0),
    (PACK,), (FOUR, OUT, 0),
)
PIECES = (2, 2, 1, 1, 3)
REDUCED = ()


class Store:
    pass


def shards(
    tokens,
    seq_lengths,
    seq_slots,
    w_attn,
    w_forget,
    b_forget,
    w_out,
    w_gate,
    w_up,
    w_down,
    gain_attn,
    gain_ffn,
    out_grad,
):
    count_seq = seq_slots.shape[0]
    piece_rows = tokens.shape[2]
    width = tokens.shape[3]
    groups = lax.axis_size("dp")
    row_index = lax.axis_index("row")
    pair, core = row_index // 2, row_index % 2
    col = lax.axis_index("col")
    group = lax.axis_index("dp")
    part_rows = out_grad.shape[2]
    own_heads = b_forget.shape[0] // 2
    all_heads = b_forget.shape[0] * lax.axis_size("col")
    head_size = w_out.shape[0] // (2 * own_heads)
    where = jnp.stack([core, col]).astype(jnp.int32)

    order = [None]

    def tie(values):
        return values if order[0] is None else after(values, order[0])

    def step(op, values, *others):
        out = op(tie(values), *others)
        order[0] = out[0] if isinstance(out, (list, tuple)) else out
        return out

    my_slot = 2 * group + pair
    my_length = jnp.sum(jnp.where(seq_slots == my_slot, seq_lengths, 0))
    scalars = jnp.stack([pair, core, col, my_length]).astype(jnp.int32)
    flat_tokens = tokens.reshape(count_seq, piece_rows, width)

    small = jnp.concatenate([w_forget.T, gain_attn[None], gain_ffn[None]], axis=0)
    small = joined(small, swap_core(small), core, 1)
    attn_cut = cut(w_attn, 1 - core, 1)
    order[0] = attn_cut
    gate_cut = step(cut, w_gate, 1 - core, 1)
    attn_got, gate_got = swap_core(attn_cut), swap_core(gate_cut)
    blocks = -(-small.shape[0] // piece_rows)
    extra = jnp.pad(small, ((0, blocks * piece_rows - small.shape[0]), (0, width // 2)))
    payload = take_slots(flat_tokens, seq_slots, 1 - pair, extra.reshape(blocks, piece_rows, width))
    payload_got = swap_pair(payload)
    arrived = payload_got
    order[0] = payload
    kept = step(lambda v: take_slots(v, seq_slots, pair), flat_tokens)

    cots = out_grad.reshape(2, part_rows, width)
    cots_sent = tie(pick(cots, 1 - pair, 0))
    cots_got = swap_pair(cots_sent)
    order[0] = cots_sent
    gate_own = step(lay, gate_got, w_gate, core, 1)
    if groups == 4:
        gate_quarter = step(cut, gate_own, group, 0, 4)
        gate_quarter = swap_pair(gate_quarter)
        before, behind = line_gather(gate_quarter)
        lines = [[before[k], behind[k]] for k in range(3)]
    else:
        lines = [[], [], []]
    out_cut = step(cut, w_out, 1 - core, 0)
    up_cut = step(cut, w_up, 1 - core, 1)
    down_cut = step(cut, w_down, 1 - core, 0)
    attn_own = step(lay, attn_got, w_attn, core, 1)
    outgoing = step(arrange_tokens, arrived, kept, pair)
    outgoing = outgoing.reshape(2 * groups, piece_rows, width)
    rows = lax.all_to_all(outgoing, "dp", split_axis=0, concat_axis=1, tiled=True)
    rows = rows.reshape(2 * part_rows, width)
    attn_own = after(attn_own, outgoing, *([gate_quarter] if groups == 4 else []))
    attn_w = [attn_own, swap_pair(attn_own)]
    order[0] = attn_own
    out_own = step(lay, swap_core(out_cut), w_out, core, 0)
    up_own = step(lay, swap_core(up_cut), w_up, core, 1)
    down_own = step(lay, swap_core(down_cut), w_down, core, 0)
    out_w = [out_own, swap_pair(out_own)]
    up_w = [up_own, swap_pair(up_own)]
    down_w = [down_own, swap_pair(down_own)]

    small_got = payload_got[groups:].reshape(-1, width)[: small.shape[0], : width // 2]
    small = jnp.concatenate([small, small_got], axis=1)
    forget = pick(small[: 2 * own_heads].reshape(2, own_heads, width), core, 0)
    forget = jnp.pad(forget, ((0, 8 - own_heads), (0, 0)))
    gain_one = small[2 * own_heads : 2 * own_heads + 1].astype(f32)
    gain_two = small[2 * own_heads + 1 : 2 * own_heads + 2].astype(f32)
    bias = pick(b_forget.reshape(2, own_heads), core, 0).astype(f32)
    bias = jnp.broadcast_to(jnp.pad(bias, (0, 8 - own_heads))[:, None], (8, 128))

    grad_final = step(arrange_cotangent, cots, cots_got, scalars)
    wide_grad = gather_quad(grad_final)
    normed_one = step(norm, after(rows, wide_grad[1]), gain_one)
    across = swap_col(normed_one)
    wide_one = [normed_one, swap_core(normed_one), across, swap_core(after(across, *lines[0]))]
    gated, *saved = attention_forward(
        [after(normed_one, order[0], wide_grad[2], *lines[1]), *wide_one[1:]],
        *attn_w, forget, bias, where, own_heads, head_size
    )
    order[0] = gated
    part = step(lambda v: spread([(v, *out_w, None)], "out_forward"), after(gated, *lines[2]))
    sent_one = step(add, part[2], swap_core(part[3]))
    across = swap_col(sent_one)
    if groups == 4:
        gate_w = [gate_own, step(line_rows, gate_quarter, before, behind, group)]
    else:
        gate_w = [gate_own, swap_pair(gate_own)]
    middle, normed_two = step(sum_norm, after(rows, up_w[1]), part[0], swap_core(part[1]), across, gain_two)
    across = swap_col(normed_two)
    wide_two = [normed_two, swap_core(normed_two), across, swap_core(across)]
    gate_proj, up_proj, hidden = step(ffn_forward, wide_two, gate_w, up_w)

    parts = own_heads // 2
    inner = ((group == 1) | (group == 2)) if groups == 4 else (group >= 0)
    flags = jnp.stack([core, inner.astype(jnp.int32)]).astype(jnp.int32)
    shapes = (w_down.shape, w_gate.shape, w_up.shape, w_out.shape, w_attn.shape)
    grads = [None] * 5
    have = Store()
    have.units, have.projected, have.places = {}, {}, {}

    def operands(name, piece):
        pieces = PIECES[name]
        if name == ATTN:
            return grad_rows_weight, wide_one, have.projected[piece], 0, w_attn.shape[1] // (2 * pieces)
        size = shapes[name][0 if name in (DOWN, OUT) else 1] // (2 * pieces)
        if name == DOWN:
            return grad_cols_weight, hidden, wide_grad, piece * size, size
        if name == OUT:
            return grad_cols_weight, gated, have.wide_mid, 0, size
        return grad_rows_weight, wide_two, have.grad_gate if name == GATE else have.grad_up, piece * size, size

    def product(name, piece, side, got=None):
        kind, left, right, first, size = operands(name, piece)
        if kind is grad_rows_weight:
            return step(lambda v: kind(left, v, side, first, size, got), right)
        if isinstance(left, list):
            return step(lambda v: kind([v, *left[1:]], right, side, first, size, got), left[0])
        return step(lambda v: kind(v, right, side, first, size, got), left)

    def away(name, piece):
        have.units[name, piece] = swap_pair(product(name, piece, 1))

    def own(name, piece):
        mine = product(name, piece, 0, have.units[name, piece])
        chained = groups == 4 and name not in REDUCED
        have.units[name, piece] = (mine, chain_inward(mine) if chained else None)

    def reduce(*names):
        keys = [key for key in have.units if key[0] in names]
        sums = lax.psum([have.units[key][0] for key in keys], "dp")
        for key, total in zip(keys, sums):
            have.units[key] = (total, total)

    def one(name, piece):
        mine, got = have.units[name, piece]
        if groups == 4:
            mine = step(add, mine, got)
            got = chain_middle(mine)
        have.units[name, piece] = (mine, got)

    def two(name, piece):
        mine, got = have.units[name, piece]
        if groups == 4:
            mine = step(add, mine, got)
            got = chain_outward(mine)
        else:
            mine = got = lax.psum(mine, "dp")
        have.units[name, piece] = (mine, got)

    def three(name, piece):
        mine, got = have.units[name, piece]
        axis = 0 if operands(name, piece)[0] is grad_rows_weight else 1
        have.units[name, piece] = (mine, got, axis, swap_core(step(settle, mine, got, flags, axis)))

    def four(name, piece):
        mine, got, axis, beside = have.units[name, piece]
        grads[name] = step(
            lambda v: put(grads[name], shapes[name], mine, got, v, flags, axis, piece, PIECES[name]), beside
        )

    def ffn_back():
        have.grad_gate, have.grad_up = step(ffn_backward, wide_grad, down_w, gate_proj, up_proj)

    def ffn_nffn():
        terms = [(have.grad_up, *up_w, 0)]
        part = step(lambda v: spread([(v, *gate_w, 0), *terms], "ffn_nffn"), have.grad_gate)
        have.part_three = [*part, swap_core(part[3]), swap_core(part[1])]

    def down_fwd():
        part = step(lambda v: spread([(v, *down_w, None)], "down_forward"), hidden)
        have.part_two = [*part, swap_core(part[3]), swap_core(part[1])]

    def sums(part):
        return swap_col(step(add, part[2], part[4]))

    def sum_two():
        have.across_two = sums(have.part_two)

    def sum_three():
        have.across_three = sums(have.part_three)

    def sum_four():
        have.across_four = sums(have.part_four)

    def norm_three():
        part = have.part_three
        have.grad_middle, grad_attn, have.gain_two = step(
            norm_backward, middle, part[0], part[5], have.across_three, grad_final, gain_two
        )
        have.wide_mid = gather_quad(grad_attn)

    def final():
        part = have.part_two
        kept, away = step(final_rows, middle, part[0], part[5], have.across_two, scalars)
        have.final = (kept, swap_pair(away))

    def att(piece):
        have.projected[piece], have.places[piece] = step(
            lambda v: attention_backward([v, *have.wide_mid[1:]], out_w, saved, where, piece, head_size),
            have.wide_mid[0],
        )

    def log():
        places = [have.places[k] for k in range(parts)]
        have.grad_logits = step(lambda v: grad_log([v, *places[1:]], saved[2], where, 2 * part_rows), places[0])

    def nattn():
        grad = have.projected
        part = step(
            lambda v: spread(
                [(grad[k] if k else v, *attn_w, k) for k in range(parts)],
                "attn_nattn",
                (have.grad_logits, forget),
            ),
            grad[0],
        )
        have.part_four = [*part, swap_core(part[3]), swap_core(part[1])]

    def norm_four():
        part = have.part_four
        grad_rows, have.gain_one = step(
            norm_backward, rows, part[0], part[5], have.across_four, have.grad_middle, gain_one, pair, groups
        )
        have.returned = lax.all_to_all(grad_rows, "dp", split_axis=0, concat_axis=0, tiled=True)

    def back():
        returned = tie(have.returned)
        sent = pick(returned, 1 - pair, 1)
        have.back = (pick(returned, pair, 1), swap_pair(sent))
        order[0] = sent

    def tokens_last():
        stay, got = have.back
        stay = tie(stay)
        by_slot = jnp.stack([jnp.where(pair == 0, stay, got), jnp.where(pair == 0, got, stay)], 1)
        have.tokens = jnp.take(by_slot.reshape(count_seq, piece_rows, width), seq_slots, axis=0, mode="clip")
        order[0] = have.tokens

    def small_first():
        pack = step(
            small_grads, have.grad_logits, wide_one, have.gain_one, have.gain_two, scalars, all_heads, own_heads
        )
        have.small = (pack, swap_core(pack))

    def small_next(stage):
        pack, got = have.small
        if stage >= 3 and groups != 4:
            have.small = (pack if stage > 3 else lax.psum(step(add, pack, got), "dp"), None)
            return
        pack = step(add, pack, got)
        swap = (swap_col, swap_pair, chain_inward, chain_middle, chain_outward)[stage - 1]
        if stage == 2 and groups != 4:
            swap = swap_pair
        have.small = (pack, swap(pack))

    def block():
        kept, got = have.final
        have.block_out = joined(tie(kept)[None], got[None], pair, 0)
        order[0] = have.block_out

    def pack_last():
        have.pack, got = have.small
        if groups == 4:
            have.pack = jnp.where(inner, tie(have.pack), got)
            order[0] = have.pack

    single = {
        BLOCK: block,
        PACK: pack_last,
        FFN_BACK: ffn_back,
        FFN_NFFN: ffn_nffn,
        DOWN_FWD: down_fwd,
        SUM_TWO: sum_two,
        SUM_THREE: sum_three,
        SUM_FOUR: sum_four,
        NORM_THREE: norm_three,
        NORM_FOUR: norm_four,
        FINAL: final,
        LOG: log,
        NATTN: nattn,
        BACK: back,
        TOKENS: tokens_last,
        SMALL: small_first,
        ATT: att,
        REDUCE: reduce,
        SMALL_NEXT: small_next,
        AWAY: away,
        OWN: own,
        ONE: one,
        TWO: two,
        THREE: three,
        FOUR: four,
    }
    for entry in ORDER:
        single[entry[0]](*entry[1:])

    block_out, pack = have.block_out, have.pack
    block_width = gain_attn.shape[0]
    mine = lax.dynamic_slice_in_dim(pack, row_index * block_width, block_width, 1)
    forget_grad = lax.dynamic_slice_in_dim(mine, col * 2 * own_heads, 2 * own_heads, 0).T
    bias_grad = lax.dynamic_slice_in_dim(pack[all_heads + 2], col * 2 * own_heads, 2 * own_heads)
    return (
        block_out[:, None],
        have.tokens[:, None],
        grads[ATTN],
        forget_grad,
        bias_grad,
        grads[OUT],
        grads[GATE],
        grads[UP],
        grads[DOWN],
        mine[all_heads],
        mine[all_heads + 1],
    )


def solution(mesh):
    return jax.shard_map(
        shards,
        mesh=mesh,
        in_specs=(
            P(None, ("row", "col"), "dp", None),
            P(),
            P(),
            P("row", "col"),
            P("row", "col"),
            P("col"),
            P("col", "row"),
            P("row", "col"),
            P("row", "col"),
            P("col", "row"),
            P("row"),
            P("row"),
            P("dp", ("row", "col"), None, None),
        ),
        out_specs=(
            P("dp", ("row", "col"), None, None),
            P(None, ("row", "col"), "dp", None),
            P("row", "col"),
            P("row", "col"),
            P("col"),
            P("col", "row"),
            P("row", "col"),
            P("row", "col"),
            P("col", "row"),
            P("row"),
            P("row"),
        ),
        check_vma=False,
    )
```
